128 devices in a mesh: song: 16 (over x_lo, z, core), tensor: 8 (over x_hi, y).
Axes of the slice: x: 4 (x_hi: 2, x_lo: 2; x = x_hi * 2 + x_lo), y: 4, z: 4, core: 2. Of those that a mesh axis runs over, the one named last changes fastest.
Arguments:
- upper_codes: int32 [4096], P('song'), may hold values from 0 to 2047
- middle_codes: int32 [16384], P('song'), may hold values from 0 to 2047
- upper_table: bfloat16 [2048, 1024], P(None, 'tensor'), may hold values from -6 to 6
- dilated_weight: bfloat16 [4, 3, 1024, 1024], P(None, None, 'tensor'), may hold values from -0.109375 to 0.109375
- mixing_weight: bfloat16 [4, 1024, 1024], P(None, None, 'tensor'), may hold values from -0.1875 to 0.1875
- upsample_weight: bfloat16 [1024, 7680], P('tensor'), may hold values from -0.1875 to 0.1875
- middle_table: bfloat16 [2048, 1920], P('tensor'), may hold values from -6 to 6
- norm_gain: float32 [1920], replicated, may hold values from 0.1 to 1.9
- qkv_weight: bfloat16 [1920, 16, 384], P(None, 'tensor'), may hold values from -4 to 4
Outputs:
- context: bfloat16 [16384, 2048], P('song', 'tensor')
The draws below stay inside these ranges and needn't reach their ends.
All inputs are finite; a program needn't handle non-finite values.
Results may differ from the reference program's by a relative error of at most 0.0145.
Values may be sent and summed in bfloat16 or wider, within the bound.
No kernel may reach another device: no remote copies, remote signals or barrier semaphores. Data moves between devices by JAX's collectives and lax.ppermute only.
A program may use at most 128 MiB of HBM per device.

```python
import jax
import jax.numpy as jnp
from jax import lax

D = 1920
C = 1024
VOCAB = 2048
HEADS = 16
HD = 128
BLOCKS = 4
TOK_DEV = 1024
TOKENS = 16384
UPPER = 4096
N_SONG = 16


def draw_qkv_weight(key, part):
    base = jax.random.normal(key, (D, HEADS, 3 * HD), jnp.float32) * D ** (-0.5)
    base = jnp.clip(base, -6.0 * D ** (-0.5), 6.0 * D ** (-0.5))
    return base.astype(jnp.bfloat16)


def plant(array, rng, least, largest):
    longest = array.shape.index(max(array.shape))
    spots = []
    for shift in (0, 1):
        where = [jax.random.randint(jax.random.fold_in(rng, axis), (), 0, length) for axis, length in enumerate(array.shape)]
        where[longest] = (where[longest] + shift) % array.shape[longest]
        spots.append(tuple(where))
    return array.at[spots[0]].set(least).at[spots[1]].set(largest)


def block_levels(key, dims, cuts, smallest, largest):
    gain, own = 1.0, jax.random.fold_in(key, 6)
    for dim, parts in cuts:
        heights = jnp.exp(jax.random.uniform(jax.random.fold_in(own, dim), (parts,), jnp.float32, smallest / len(cuts), largest / len(cuts)))
        gain = gain * jnp.repeat(heights, dims[dim] // parts).reshape([-1 if axis == dim else 1 for axis in range(len(dims))])
    return gain


def bell_draw(rng, dims, width, most, cuts=(), kind=jnp.bfloat16):
    factor_of = block_levels(rng, dims, cuts, -0.22, 0.18) if cuts else 1.0
    values = jax.random.normal(rng, dims, jnp.float32) * width * factor_of
    return jnp.minimum(jnp.maximum(values, -most), most).astype(kind)


def setup_inputs(seed: int = 0) -> dict:
    key_list = jax.random.split(jax.random.key(seed), 10)
    return {
        "upper_codes": plant(jax.random.randint(key_list[0], (UPPER,), 0, VOCAB), jax.random.fold_in(key_list[0], 1), 0, VOCAB - 1).astype(jnp.int32),
        "middle_codes": plant(jax.random.randint(key_list[1], (TOKENS,), 0, VOCAB), jax.random.fold_in(key_list[1], 1), 0, VOCAB - 1).astype(jnp.int32),
        "upper_table": bell_draw(key_list[2], (VOCAB, C), 1.0, 6.0, ((1, 8),)),
        "dilated_weight": bell_draw(key_list[3], (BLOCKS, 3, C, C), (3 * C) ** -0.5, 0.109375, ((2, 8),)),
        "mixing_weight": bell_draw(key_list[4], (BLOCKS, C, C), C ** -0.5, 0.1875, ((2, 8),)),
        "upsample_weight": bell_draw(key_list[5], (C, 4 * D), C ** -0.5, 0.1875, ((0, 8),)),
        "middle_table": bell_draw(key_list[6], (VOCAB, D), 1.0, 6.0, ((0, 8),)),
        "norm_gain": jnp.clip(1.0 + 0.18 * jax.random.normal(key_list[7], (D,), jnp.float32), 0.1, 1.9),
        "qkv_weight": draw_qkv_weight(jax.random.fold_in(key_list[9], 71), 0),
    }


def attend(q, k, v):
    scale = 1.0 / HD ** 0.5
    pad = jnp.zeros((2 * TOK_DEV, HEADS, HD), jnp.bfloat16)
    keys_padded = jnp.concatenate([pad, k], axis=0)
    vals_padded = jnp.concatenate([pad, v], axis=0)
    query_pos = jnp.arange(TOK_DEV, dtype=jnp.int32)
    key_rel = jnp.arange(3 * TOK_DEV, dtype=jnp.int32) - 2 * TOK_DEV

    def one_block(block):
        start = (block * TOK_DEV).astype(jnp.int32)
        q_blk = lax.dynamic_slice_in_dim(q, start, TOK_DEV, 0)
        k_blk = lax.dynamic_slice_in_dim(keys_padded, start, 3 * TOK_DEV, 0)
        v_blk = lax.dynamic_slice_in_dim(vals_padded, start, 3 * TOK_DEV, 0)
        scores = jnp.einsum('qhd,khd->hqk', q_blk.astype(jnp.float32), k_blk.astype(jnp.float32)) * scale
        valid = (key_rel[None, :] <= query_pos[:, None]) & (key_rel[None, :] >= -start)
        scores = jnp.where(valid[None], scores, -1e+30)
        top = lax.optimization_barrier(jnp.max(scores, axis=-1, keepdims=True))
        expo = jnp.exp(scores - top)
        weights = (expo / lax.optimization_barrier(jnp.sum(expo, axis=-1, keepdims=True))).astype(jnp.bfloat16)
        out = jnp.einsum('hqk,khd->qhd', weights.astype(jnp.float32), v_blk.astype(jnp.float32))
        return out.astype(jnp.bfloat16)
    blocks = lax.map(one_block, jnp.arange(N_SONG, dtype=jnp.int32))
    return blocks.reshape(TOKENS, HEADS * HD)

def reference(upper_codes, middle_codes, upper_table, dilated_weight, mixing_weight, upsample_weight, middle_table, norm_gain, qkv_weight):
    state = jnp.take(upper_table, upper_codes, axis=0).astype(jnp.float32)
    count = state.shape[0]
    for level in range(BLOCKS):
        step = 3 ** level
        state_bf = jnp.maximum(state, 0.0).astype(jnp.bfloat16)
        padded = jnp.pad(state_bf, ((step, step), (0, 0)))
        acc = jnp.zeros((count, C), jnp.float32)
        for tap in range(3):
            acc = acc + jnp.dot(padded[tap * step:tap * step + count], dilated_weight[level, tap], preferred_element_type=jnp.float32)
        rect = jnp.maximum(acc, 0.0).astype(jnp.bfloat16)
        state = state + jnp.dot(rect, mixing_weight[level], preferred_element_type=jnp.float32)
    final = state.astype(jnp.bfloat16)
    upsampled = jnp.dot(final, upsample_weight, preferred_element_type=jnp.float32).reshape(TOKENS, D)
    frames = upsampled + jnp.take(middle_table, middle_codes, axis=0).astype(jnp.float32)
    mean = lax.optimization_barrier(jnp.mean(frames, axis=1, keepdims=True))
    var = lax.optimization_barrier(jnp.mean((frames - mean) ** 2, axis=1, keepdims=True))
    normed = ((frames - mean) * lax.rsqrt(var + 1e-05) * norm_gain[None, :]).astype(jnp.bfloat16)
    projected = jnp.dot(normed, qkv_weight.reshape(D, HEADS * 3 * HD), preferred_element_type=jnp.float32)
    projected = projected.astype(jnp.bfloat16).reshape(TOKENS, HEADS, 3 * HD)
    q = projected[:, :, 0:HD]
    k = projected[:, :, HD:2 * HD]
    v = projected[:, :, 2 * HD:3 * HD]
    return attend(q, k, v)
```

```python
import functools

import jax
import jax.numpy as jnp
from jax import lax
from jax.experimental import pallas as pl
from jax.experimental.pallas import tpu as pltpu
from jax.sharding import PartitionSpec as P

BF = jnp.bfloat16
F32 = jnp.float32
D = 1920
C = 1024
VOCAB = 2048
UPPER = 4096
HALF = 128
HALO = (40, 39, 36, 27, 0)
ROWS = (208, 208, 208, 192, 128)
VMEM_LIMIT = 60 << 20

Y_GROUPS = [[0, 1, 2, 3], [4, 5, 6, 7]]


def params(**kw):
    return pltpu.CompilerParams(vmem_limit_bytes=VMEM_LIMIT, **kw)


def cost(flops, nbytes, trans=0):
    return pl.CostEstimate(flops=flops, bytes_accessed=nbytes, transcendentals=trans)


def dot(a, b):
    return jnp.dot(a, b, preferred_element_type=F32)


def send_terms(level, info, h_ref, own_ref, got_ref, sib_ref, out_ref):
    step = 3**level
    core = info[0]
    count = HALF + 2 * HALO[level + 1]
    padded = out_ref.shape[1]
    rows = h_ref.shape[0]
    first = info[1] - HALO[level]
    pos = first + lax.broadcasted_iota(jnp.int32, (rows, 1), 0)
    inside = (pos >= 0) & (pos < UPPER)
    h_ref[...] = jnp.where(inside, h_ref[...], 0.0)
    own_at = pl.multiple_of(core * 512, 512)
    sib_at = pl.multiple_of((1 - core) * 512, 512)
    near = jnp.zeros((count, 512), F32)
    away = jnp.zeros((count, 512), F32)
    for tap in range(3):
        hb = jnp.maximum(h_ref[tap * step : tap * step + count, :], 0.0).astype(BF)
        mine, other = hb[:, :128], hb[:, 128:]
        lines = slice(tap * 128, tap * 128 + 128)
        near += dot(mine, own_ref[tap, :, pl.ds(own_at, 512)]) + dot(other, got_ref[lines, :])
        away += dot(mine, own_ref[tap, :, pl.ds(sib_at, 512)]) + dot(other, sib_ref[lines, :])
    near, away = near.astype(BF), away.astype(BF)
    for y in range(4):
        cols = slice(y * 128, y * 128 + 128)
        out_ref[y, :count, :128] = near[:, cols]
        out_ref[y, :count, 128:] = away[:, cols]
        if padded > count:
            out_ref[y, count:, :] = jnp.zeros((padded - count, 256), BF)


def first_kernel(info, codes_ref, table_ref, own_ref, got_ref, sib_ref, h_ref, out_ref, work):
    codes = codes_ref[...]
    rows = codes.shape[0]
    lane = lax.broadcasted_iota(jnp.int32, (rows, 1024), 1)
    core = info[0]
    one = jnp.ones((), BF)
    zero = jnp.zeros((), BF)
    h_own = jnp.zeros((rows, 128), F32)
    h_oth = jnp.zeros((rows, 128), F32)
    for part in range(2):
        hot = jnp.where(codes == lane + part * 1024, one, zero)
        h_own += dot(hot, table_ref[part * 1024 : part * 1024 + 1024, :])
    for src, begin in ((got_ref, core * 1024), (sib_ref, (1 - core) * 1024)):
        hot = jnp.where(codes - begin == lane, one, zero)
        for q in range(4):
            h_oth += dot(hot[:, q * 256 : q * 256 + 256], src[512:768, q * 128 : q * 128 + 128])
    work[:, :128] = h_own
    work[:, 128:] = h_oth
    h_ref[...] = work[...]
    send_terms(0, info, work, own_ref, got_ref, sib_ref, out_ref)


def mixed(level, info, r_ref, h_ref, mix_ref, got_ref, sib_ref):
    step = 3**level
    core = info[0]
    count = HALF + 2 * HALO[level + 1]
    h_own = h_ref[step : step + count, :128]
    h_oth = h_ref[step : step + count, 128:]
    for half, got, begin in ((0, got_ref, core * 512), (1, sib_ref, (1 - core) * 512)):
        r = jnp.concatenate(
            [r_ref[y, :, half * 128 : half * 128 + 128] for y in range(4)], axis=1
        )[:count]
        h_own += dot(r, mix_ref[pl.ds(pl.multiple_of(begin, 512), 512), :])
        for y in range(4):
            cols = slice(y * 128, y * 128 + 128)
            h_oth += dot(r[:, cols], got[384:512, cols])
    return h_own, h_oth


def middle_kernel(level, info, r_ref, h_ref, mix_ref, got_ref, sib_ref, own_ref, got1_ref, sib1_ref, new_ref, out_ref, work):
    count = HALF + 2 * HALO[level + 1]
    h_own, h_oth = mixed(level, info, r_ref, h_ref, mix_ref, got_ref, sib_ref)
    if work.shape[0] > count:
        work[count:, :] = jnp.zeros((work.shape[0] - count, 256), F32)
    work[:count, :128] = h_own
    work[:count, 128:] = h_oth
    new_ref[...] = work[...]
    send_terms(level + 1, info, work, own_ref, got1_ref, sib1_ref, out_ref)


def last_kernel(info, r_ref, h_ref, mix_ref, got_ref, sib_ref, out_ref):
    h_own, h_oth = mixed(3, info, r_ref, h_ref, mix_ref, got_ref, sib_ref)
    h_own, h_oth = h_own.astype(BF), h_oth.astype(BF)
    for peer in range(8):
        out_ref[peer, :, :128] = h_own
        out_ref[peer, :, 128:] = h_oth


def relu_kernel(in_ref, out_ref):
    total = in_ref[0].astype(F32)
    for y in range(1, 4):
        total += in_ref[y].astype(F32)
    r = jnp.maximum(total, 0.0).astype(BF)
    for y in range(4):
        out_ref[y] = r


def call(body, outs, scratch=(), smem=1, n=0, flops=10**9, name=None):
    specs = [pl.BlockSpec(memory_space=pltpu.SMEM)] * smem + [pl.BlockSpec(memory_space=pltpu.VMEM)] * n
    return pl.pallas_call(
        body,
        out_shape=outs,
        in_specs=specs,
        out_specs=jax.tree.map(lambda _: pl.BlockSpec(memory_space=pltpu.VMEM), outs),
        scratch_shapes=list(scratch),
        compiler_params=params(),
        cost_estimate=cost(flops, 4 << 20),
        name=name,
    )


def shape(*dims, dtype=BF):
    return jax.ShapeDtypeStruct(dims, dtype)


def frames_kernel(codes_ref, hf_ref, gain_ref, qkv_ref, full_ref, q_ref, kv_ref, weights, table, hf, wide, sems, table_sem):
    def weight_copy(phase, t):
        cols = pl.ds((phase % 2) * D, D)
        return pltpu.make_async_copy(
            full_ref.at[:, phase // 2, t, :, cols], weights.at[phase, t], sems.at[phase, t]
        )

    def table_copy(part):
        return pltpu.make_async_copy(
            full_ref.at[:, part, :, :, pl.ds(2 * D, D)], table.at[:, part], table_sem.at[part]
        )

    for part in range(2):
        table_copy(part).start()
    for phase in range(4):
        for t in range(8):
            weight_copy(phase, t).start()
    for half in range(2):
        for j in range(8):
            at = 0 if j // 4 == half else 128
            hf[half * 128 : half * 128 + 128, j * 128 : j * 128 + 128] = hf_ref[
                half * 4 + j % 4, :, at : at + 128
            ]
    for part in range(2):
        table_copy(part).wait()

    lane = lax.broadcasted_iota(jnp.int32, (256, VOCAB), 1)
    for phase in range(4):
        hot = jnp.where(codes_ref[phase] == lane, jnp.ones((), BF), jnp.zeros((), BF))
        for t in range(8):
            weight_copy(phase, t).wait()
        x = dot(hf[...], weights[phase].reshape(C, D)) + dot(hot, table[...].reshape(VOCAB, D))
        mean = jnp.mean(x, axis=1, keepdims=True)
        x = x - mean
        var = jnp.mean(x * x, axis=1, keepdims=True)
        xn = (x * lax.rsqrt(var + 1e-5) * gain_ref[...]).astype(BF)
        y = dot(xn, qkv_ref[...])
        for part in range(6):
            wide[part, pl.ds(phase, 256, stride=4), :] = y[:, part * 128 : part * 128 + 128]
    for head in range(2):
        cols = slice(head * 128, head * 128 + 128)
        q_ref[:, cols] = wide[head * 3].astype(BF)
        kv_ref[:, cols] = wide[head * 3 + 1].astype(BF)
        kv_ref[:, 256 + head * 128 : 384 + head * 128] = wide[head * 3 + 2].astype(BF)


def frames(codes, hf, gain, qkv, full):
    vm = pl.BlockSpec(memory_space=pltpu.VMEM)
    return pl.pallas_call(
        frames_kernel,
        out_shape=(shape(1024, 256), shape(1024, 512)),
        in_specs=[vm, vm, vm, vm, pl.BlockSpec(memory_space=pltpu.HBM)],
        out_specs=(vm, vm),
        scratch_shapes=[
            pltpu.VMEM((4, 8, 8, 16, D), BF),
            pltpu.VMEM((8, 2, 8, 16, D), BF),
            pltpu.VMEM((256, C), BF),
            pltpu.VMEM((6, 1024, 128), F32),
            pltpu.SemaphoreType.DMA((4, 8)),
            pltpu.SemaphoreType.DMA((2,)),
        ],
        compiler_params=params(),
        cost_estimate=cost(15 * 10**9, 30 << 20),
        name="frames",
    )(codes, hf, gain, qkv, full)


SCALE = 128**-0.5 * 1.4426950408889634
TILE = 256


def scores_of(q, k):
    return lax.dot_general(q, k, (((1,), (1,)), ((), ())), preferred_element_type=F32) * SCALE


def own_kernel(q_ref, kv_ref, acc_ref, top_ref, sum_ref):
    for head in range(2):
        cols = slice(head * 128, head * 128 + 128)
        vals = slice(256 + head * 128, 384 + head * 128)
        for tile in range(1024 // TILE):
            lines = slice(tile * TILE, tile * TILE + TILE)
            keys = (tile + 1) * TILE
            s = scores_of(q_ref[lines, cols], kv_ref[:keys, cols])
            row = tile * TILE + lax.broadcasted_iota(jnp.int32, (TILE, keys), 0)
            col = lax.broadcasted_iota(jnp.int32, (TILE, keys), 1)
            s = jnp.where(col <= row, s, -1e30)
            top = jnp.max(s, axis=1, keepdims=True)
            p = jnp.exp2(s - top)
            top_ref[lines, head : head + 1] = top
            sum_ref[lines, head : head + 1] = jnp.sum(p, axis=1, keepdims=True)
            acc_ref[lines, cols] = dot(p.astype(BF), kv_ref[:keys, vals])


def past_kernel(info, q_ref, near_ref, far_ref, acc_ref, top_ref, sum_ref, out_ref, acc, tops, sums):
    acc[...] = acc_ref[...]
    tops[...] = top_ref[...]
    sums[...] = sum_ref[...]

    def fold(kv_ref):
        for head in range(2):
            cols = slice(head * 128, head * 128 + 128)
            vals = slice(256 + head * 128, 384 + head * 128)
            for tile in range(1024 // TILE):
                lines = slice(tile * TILE, tile * TILE + TILE)
                s = scores_of(q_ref[lines, cols], kv_ref[:, cols])
                old = tops[lines, head : head + 1]
                top = jnp.maximum(old, jnp.max(s, axis=1, keepdims=True))
                p = jnp.exp2(s - top)
                keep = jnp.exp2(old - top)
                tops[lines, head : head + 1] = top
                sums[lines, head : head + 1] = keep * sums[lines, head : head + 1] + jnp.sum(
                    p, axis=1, keepdims=True
                )
                acc[lines, cols] = keep * acc[lines, cols] + dot(p.astype(BF), kv_ref[:, vals])

    @pl.when(info[2] >= 1)
    def _():
        fold(near_ref)

    @pl.when(info[2] >= 2)
    def _():
        fold(far_ref)

    for head in range(2):
        cols = slice(head * 128, head * 128 + 128)
        out_ref[:, cols] = (acc[:, cols] / sums[:, head : head + 1]).astype(BF)


EVERY = ("song", "tensor")


def other_half():
    pairs = []
    for song in range(16):
        for rank in range(8):
            pairs.append((song * 8 + rank, (song ^ 8) * 8 + (rank ^ 4)))
    return pairs


def to_sibling(value):
    return lax.ppermute(value, "song", [(i, i ^ 1) for i in range(16)])


def exchange(value, axis="tensor", groups=None):
    return lax.all_to_all(value, axis, 0, 0, axis_index_groups=groups, tiled=True)


def on_device(
    upper_codes,
    middle_codes,
    upper_table,
    dilated_weight,
    mixing_weight,
    upsample_weight,
    middle_table,
    norm_gain,
    qkv_weight,
):
    song = lax.axis_index("song")
    rank = lax.axis_index("tensor")
    core = song % 2
    x_hi = rank // 4
    begin = song * 256 + x_hi * HALF
    info = jnp.stack([core, begin, song]).astype(jnp.int32)

    dil_half = lax.dynamic_slice_in_dim(dilated_weight, core * 512, 512, 3)
    mix_half = lax.dynamic_slice_in_dim(mixing_weight, core * 512, 512, 1)
    mix_pack = jnp.concatenate([mix_half[:, i * 128 : i * 128 + 128] for i in range(4)], axis=2)
    tab_half = lax.dynamic_slice_in_dim(upper_table, core * 1024, 1024, 0)
    tab_pack = jnp.concatenate([tab_half[i * 256 : i * 256 + 256] for i in range(4)], axis=1)
    pack0 = jnp.concatenate([dil_half[0].reshape(384, 512), mix_pack[0], tab_pack], axis=0)
    got0 = lax.ppermute(pack0, EVERY, other_half())
    sib0 = to_sibling(got0)
    pack1 = jnp.concatenate([dil_half[1:].reshape(3, 384, 512), mix_pack[1:]], axis=1)
    pack1, got0 = lax.optimization_barrier((pack1, got0))
    got1 = lax.ppermute(pack1, EVERY, other_half())
    sib1 = to_sibling(got1)
    got = [got0, got1[0], got1[1], got1[2]]
    sib = [sib0, sib1[0], sib1[1], sib1[2]]

    after = lax.ppermute(upper_codes[-40:], "song", [(i, i + 1) for i in range(15)])
    before = lax.ppermute(upper_codes[:40], "song", [(i + 1, i) for i in range(15)])
    codes = jnp.concatenate([after, upper_codes, before])
    codes = lax.dynamic_slice_in_dim(codes, x_hi * HALF, HALF + 80)[:, None]

    up_part = lax.dynamic_slice(upsample_weight, (song // 2 * 16, core * 2 * D), (16, 2 * D))
    mid_part = lax.dynamic_slice_in_dim(middle_table, song * 16, 16, 0)
    part = jnp.concatenate([up_part, mid_part], axis=1)
    parts = exchange(jnp.broadcast_to(part[None], (8, 16, 3 * D)))
    full = lax.all_gather(parts, "song", axis=0, tiled=False)
    full = full.reshape(8, 2, 8, 16, 3 * D)

    h, terms = call(
        first_kernel,
        (shape(ROWS[0], 256, dtype=F32), shape(4, ROWS[1], 256)),
        [pltpu.VMEM((ROWS[0], 256), F32)],
        n=5,
        name="cond0",
    )(info, codes, upper_table, dilated_weight[0], got[0], sib[0])
    for level in range(4):
        terms = exchange(terms, groups=Y_GROUPS)
        spread = call(relu_kernel, shape(*terms.shape), smem=0, n=1, name="relu")(terms)
        r = exchange(spread, groups=Y_GROUPS)
        if level < 3:
            h, terms = call(
                functools.partial(middle_kernel, level),
                (shape(ROWS[level + 1], 256, dtype=F32), shape(4, ROWS[level + 2], 256)),
                [pltpu.VMEM((ROWS[level + 1], 256), F32)],
                n=8,
                name="cond",
            )(
                info,
                r,
                h,
                mixing_weight[level],
                got[level],
                sib[level],
                dilated_weight[level + 1],
                got[level + 1],
                sib[level + 1],
            )
        else:
            spread = call(last_kernel, shape(8, HALF, 256), n=5, name="cond_end")(
                info, r, h, mixing_weight[level], got[level], sib[level]
            )
    hf = exchange(spread)

    mid = middle_codes.reshape(256, 4).T
    mid = (mid % 256) // 16 * 128 + mid // 256 * 16 + mid % 16
    queries, kv = frames(mid[:, :, None], hf, norm_gain[None], qkv_weight.reshape(D, 768), full)

    far = lax.ppermute(kv, "song", [(i, i + 2) for i in range(14)])
    pair = lax.ppermute(kv, "song", [(i, i + 1) for i in range(0, 16, 2)])
    relay = lax.ppermute(far, "song", [(i + 1, i) for i in range(0, 16, 2)])
    near = jnp.where(core == 1, pair, relay)
    acc, top, total = call(
        own_kernel,
        (shape(1024, 256, dtype=F32), shape(1024, 2, dtype=F32), shape(1024, 2, dtype=F32)),
        smem=0,
        n=2,
        name="own",
    )(queries, kv)
    return call(
        past_kernel,
        shape(1024, 256),
        [pltpu.VMEM((1024, 256), F32), pltpu.VMEM((1024, 2), F32), pltpu.VMEM((1024, 2), F32)],
        n=6,
        flops=3 * 10**9,
        name="past",
    )(info, queries, near, far, acc, top, total)


def solution(mesh):
    placed = (
        P("song"),
        P("song"),
        P(None, "tensor"),
        P(None, None, "tensor", None),
        P(None, None, "tensor"),
        P("tensor", None),
        P("tensor", None),
        P(),
        P(None, "tensor", None),
    )
    return jax.shard_map(
        on_device, mesh=mesh, in_specs=placed, out_specs=P("song", "tensor"), check_vma=False
    )
```

```python
import functools

import jax
import jax.numpy as jnp
from jax import lax
from jax.experimental import pallas as pl
from jax.experimental.pallas import tpu as pltpu
from jax.sharding import PartitionSpec as P

BF = jnp.bfloat16
F32 = jnp.float32
D = 1920
C = 1024
VOCAB = 2048
UPPER = 4096
HALF = 128
HALO = (40, 39, 36, 27, 0)
ROWS = (208, 208, 208, 192, 128)
VMEM_LIMIT = 60 << 20

Y_GROUPS = [[0, 1, 2, 3], [4, 5, 6, 7]]


def params(**kw):
    return pltpu.CompilerParams(vmem_limit_bytes=VMEM_LIMIT, **kw)


def cost(flops, nbytes, trans=0):
    return pl.CostEstimate(flops=flops, bytes_accessed=nbytes, transcendentals=trans)


def dot(a, b):
    return jnp.dot(a, b, preferred_element_type=F32)


def send_terms(level, info, h_ref, own_ref, got_ref, sib_ref, out_ref):
    step = 3**level
    core = info[0]
    count = HALF + 2 * HALO[level + 1]
    padded = out_ref.shape[1]
    rows = h_ref.shape[0]
    first = info[1] - HALO[level]
    pos = first + lax.broadcasted_iota(jnp.int32, (rows, 1), 0)
    inside = (pos >= 0) & (pos < UPPER)
    h_ref[...] = jnp.where(inside, h_ref[...], 0.0)
    own_at = pl.multiple_of(core * 512, 512)
    sib_at = pl.multiple_of((1 - core) * 512, 512)
    near = jnp.zeros((count, 512), F32)
    away = jnp.zeros((count, 512), F32)
    for tap in range(3):
        hb = jnp.maximum(h_ref[tap * step : tap * step + count, :], 0.0).astype(BF)
        mine, other = hb[:, :128], hb[:, 128:]
        lines = slice(tap * 128, tap * 128 + 128)
        near += dot(mine, own_ref[tap, :, pl.ds(own_at, 512)]) + dot(other, got_ref[lines, :])
        away += dot(mine, own_ref[tap, :, pl.ds(sib_at, 512)]) + dot(other, sib_ref[lines, :])
    near, away = near.astype(BF), away.astype(BF)
    for y in range(4):
        cols = slice(y * 128, y * 128 + 128)
        out_ref[y, :count, :128] = near[:, cols]
        out_ref[y, :count, 128:] = away[:, cols]
        if padded > count:
            out_ref[y, count:, :] = jnp.zeros((padded - count, 256), BF)


def first_kernel(info, codes_ref, table_ref, dil_hbm, got_ref, sib_ref, h_ref, out_ref, work, own_ref, sem):
    fetch = pltpu.make_async_copy(dil_hbm.at[0], own_ref, sem)
    fetch.start()
    codes = codes_ref[...]
    rows = codes.shape[0]
    lane = lax.broadcasted_iota(jnp.int32, (rows, 1024), 1)
    core = info[0]
    one = jnp.ones((), BF)
    zero = jnp.zeros((), BF)
    h_own = jnp.zeros((rows, 128), F32)
    h_oth = jnp.zeros((rows, 128), F32)
    for part in range(2):
        hot = jnp.where(codes == lane + part * 1024, one, zero)
        h_own += dot(hot, table_ref[part * 1024 : part * 1024 + 1024, :])
    for src, begin in ((got_ref, core * 1024), (sib_ref, (1 - core) * 1024)):
        hot = jnp.where(codes - begin == lane, one, zero)
        for q in range(4):
            h_oth += dot(hot[:, q * 256 : q * 256 + 256], src[512:768, q * 128 : q * 128 + 128])
    work[:, :128] = h_own
    work[:, 128:] = h_oth
    h_ref[...] = work[...]
    fetch.wait()
    send_terms(0, info, work, own_ref, got_ref, sib_ref, out_ref)


def mixed(level, info, r_ref, h_ref, mix_ref, got_ref, sib_ref):
    step = 3**level
    core = info[0]
    count = HALF + 2 * HALO[level + 1]
    h_own = h_ref[step : step + count, :128]
    h_oth = h_ref[step : step + count, 128:]
    for half, got, begin in ((0, got_ref, core * 512), (1, sib_ref, (1 - core) * 512)):
        r = jnp.concatenate(
            [r_ref[y, :, half * 128 : half * 128 + 128] for y in range(4)], axis=1
        )[:count]
        h_own += dot(r, mix_ref[pl.ds(pl.multiple_of(begin, 512), 512), :])
        for y in range(4):
            cols = slice(y * 128, y * 128 + 128)
            h_oth += dot(r[:, cols], got[:, cols])
    return h_own, h_oth


def lines_of(level, hbm, begin, size):
    ref = hbm if level == 0 else hbm.at[level - 1]
    return ref.at[pl.ds(begin, size), :]


def mixing_copies(level, mix_hbm, got_hbm, sib_hbm, mix_ref, got_ref, sib_ref, sems):
    pairs = (
        (mix_hbm.at[level], mix_ref),
        (lines_of(level, got_hbm, 384, 128), got_ref),
        (lines_of(level, sib_hbm, 384, 128), sib_ref),
    )
    return [pltpu.make_async_copy(a, b, sems.at[i]) for i, (a, b) in enumerate(pairs)]


def middle_kernel(
    level, info, r_ref, h_ref, mix_hbm, got_hbm, sib_hbm, dil_hbm, got1_hbm, sib1_hbm, new_ref, out_ref,
    mix_ref, got_ref, sib_ref, sems, own_ref, got1_ref, sib1_ref, sems1, work,
):
    first = mixing_copies(level, mix_hbm, got_hbm, sib_hbm, mix_ref, got_ref, sib_ref, sems)
    pairs = (
        (dil_hbm.at[level + 1], own_ref),
        (lines_of(level + 1, got1_hbm, 0, 384), got1_ref),
        (lines_of(level + 1, sib1_hbm, 0, 384), sib1_ref),
    )
    then = [pltpu.make_async_copy(a, b, sems1.at[i]) for i, (a, b) in enumerate(pairs)]
    for copy in first + then:
        copy.start()
    for copy in first:
        copy.wait()
    count = HALF + 2 * HALO[level + 1]
    h_own, h_oth = mixed(level, info, r_ref, h_ref, mix_ref, got_ref, sib_ref)
    if work.shape[0] > count:
        work[count:, :] = jnp.zeros((work.shape[0] - count, 256), F32)
    work[:count, :128] = h_own
    work[:count, 128:] = h_oth
    new_ref[...] = work[...]
    for copy in then:
        copy.wait()
    send_terms(level + 1, info, work, own_ref, got1_ref, sib1_ref, out_ref)


def last_kernel(info, r_ref, h_ref, mix_hbm, got_hbm, sib_hbm, out_ref, mix_ref, got_ref, sib_ref, sems):
    first = mixing_copies(3, mix_hbm, got_hbm, sib_hbm, mix_ref, got_ref, sib_ref, sems)
    for copy in first:
        copy.start()
    for copy in first:
        copy.wait()
    h_own, h_oth = mixed(3, info, r_ref, h_ref, mix_ref, got_ref, sib_ref)
    h_own, h_oth = h_own.astype(BF), h_oth.astype(BF)
    for peer in range(8):
        out_ref[peer, :, :128] = h_own
        out_ref[peer, :, 128:] = h_oth


def call(body, outs, scratch=(), smem=1, n=0, hbm=0, after=0, flops=10**9, name=None):
    def spec(space):
        return pl.BlockSpec(memory_space=space)

    specs = [spec(pltpu.SMEM)] * smem + [spec(pltpu.VMEM)] * n
    specs += [spec(pl.ANY)] * hbm + [spec(pltpu.VMEM)] * after
    return pl.pallas_call(
        body,
        out_shape=outs,
        in_specs=specs,
        out_specs=jax.tree.map(lambda _: spec(pltpu.VMEM), outs),
        scratch_shapes=list(scratch),
        compiler_params=params(),
        cost_estimate=cost(flops, 4 << 20),
        name=name,
    )


def shape(*dims, dtype=BF):
    return jax.ShapeDtypeStruct(dims, dtype)


COLS = 384


def frames_kernel(pair, codes_ref, hf_ref, gain_ref, qkv_ref, full_ref, q_ref, kv_ref, weights, table, hf, x, xn, hot, sems, table_sem):
    def weight_copy(phase, t):
        return pltpu.make_async_copy(
            full_ref.at[:, pair, t, :, pl.ds(phase * D, D)], weights.at[phase, t], sems.at[phase, t]
        )

    def table_copy(part):
        return pltpu.make_async_copy(
            full_ref.at[:, part, :, :, pl.ds(2 * D, D)], table.at[:, part], table_sem.at[part]
        )

    for part in range(2):
        table_copy(part).start()
    for phase in range(2):
        for t in range(8):
            weight_copy(phase, t).start()
    for half in range(2):
        for j in range(8):
            at = 0 if j // 4 == half else 128
            hf[half * 128 : half * 128 + 128, j * 128 : j * 128 + 128] = hf_ref[
                half * 4 + j % 4, :, at : at + 128
            ]
    lane = lax.broadcasted_iota(jnp.int32, (512, VOCAB), 1)
    hot[...] = jnp.where(codes_ref[...] == lane, jnp.ones((), BF), jnp.zeros((), BF))
    for part in range(2):
        table_copy(part).wait()
    for n in range(0, D, COLS):
        cols = slice(n, n + COLS)
        x[:, cols] = dot(hot[...], table[:, :, :, :, cols].reshape(VOCAB, COLS))
    for phase in range(2):
        for t in range(8):
            weight_copy(phase, t).wait()
        lines = slice(phase * 256, phase * 256 + 256)
        total = jnp.zeros((256, 1), F32)
        for n in range(0, D, COLS):
            cols = slice(n, n + COLS)
            y = x[lines, cols] + dot(hf[...], weights[phase, :, :, :, cols].reshape(C, COLS))
            x[lines, cols] = y
            total += jnp.sum(y, axis=1, keepdims=True)
        mean = total * (1.0 / D)
        square = jnp.zeros((256, 1), F32)
        for n in range(0, D, COLS):
            y = x[lines, n : n + COLS] - mean
            square += jnp.sum(y * y, axis=1, keepdims=True)
        factor = lax.rsqrt(square * (1.0 / D) + 1e-5)
        for n in range(0, D, COLS):
            cols = slice(n, n + COLS)
            xn[:, cols] = ((x[lines, cols] - mean) * factor * gain_ref[:, cols]).astype(BF)
        for head in range(2):
            y = dot(xn[...], qkv_ref[:, head * 384 : head * 384 + 384]).astype(BF)
            cols = slice(head * 128, head * 128 + 128)
            q_ref[lines, cols] = y[:, :128]
            kv_ref[lines, cols] = y[:, 128:256]
            kv_ref[lines, 256 + head * 128 : 384 + head * 128] = y[:, 256:]


def frames(pair, codes, hf, gain, qkv, full):
    vm = pl.BlockSpec(memory_space=pltpu.VMEM)
    return pl.pallas_call(
        functools.partial(frames_kernel, pair),
        out_shape=(shape(512, 256), shape(512, 512)),
        in_specs=[vm, vm, vm, vm, pl.BlockSpec(memory_space=pltpu.HBM)],
        out_specs=(vm, vm),
        scratch_shapes=[
            pltpu.VMEM((2, 8, 8, 16, D), BF),
            pltpu.VMEM((8, 2, 8, 16, D), BF),
            pltpu.VMEM((256, C), BF),
            pltpu.VMEM((512, D), F32),
            pltpu.VMEM((256, D), BF),
            pltpu.VMEM((512, VOCAB), BF),
            pltpu.SemaphoreType.DMA((2, 8)),
            pltpu.SemaphoreType.DMA((2,)),
        ],
        compiler_params=params(),
        cost_estimate=cost(8 * 10**9, 20 << 20),
        name="frames",
    )(codes, hf, gain, qkv, full)


SCALE = 128**-0.5 * 1.4426950408889634


def scores_of(q, k):
    return lax.dot_general(q, k, (((1,), (1,)), ((), ())), preferred_element_type=F32) * SCALE


def own_kernel(q0_ref, q1_ref, kv0_ref, kv1_ref, acc_ref, top_ref, sum_ref):
    for head in range(2):
        cols = slice(head * 128, head * 128 + 128)
        vals = slice(256 + head * 128, 384 + head * 128)
        for part in range(2):
            keys = part * 128 + 128
            wide = (slice(0, keys), slice(256, 256 + keys))
            k = jnp.concatenate([ref[at, cols] for ref in (kv0_ref, kv1_ref) for at in wide], axis=0)
            v = jnp.concatenate([ref[at, vals] for ref in (kv0_ref, kv1_ref) for at in wide], axis=0)
            col = lax.broadcasted_iota(jnp.int32, (128, 4 * keys), 1)
            col = col % keys * 4 + col // keys
            row = (part * 128 + lax.broadcasted_iota(jnp.int32, (128, 4 * keys), 0)) * 4
            for phase in range(4):
                at = phase % 2 * 256 + part * 128
                q = (q0_ref, q1_ref)[phase // 2][at : at + 128, cols]
                s = jnp.where(col <= row + phase, scores_of(q, k), -1e30)
                top = jnp.max(s, axis=1, keepdims=True)
                p = jnp.exp2(s - top)
                at = phase * 256 + part * 128
                lines = slice(at, at + 128)
                top_ref[lines, head : head + 1] = top
                sum_ref[lines, head : head + 1] = jnp.sum(p, axis=1, keepdims=True)
                acc_ref[lines, cols] = dot(p.astype(BF), v)


def fold(q0_ref, q1_ref, kv0_ref, kv1_ref, acc, tops, sums):
    for head in range(2):
        cols = slice(head * 128, head * 128 + 128)
        vals = slice(256 + head * 128, 384 + head * 128)
        k = jnp.concatenate([kv0_ref[:, cols], kv1_ref[:, cols]], axis=0)
        v = jnp.concatenate([kv0_ref[:, vals], kv1_ref[:, vals]], axis=0)
        for phase in range(4):
            at = phase % 2 * 256
            lines = slice(phase * 256, phase * 256 + 256)
            s = scores_of((q0_ref, q1_ref)[phase // 2][at : at + 256, cols], k)
            old = tops[lines, head : head + 1]
            top = jnp.maximum(old, jnp.max(s, axis=1, keepdims=True))
            p = jnp.exp2(s - top)
            keep = jnp.exp2(old - top)
            tops[lines, head : head + 1] = top
            sums[lines, head : head + 1] = keep * sums[lines, head : head + 1] + jnp.sum(
                p, axis=1, keepdims=True
            )
            acc[lines, cols] = keep * acc[lines, cols] + dot(p.astype(BF), v)


def far_kernel(info, q0_ref, q1_ref, kv0_ref, kv1_ref, acc_ref, top_ref, sum_ref, acc, tops, sums):
    acc[...] = acc_ref[...]
    tops[...] = top_ref[...]
    sums[...] = sum_ref[...]

    @pl.when(info[2] >= 2)
    def _():
        fold(q0_ref, q1_ref, kv0_ref, kv1_ref, acc, tops, sums)


def near_kernel(info, q0_ref, q1_ref, kv0_ref, kv1_ref, acc_ref, top_ref, sum_ref, out_ref, acc, tops, sums, wide):
    acc[...] = acc_ref[...]
    tops[...] = top_ref[...]
    sums[...] = sum_ref[...]

    @pl.when(info[2] >= 1)
    def _():
        fold(q0_ref, q1_ref, kv0_ref, kv1_ref, acc, tops, sums)

    for head in range(2):
        cols = slice(head * 128, head * 128 + 128)
        for phase in range(4):
            lines = slice(phase * 256, phase * 256 + 256)
            wide[pl.ds(phase, 256, stride=4), :] = acc[lines, cols] / sums[lines, head : head + 1]
        out_ref[:, cols] = wide[...].astype(BF)


EVERY = ("song", "tensor")


def other_half():
    pairs = []
    for song in range(16):
        for rank in range(8):
            pairs.append((song * 8 + rank, (song ^ 8) * 8 + (rank ^ 4)))
    return pairs


def to_sibling(value):
    return lax.ppermute(value, "song", [(i, i ^ 1) for i in range(16)])


def exchange(value, axis="tensor", groups=None):
    return lax.all_to_all(value, axis, 0, 0, axis_index_groups=groups, tiled=True)


def on_device(
    upper_codes,
    middle_codes,
    upper_table,
    dilated_weight,
    mixing_weight,
    upsample_weight,
    middle_table,
    norm_gain,
    qkv_weight,
):
    song = lax.axis_index("song")
    rank = lax.axis_index("tensor")
    core = song % 2
    x_hi = rank // 4
    begin = song * 256 + x_hi * HALF
    info = jnp.stack([core, begin, song]).astype(jnp.int32)

    after = lax.ppermute(upper_codes[-40:], "song", [(i, i + 1) for i in range(15)])
    before = lax.ppermute(upper_codes[:40], "song", [(i + 1, i) for i in range(15)])
    codes = jnp.concatenate([after, upper_codes, before])
    codes = lax.dynamic_slice_in_dim(codes, x_hi * HALF, HALF + 80)[:, None]

    dil_half = lax.dynamic_slice_in_dim(dilated_weight, core * 512, 512, 3)
    mix_half = lax.dynamic_slice_in_dim(mixing_weight, core * 512, 512, 1)
    mix_pack = jnp.concatenate([mix_half[:, i * 128 : i * 128 + 128] for i in range(4)], axis=2)
    tab_half = lax.dynamic_slice_in_dim(upper_table, core * 1024, 1024, 0)
    tab_pack = jnp.concatenate([tab_half[i * 256 : i * 256 + 256] for i in range(4)], axis=1)
    pack0 = jnp.concatenate([dil_half[0].reshape(384, 512), mix_pack[0], tab_pack], axis=0)
    got0 = lax.ppermute(pack0, EVERY, other_half())

    up_part = lax.dynamic_slice(upsample_weight, (song // 2 * 16, core * 2 * D), (16, 2 * D))
    mid_part = lax.dynamic_slice_in_dim(middle_table, song * 16, 16, 0)
    part = jnp.concatenate([up_part, mid_part], axis=1)
    part, pack0 = lax.optimization_barrier((part, pack0))
    parts = exchange(jnp.broadcast_to(part[None], (8, 16, 3 * D)))
    parts, got0 = lax.optimization_barrier((parts, got0))
    full = lax.all_gather(parts, "song", axis=0, tiled=False)
    full = full.reshape(8, 2, 8, 16, 3 * D)

    sib0 = to_sibling(got0)
    pack1 = jnp.concatenate([dil_half[1:].reshape(3, 384, 512), mix_pack[1:]], axis=1)
    pack1, got0 = lax.optimization_barrier((pack1, got0))
    got1 = lax.ppermute(pack1, EVERY, other_half())

    h, terms = call(
        first_kernel,
        (shape(ROWS[0], 256, dtype=F32), shape(4, ROWS[1], 256)),
        [pltpu.VMEM((ROWS[0], 256), F32), pltpu.VMEM((3, 128, 1024), BF), pltpu.SemaphoreType.DMA],
        n=2,
        hbm=1,
        after=2,
        name="cond0",
    )(info, codes, upper_table, dilated_weight, got0, sib0)
    got = sib = None
    for level in range(4):
        terms = exchange(terms, groups=Y_GROUPS)
        if level == 0:
            got1, terms = lax.optimization_barrier((got1, terms))
            sib1 = to_sibling(got1)
        total = terms[0].astype(F32)
        for y in range(1, 4):
            total = total + terms[y].astype(F32)
        r = jnp.maximum(total, 0.0).astype(BF)
        r = exchange(jnp.broadcast_to(r[None], terms.shape), groups=Y_GROUPS)
        scratch = [
            pltpu.VMEM((1024, 128), BF),
            pltpu.VMEM((128, 512), BF),
            pltpu.VMEM((128, 512), BF),
            pltpu.SemaphoreType.DMA((3,)),
        ]
        old = (got0, sib0) if level == 0 else (got1, sib1)
        if level < 3:
            scratch += [
                pltpu.VMEM((3, 128, 1024), BF),
                pltpu.VMEM((384, 512), BF),
                pltpu.VMEM((384, 512), BF),
                pltpu.SemaphoreType.DMA((3,)),
                pltpu.VMEM((ROWS[level + 1], 256), F32),
            ]
            h, terms = call(
                functools.partial(middle_kernel, level),
                (shape(ROWS[level + 1], 256, dtype=F32), shape(4, ROWS[level + 2], 256)),
                scratch,
                n=2,
                hbm=6,
                name="cond",
            )(info, r, h, mixing_weight, *old, dilated_weight, got1, sib1)
        else:
            spread = call(
                last_kernel, shape(8, HALF, 256), scratch, n=2, hbm=3, name="cond_end"
            )(info, r, h, mixing_weight, *old)
    hf = exchange(spread)

    mid = middle_codes.reshape(256, 4).T.reshape(1024, 1)
    mid = (mid % 256) // 16 * 128 + mid // 256 * 16 + mid % 16
    gain = norm_gain[None]
    qkv = qkv_weight.reshape(D, 768)

    def from_two_back(value):
        return lax.ppermute(value, "song", [(i, i + 2) for i in range(14)])

    q0, kv0 = frames(0, mid[:512], hf, gain, qkv, full)
    far0 = from_two_back(kv0)
    q1, kv1 = frames(1, mid[512:], hf, gain, qkv, full)
    far1 = from_two_back(kv1)
    near0 = to_sibling(jnp.where(core == 0, kv0, far0))
    state = (shape(1024, 256, dtype=F32), shape(1024, 2, dtype=F32), shape(1024, 2, dtype=F32))
    work = [pltpu.VMEM((1024, 256), F32), pltpu.VMEM((1024, 2), F32), pltpu.VMEM((1024, 2), F32)]
    kept = call(own_kernel, state, smem=0, n=4, flops=10**9, name="own")(q0, q1, kv0, kv1)
    far1, kept = lax.optimization_barrier((far1, kept))
    near1 = to_sibling(jnp.where(core == 0, kv1, far1))
    kept = call(far_kernel, state, n=7, flops=2 * 10**9, name="far")(info, q0, q1, far0, far1, *kept)
    return call(
        near_kernel,
        shape(1024, 256),
        work + [pltpu.VMEM((1024, 128), F32)],
        n=7,
        flops=2 * 10**9,
        name="near",
    )(info, q0, q1, near0, near1, *kept)


def solution(mesh):
    placed = (
        P("song"),
        P("song"),
        P(None, "tensor"),
        P(None, None, "tensor", None),
        P(None, None, "tensor"),
        P("tensor", None),
        P("tensor", None),
        P(),
        P(None, "tensor", None),
    )
    return jax.shard_map(
        on_device, mesh=mesh, in_specs=placed, out_specs=P("song", "tensor"), check_vma=False
    )
```

```python
import functools

import jax
import jax.numpy as jnp
from jax import lax
from jax.experimental import pallas as pl
from jax.experimental.pallas import tpu as pltpu
from jax.sharding import PartitionSpec as P

BF = jnp.bfloat16
F32 = jnp.float32
D = 1920
C = 1024
VOCAB = 2048
UPPER = 4096
HALF = 128
HALO = (40, 39, 36, 27, 0)
ROWS = (208, 208, 208, 192, 128)
VMEM_LIMIT = 60 << 20

Y_GROUPS = [[0, 1, 2, 3], [4, 5, 6, 7]]


def params(**kw):
    return pltpu.CompilerParams(vmem_limit_bytes=VMEM_LIMIT, **kw)


def cost(flops, nbytes, trans=0):
    return pl.CostEstimate(flops=flops, bytes_accessed=nbytes, transcendentals=trans)


def dot(a, b):
    return jnp.dot(a, b, preferred_element_type=F32)


def dilated_copies(level, info, dil_hbm, got_hbm, sib_hbm, near_ref, away_ref, sems):
    own = pl.multiple_of(info[0] * 512, 512)
    other = pl.multiple_of((1 - info[0]) * 512, 512)
    pairs = []
    for ref, hbm, begin in ((near_ref, got_hbm, own), (away_ref, sib_hbm, other)):
        part = hbm if level == 0 else hbm.at[level - 1]
        pairs.append((dil_hbm.at[level, :, :, pl.ds(begin, 512)], ref.at[:, pl.ds(0, 128), :]))
        for tap in range(3):
            pairs.append((part.at[pl.ds(tap * 128, 128), :], ref.at[tap, pl.ds(128, 128), :]))
    return [pltpu.make_async_copy(a, b, sems.at[i]) for i, (a, b) in enumerate(pairs)]


def mixing_copies(level, info, mix_hbm, got_hbm, sib_hbm, mix_ref, sems):
    pairs = []
    for half, hbm in enumerate((got_hbm, sib_hbm)):
        part = hbm if level == 0 else hbm.at[level - 1]
        begin = info[0] if half == 0 else 1 - info[0]
        rows = pl.ds(pl.multiple_of(begin * 512, 512), 512)
        pairs.append((mix_hbm.at[level, rows, :], mix_ref.at[half, :, pl.ds(0, 128)]))
        for y in range(4):
            pairs.append(
                (
                    part.at[pl.ds(384, 128), pl.ds(y * 128, 128)],
                    mix_ref.at[half, pl.ds(y * 128, 128), pl.ds(128, 128)],
                )
            )
    return [pltpu.make_async_copy(a, b, sems.at[i]) for i, (a, b) in enumerate(pairs)]


def send_terms(level, info, h_ref, near_ref, away_ref, out_ref):
    step = 3**level
    count = HALF + 2 * HALO[level + 1]
    padded = out_ref.shape[1]
    rows = h_ref.shape[0]
    first = info[1] - HALO[level]
    pos = first + lax.broadcasted_iota(jnp.int32, (rows, 1), 0)
    inside = (pos >= 0) & (pos < UPPER)
    h_ref[...] = jnp.where(inside, jnp.maximum(h_ref[...], 0.0), 0.0)
    taps = [h_ref[tap * step : tap * step + count, :].astype(BF) for tap in range(3)]
    for half, ref in enumerate((near_ref, away_ref)):
        total = dot(taps[0], ref[0]) + dot(taps[1], ref[1]) + dot(taps[2], ref[2])
        total = total.astype(BF)
        for y in range(4):
            out_ref[y, :count, half * 128 : half * 128 + 128] = total[:, y * 128 : y * 128 + 128]
    if padded > count:
        for y in range(4):
            out_ref[y, count:, :] = jnp.zeros((padded - count, 256), BF)


def start(copies):
    for copy in copies:
        copy.start()


def finish(copies):
    for copy in copies:
        copy.wait()


DILATED = [pltpu.VMEM((3, 256, 512), BF), pltpu.VMEM((3, 256, 512), BF), pltpu.SemaphoreType.DMA((8,))]
MIXING = [pltpu.VMEM((2, 512, 256), BF), pltpu.SemaphoreType.DMA((10,))]


def first_kernel(info, codes_ref, table_ref, dil_hbm, got_ref, sib_ref, h_ref, out_ref, near_ref, away_ref, sems, work):
    copies = dilated_copies(0, info, dil_hbm, got_ref, sib_ref, near_ref, away_ref, sems)
    start(copies)
    codes = codes_ref[...]
    rows = codes.shape[0]
    lane = lax.broadcasted_iota(jnp.int32, (rows, 1024), 1)
    core = info[0]
    one = jnp.ones((), BF)
    zero = jnp.zeros((), BF)
    h_own = jnp.zeros((rows, 128), F32)
    h_oth = jnp.zeros((rows, 128), F32)
    for src, begin in ((got_ref, core * 1024), (sib_ref, (1 - core) * 1024)):
        hot = jnp.where(codes - begin == lane, one, zero)
        h_own += dot(hot, table_ref[pl.ds(pl.multiple_of(begin, 1024), 1024), :])
        for q in range(4):
            h_oth += dot(hot[:, q * 256 : q * 256 + 256], src[512:768, q * 128 : q * 128 + 128])
    work[:, :128] = h_own
    work[:, 128:] = h_oth
    h_ref[...] = work[...]
    finish(copies)
    send_terms(0, info, work, near_ref, away_ref, out_ref)


def mixed(level, r_ref, h_ref, mix_ref):
    step = 3**level
    count = HALF + 2 * HALO[level + 1]
    h = h_ref[step : step + count, :]
    for half in range(2):
        r = jnp.concatenate([r_ref[y, :, half * 128 : half * 128 + 128] for y in range(4)], axis=1)
        h += dot(r, mix_ref[half])[:count]
    return h


def middle_kernel(level, info, r_ref, h_ref, mix_hbm, got_hbm, sib_hbm, dil_hbm, got1_hbm, sib1_hbm, new_ref, out_ref, mix_ref, mix_sems, near_ref, away_ref, sems, work):
    first = mixing_copies(level, info, mix_hbm, got_hbm, sib_hbm, mix_ref, mix_sems)
    then = dilated_copies(level + 1, info, dil_hbm, got1_hbm, sib1_hbm, near_ref, away_ref, sems)
    start(first)
    start(then)
    finish(first)
    count = HALF + 2 * HALO[level + 1]
    if work.shape[0] > count:
        work[count:, :] = jnp.zeros((work.shape[0] - count, 256), F32)
    work[:count, :] = mixed(level, r_ref, h_ref, mix_ref)
    new_ref[...] = work[...]
    finish(then)
    send_terms(level + 1, info, work, near_ref, away_ref, out_ref)


def last_kernel(info, r_ref, h_ref, mix_hbm, got_hbm, sib_hbm, out_ref, mix_ref, mix_sems):
    copies = mixing_copies(3, info, mix_hbm, got_hbm, sib_hbm, mix_ref, mix_sems)
    start(copies)
    finish(copies)
    h = mixed(3, r_ref, h_ref, mix_ref).astype(BF)
    for peer in range(8):
        out_ref[peer] = h


def call(body, outs, scratch=(), smem=1, n=0, hbm=0, after=0, flops=10**9, name=None):
    def spec(space):
        return pl.BlockSpec(memory_space=space)

    specs = [spec(pltpu.SMEM)] * smem + [spec(pltpu.VMEM)] * n
    specs += [spec(pl.ANY)] * hbm + [spec(pltpu.VMEM)] * after
    return pl.pallas_call(
        body,
        out_shape=outs,
        in_specs=specs,
        out_specs=jax.tree.map(lambda _: spec(pltpu.VMEM), outs),
        scratch_shapes=list(scratch),
        compiler_params=params(),
        cost_estimate=cost(flops, 4 << 20),
        name=name,
    )


def shape(*dims, dtype=BF):
    return jax.ShapeDtypeStruct(dims, dtype)


CHUNKS = ((0, 512), (512, 512), (1024, 512), (1536, 384))


def embed_kernel(codes_ref, full_ref, out_ref, table, hot, sems):
    def fetch(i):
        begin, size = CHUNKS[i]
        return pltpu.make_async_copy(
            full_ref.at[:, :, :, :, pl.ds(2 * D + begin, size)],
            table.at[:, :, :, :, pl.ds(begin, size)],
            sems.at[i],
        )

    start([fetch(i) for i in range(4)])
    lane = lax.broadcasted_iota(jnp.int32, (256, VOCAB), 1)

    def body(m, carry):
        lines = pl.ds(pl.multiple_of(m * 256, 256), 256)
        hot[...] = jnp.where(codes_ref[lines, :] == lane, jnp.ones((), BF), jnp.zeros((), BF))
        for i, (begin, size) in enumerate(CHUNKS):
            cols = slice(begin, begin + size)

            @pl.when(m == 0)
            def _():
                fetch(i).wait()

            out_ref[lines, cols] = dot(hot[...], table[:, :, :, :, cols].reshape(VOCAB, size)).astype(BF)
        return carry

    lax.fori_loop(0, 4, body, 0)


def embed(codes, full):
    return pl.pallas_call(
        embed_kernel,
        out_shape=shape(1024, D),
        in_specs=[pl.BlockSpec(memory_space=pltpu.VMEM), pl.BlockSpec(memory_space=pltpu.HBM)],
        out_specs=pl.BlockSpec(memory_space=pltpu.VMEM),
        scratch_shapes=[
            pltpu.VMEM((8, 2, 8, 16, D), BF),
            pltpu.VMEM((256, VOCAB), BF),
            pltpu.SemaphoreType.DMA((4,)),
        ],
        compiler_params=params(),
        cost_estimate=cost(8 * 10**9, 12 << 20),
        name="embed",
    )(codes, full)


def frames_kernel(pair, emb_ref, hf_ref, gain_ref, qkv_ref, full_ref, q_ref, kv_ref, weights, emb, hf, x, xn, sems, emb_sem):
    def weight_copy(phase, t):
        cols = pl.ds(pl.multiple_of(phase * D, 128), D)
        return pltpu.make_async_copy(
            full_ref.at[:, pair, t, :, cols], weights.at[phase, t], sems.at[phase, t]
        )

    fetch = pltpu.make_async_copy(emb_ref.at[pl.ds(pair * 512, 512), :], emb, emb_sem)
    fetch.start()
    for phase in range(2):
        start([weight_copy(phase, t) for t in range(8)])
    for half in range(2):
        for j in range(8):
            at = 0 if j // 4 == half else 128
            hf[half * 128 : half * 128 + 128, j * 128 : j * 128 + 128] = hf_ref[
                half * 4 + j % 4, :, at : at + 128
            ]
    fetch.wait()

    def body(phase, carry):
        finish([weight_copy(phase, t) for t in range(8)])
        lines = pl.ds(pl.multiple_of(phase * 256, 256), 256)
        total = jnp.zeros((256, 1), F32)
        for begin, size in CHUNKS:
            cols = slice(begin, begin + size)
            y = dot(hf[...], weights[phase, :, :, :, cols].reshape(C, size))
            y += emb[lines, cols].astype(F32)
            x[:, cols] = y
            total += jnp.sum(y, axis=1, keepdims=True)
        mean = total * (1.0 / D)
        square = jnp.zeros((256, 1), F32)
        for begin, size in CHUNKS:
            y = x[:, begin : begin + size] - mean
            square += jnp.sum(y * y, axis=1, keepdims=True)
        factor = lax.rsqrt(square * (1.0 / D) + 1e-5)
        for begin, size in CHUNKS:
            cols = slice(begin, begin + size)
            xn[:, cols] = ((x[:, cols] - mean) * factor * gain_ref[:, cols]).astype(BF)
        y = dot(xn[...], qkv_ref[...]).astype(BF)
        for head in range(2):
            at = head * 384
            cols = slice(head * 128, head * 128 + 128)
            q_ref[lines, cols] = y[:, at : at + 128]
            kv_ref[lines, cols] = y[:, at + 128 : at + 256]
            kv_ref[lines, 256 + head * 128 : 384 + head * 128] = y[:, at + 256 : at + 384]
        return carry

    lax.fori_loop(0, 2, body, 0)


def frames(pair, emb, hf, gain, qkv, full):
    vm = pl.BlockSpec(memory_space=pltpu.VMEM)
    return pl.pallas_call(
        functools.partial(frames_kernel, pair),
        out_shape=(shape(512, 256), shape(512, 512)),
        in_specs=[pl.BlockSpec(memory_space=pl.ANY), vm, vm, vm, pl.BlockSpec(memory_space=pltpu.HBM)],
        out_specs=(vm, vm),
        scratch_shapes=[
            pltpu.VMEM((2, 8, 8, 16, D), BF),
            pltpu.VMEM((512, D), BF),
            pltpu.VMEM((256, C), BF),
            pltpu.VMEM((256, D), F32),
            pltpu.VMEM((256, D), BF),
            pltpu.SemaphoreType.DMA((2, 8)),
            pltpu.SemaphoreType.DMA,
        ],
        compiler_params=params(),
        cost_estimate=cost(4 * 10**9, 12 << 20),
        name="frames",
    )(emb, hf, gain, qkv, full)


SCALE = 128**-0.5 * 1.4426950408889634


def scores_of(q, k):
    return lax.dot_general(q, k, (((1,), (1,)), ((), ())), preferred_element_type=F32) * SCALE


def gather_rows(dest, first, second):
    dest[:512, :] = first[...]
    dest[512:, :] = second[...]


def own_kernel(q0_ref, q1_ref, kv0_ref, kv1_ref, acc_ref, top_ref, sum_ref, q_all):
    gather_rows(q_all, q0_ref, q1_ref)
    for part in range(2):
        keys = part * 128 + 128
        wide = (slice(0, keys), slice(256, 256 + keys))
        kv = jnp.concatenate([ref[at, :] for ref in (kv0_ref, kv1_ref) for at in wide], axis=0)
        col = lax.broadcasted_iota(jnp.int32, (128, 4 * keys), 1)
        col = col % keys * 4 + col // keys
        row = (part * 128 + lax.broadcasted_iota(jnp.int32, (128, 4 * keys), 0)) * 4

        def body(phase, carry):
            lines = pl.ds(pl.multiple_of(phase * 256 + part * 128, 128), 128)
            seen = col <= row + phase
            for head in range(2):
                cols = slice(head * 128, head * 128 + 128)
                vals = slice(256 + head * 128, 384 + head * 128)
                s = jnp.where(seen, scores_of(q_all[lines, cols], kv[:, cols]), -1e30)
                top = jnp.max(s, axis=1, keepdims=True)
                p = jnp.exp2(s - top)
                top_ref[lines, head : head + 1] = top
                sum_ref[lines, head : head + 1] = jnp.sum(p, axis=1, keepdims=True)
                acc_ref[lines, cols] = dot(p.astype(BF), kv[:, vals])
            return carry

        lax.fori_loop(0, 4, body, 0)


def past_kernel(last, info, q0_ref, q1_ref, far_ref, near_ref, acc_ref, top_ref, sum_ref, *refs):
    if last:
        out_ref, acc, tops, sums, q_all, wide = refs
    else:
        acc, tops, sums, q_all = refs
    gather_rows(q_all, q0_ref, q1_ref)
    acc[...] = acc_ref[...]
    tops[...] = top_ref[...]
    sums[...] = sum_ref[...]

    def fold(kv_ref):
        def body(phase, carry):
            lines = pl.ds(pl.multiple_of(phase * 256, 256), 256)
            for head in range(2):
                cols = slice(head * 128, head * 128 + 128)
                vals = slice(256 + head * 128, 384 + head * 128)
                one = slice(head, head + 1)
                s = scores_of(q_all[lines, cols], kv_ref[:, cols])
                old = tops[lines, one]
                top = jnp.maximum(old, jnp.max(s, axis=1, keepdims=True))
                p = jnp.exp2(s - top)
                keep = jnp.exp2(old - top)
                tops[lines, one] = top
                sums[lines, one] = keep * sums[lines, one] + jnp.sum(p, axis=1, keepdims=True)
                acc[lines, cols] = keep * acc[lines, cols] + dot(p.astype(BF), kv_ref[:, vals])
            return carry

        lax.fori_loop(0, 4, body, 0)

    @pl.when(info[2] >= 2)
    def _():
        fold(far_ref)

    @pl.when(info[2] >= 1)
    def _():
        fold(near_ref)

    if last:
        for head in range(2):
            cols = slice(head * 128, head * 128 + 128)
            for phase in range(4):
                lines = slice(phase * 256, phase * 256 + 256)
                wide[pl.ds(phase, 256, stride=4), :] = acc[lines, cols] / sums[lines, head : head + 1]
            out_ref[:, cols] = wide[...].astype(BF)


EVERY = ("song", "tensor")


def other_half():
    pairs = []
    for song in range(16):
        for rank in range(8):
            pairs.append((song * 8 + rank, (song ^ 8) * 8 + (rank ^ 4)))
    return pairs


def to_sibling(value):
    return lax.ppermute(value, "song", [(i, i ^ 1) for i in range(16)])


def exchange(value, axis="tensor", groups=None):
    return lax.all_to_all(value, axis, 0, 0, axis_index_groups=groups, tiled=True)


def on_device(
    upper_codes,
    middle_codes,
    upper_table,
    dilated_weight,
    mixing_weight,
    upsample_weight,
    middle_table,
    norm_gain,
    qkv_weight,
):
    song = lax.axis_index("song")
    rank = lax.axis_index("tensor")
    core = song % 2
    x_hi = rank // 4
    begin = song * 256 + x_hi * HALF
    info = jnp.stack([core, begin, song]).astype(jnp.int32)

    after = lax.ppermute(upper_codes[-40:], "song", [(i, i + 1) for i in range(15)])
    before = lax.ppermute(upper_codes[:40], "song", [(i + 1, i) for i in range(15)])
    codes = jnp.concatenate([after, upper_codes, before])
    codes = lax.dynamic_slice_in_dim(codes, x_hi * HALF, HALF + 80)[:, None]

    dil_half = lax.dynamic_slice_in_dim(dilated_weight, core * 512, 512, 3)
    mix_half = lax.dynamic_slice_in_dim(mixing_weight, core * 512, 512, 1)
    mix_pack = jnp.concatenate([mix_half[:, i * 128 : i * 128 + 128] for i in range(4)], axis=2)
    tab_half = lax.dynamic_slice_in_dim(upper_table, core * 1024, 1024, 0)
    tab_pack = jnp.concatenate([tab_half[i * 256 : i * 256 + 256] for i in range(4)], axis=1)
    pack0 = jnp.concatenate([dil_half[0].reshape(384, 512), mix_pack[0], tab_pack], axis=0)
    got0 = lax.ppermute(pack0, EVERY, other_half())

    up_part = lax.dynamic_slice(upsample_weight, (song // 2 * 16, core * 2 * D), (16, 2 * D))
    mid_part = lax.dynamic_slice_in_dim(middle_table, song * 16, 16, 0)
    part = jnp.concatenate([up_part, mid_part], axis=1)
    parts = lax.all_gather(part, "tensor", axis=0, tiled=False)

    sib0 = to_sibling(got0)
    pack1 = jnp.concatenate([dil_half[1:].reshape(3, 384, 512), mix_pack[1:]], axis=1)
    pack1, got0 = lax.optimization_barrier((pack1, got0))
    got1 = lax.ppermute(pack1, EVERY, other_half())

    h, terms = call(
        first_kernel,
        (shape(ROWS[0], 256, dtype=F32), shape(4, ROWS[1], 256)),
        [*DILATED, pltpu.VMEM((ROWS[0], 256), F32)],
        n=2,
        hbm=1,
        after=2,
        name="cond0",
    )(info, codes, upper_table, dilated_weight, got0, sib0)
    for level in range(4):
        terms = exchange(terms, groups=Y_GROUPS)
        if level == 0:
            parts, got1, terms = lax.optimization_barrier((parts, got1, terms))
            full = lax.all_gather(parts, "song", axis=0, tiled=False).reshape(8, 2, 8, 16, 3 * D)
            sib1 = to_sibling(got1)
        total = terms[0].astype(F32)
        for y in range(1, 4):
            total = total + terms[y].astype(F32)
        r = jnp.maximum(total, 0.0).astype(BF)
        r = exchange(jnp.broadcast_to(r[None], terms.shape), groups=Y_GROUPS)
        old = (got0, sib0) if level == 0 else (got1, sib1)
        if level < 3:
            h, terms = call(
                functools.partial(middle_kernel, level),
                (shape(ROWS[level + 1], 256, dtype=F32), shape(4, ROWS[level + 2], 256)),
                [*MIXING, *DILATED, pltpu.VMEM((ROWS[level + 1], 256), F32)],
                n=2,
                hbm=6,
                name="cond",
            )(info, r, h, mixing_weight, *old, dilated_weight, got1, sib1)
        else:
            spread = call(
                last_kernel, shape(8, HALF, 256), MIXING, n=2, hbm=3, name="cond_end"
            )(info, r, h, mixing_weight, *old)
    hf = exchange(spread)

    mid = middle_codes.reshape(256, 4).T.reshape(1024, 1)
    mid = (mid % 256) // 16 * 128 + mid // 256 * 16 + mid % 16
    gain = norm_gain[None]
    qkv = qkv_weight.reshape(D, 768)

    def from_two_back(value):
        return lax.ppermute(value, "song", [(i, i + 2) for i in range(14)])

    emb = embed(mid, full)
    q0, kv0 = frames(0, emb, hf, gain, qkv, full)
    far0 = from_two_back(kv0)
    q1, kv1 = frames(1, emb, hf, gain, qkv, full)
    far1 = from_two_back(kv1)
    near0 = to_sibling(jnp.where(core == 0, kv0, far0))
    state = (shape(1024, 256, dtype=F32), shape(1024, 2, dtype=F32), shape(1024, 2, dtype=F32))
    work = [pltpu.VMEM((1024, 256), F32), pltpu.VMEM((1024, 2), F32), pltpu.VMEM((1024, 2), F32)]
    queries = pltpu.VMEM((1024, 256), BF)
    kept = call(own_kernel, state, [queries], smem=0, n=4, flops=10**9, name="own")(q0, q1, kv0, kv1)
    kept = call(
        functools.partial(past_kernel, False), state, [queries], n=7, flops=2 * 10**9, name="past"
    )(info, q0, q1, far0, near0, *kept)
    near1 = to_sibling(jnp.where(core == 0, kv1, far1))
    return call(
        functools.partial(past_kernel, True),
        shape(1024, 256),
        [*work, queries, pltpu.VMEM((1024, 128), F32)],
        n=7,
        flops=2 * 10**9,
        name="past_end",
    )(info, q0, q1, far1, near1, *kept)


def solution(mesh):
    placed = (
        P("song"),
        P("song"),
        P(None, "tensor"),
        P(None, None, "tensor", None),
        P(None, None, "tensor"),
        P("tensor", None),
        P("tensor", None),
        P(),
        P(None, "tensor", None),
    )
    return jax.shard_map(
        on_device, mesh=mesh, in_specs=placed, out_specs=P("song", "tensor"), check_vma=False
    )
```

```python
import functools

import jax
import jax.numpy as jnp
from jax import lax
from jax.experimental import pallas as pl
from jax.experimental.pallas import tpu as pltpu
from jax.sharding import PartitionSpec as P

BF = jnp.bfloat16
F32 = jnp.float32
D = 1920
C = 1024
VOCAB = 2048
UPPER = 4096
HALF = 128
HALO = (40, 39, 36, 27, 0)
ROWS = (208, 208, 208, 192, 128)
VMEM_LIMIT = 60 << 20

Y_GROUPS = [[0, 1, 2, 3], [4, 5, 6, 7]]


def params(**kw):
    return pltpu.CompilerParams(vmem_limit_bytes=VMEM_LIMIT, **kw)


def cost(flops, nbytes, trans=0):
    return pl.CostEstimate(flops=flops, bytes_accessed=nbytes, transcendentals=trans)


def dot(a, b):
    return jnp.dot(a, b, preferred_element_type=F32)


def dilated_copies(level, info, dil_hbm, got_hbm, sib_hbm, near_ref, away_ref, sems):
    own = pl.multiple_of(info[0] * 512, 512)
    other = pl.multiple_of((1 - info[0]) * 512, 512)
    pairs = []
    for ref, hbm, begin in ((near_ref, got_hbm, own), (away_ref, sib_hbm, other)):
        part = hbm if level < 2 else hbm.at[level - 2]
        pairs.append((dil_hbm.at[level, :, :, pl.ds(begin, 512)], ref.at[:, pl.ds(0, 128), :]))
        for tap in range(3):
            pairs.append((part.at[pl.ds(tap * 128, 128), :], ref.at[tap, pl.ds(128, 128), :]))
    return [pltpu.make_async_copy(a, b, sems.at[i]) for i, (a, b) in enumerate(pairs)]


def mixing_copies(level, info, mix_hbm, got_hbm, sib_hbm, mix_ref, sems):
    pairs = []
    for half, hbm in enumerate((got_hbm, sib_hbm)):
        part = hbm if level < 2 else hbm.at[level - 2]
        begin = info[0] if half == 0 else 1 - info[0]
        rows = pl.ds(pl.multiple_of(begin * 512, 512), 512)
        pairs.append((mix_hbm.at[level, rows, :], mix_ref.at[half, :, pl.ds(0, 128)]))
        for y in range(4):
            pairs.append(
                (
                    part.at[pl.ds(384, 128), pl.ds(y * 128, 128)],
                    mix_ref.at[half, pl.ds(y * 128, 128), pl.ds(128, 128)],
                )
            )
    return [pltpu.make_async_copy(a, b, sems.at[i]) for i, (a, b) in enumerate(pairs)]


def send_terms(level, info, h_ref, near_ref, away_ref, out_ref):
    step = 3**level
    count = HALF + 2 * HALO[level + 1]
    padded = out_ref.shape[1]
    rows = h_ref.shape[0]
    first = info[1] - HALO[level]
    pos = first + lax.broadcasted_iota(jnp.int32, (rows, 1), 0)
    inside = (pos >= 0) & (pos < UPPER)
    h_ref[...] = jnp.where(inside, jnp.maximum(h_ref[...], 0.0), 0.0)
    taps = [h_ref[tap * step : tap * step + count, :].astype(BF) for tap in range(3)]
    for half, ref in enumerate((near_ref, away_ref)):
        total = dot(taps[0], ref[0]) + dot(taps[1], ref[1]) + dot(taps[2], ref[2])
        total = total.astype(BF)
        for y in range(4):
            out_ref[y, :count, half * 128 : half * 128 + 128] = total[:, y * 128 : y * 128 + 128]
    if padded > count:
        for y in range(4):
            out_ref[y, count:, :] = jnp.zeros((padded - count, 256), BF)


def start(copies):
    for copy in copies:
        copy.start()


def finish(copies):
    for copy in copies:
        copy.wait()


DILATED = [pltpu.VMEM((3, 256, 512), BF), pltpu.VMEM((3, 256, 512), BF), pltpu.SemaphoreType.DMA((8,))]
MIXING = [pltpu.VMEM((2, 512, 256), BF), pltpu.SemaphoreType.DMA((10,))]


def first_kernel(info, codes_ref, table_ref, dil_hbm, got_ref, sib_ref, h_ref, out_ref, near_ref, away_ref, sems, work):
    copies = dilated_copies(0, info, dil_hbm, got_ref, sib_ref, near_ref, away_ref, sems)
    start(copies)
    codes = codes_ref[...]
    rows = codes.shape[0]
    lane = lax.broadcasted_iota(jnp.int32, (rows, 1024), 1)
    core = info[0]
    one = jnp.ones((), BF)
    zero = jnp.zeros((), BF)
    h_own = jnp.zeros((rows, 128), F32)
    h_oth = jnp.zeros((rows, 128), F32)
    for src, begin in ((got_ref, core * 1024), (sib_ref, (1 - core) * 1024)):
        hot = jnp.where(codes - begin == lane, one, zero)
        h_own += dot(hot, table_ref[pl.ds(pl.multiple_of(begin, 1024), 1024), :])
        for q in range(4):
            h_oth += dot(hot[:, q * 256 : q * 256 + 256], src[512:768, q * 128 : q * 128 + 128])
    work[:, :128] = h_own
    work[:, 128:] = h_oth
    h_ref[...] = work[...]
    finish(copies)
    send_terms(0, info, work, near_ref, away_ref, out_ref)


def mixed(level, r_ref, h_ref, mix_ref):
    step = 3**level
    count = HALF + 2 * HALO[level + 1]
    h = h_ref[step : step + count, :]
    for half in range(2):
        r = jnp.concatenate([r_ref[y, :, half * 128 : half * 128 + 128] for y in range(4)], axis=1)
        h += dot(r, mix_ref[half])[:count]
    return h


def middle_kernel(level, info, r_ref, h_ref, mix_hbm, got_hbm, sib_hbm, dil_hbm, got1_hbm, sib1_hbm, new_ref, out_ref, mix_ref, mix_sems, near_ref, away_ref, sems, work):
    first = mixing_copies(level, info, mix_hbm, got_hbm, sib_hbm, mix_ref, mix_sems)
    then = dilated_copies(level + 1, info, dil_hbm, got1_hbm, sib1_hbm, near_ref, away_ref, sems)
    start(first)
    start(then)
    finish(first)
    count = HALF + 2 * HALO[level + 1]
    if work.shape[0] > count:
        work[count:, :] = jnp.zeros((work.shape[0] - count, 256), F32)
    work[:count, :] = mixed(level, r_ref, h_ref, mix_ref)
    new_ref[...] = work[...]
    finish(then)
    send_terms(level + 1, info, work, near_ref, away_ref, out_ref)


def last_kernel(info, r_ref, h_ref, mix_hbm, got_hbm, sib_hbm, out_ref, mix_ref, mix_sems):
    copies = mixing_copies(3, info, mix_hbm, got_hbm, sib_hbm, mix_ref, mix_sems)
    start(copies)
    finish(copies)
    h = mixed(3, r_ref, h_ref, mix_ref).astype(BF)
    for peer in range(8):
        out_ref[peer] = h


def call(body, outs, scratch=(), smem=1, n=0, hbm=0, after=0, flops=10**9, name=None):
    def spec(space):
        return pl.BlockSpec(memory_space=space)

    specs = [spec(pltpu.SMEM)] * smem + [spec(pltpu.VMEM)] * n
    specs += [spec(pl.ANY)] * hbm + [spec(pltpu.VMEM)] * after
    return pl.pallas_call(
        body,
        out_shape=outs,
        in_specs=specs,
        out_specs=jax.tree.map(lambda _: spec(pltpu.VMEM), outs),
        scratch_shapes=list(scratch),
        compiler_params=params(),
        cost_estimate=cost(flops, 4 << 20),
        name=name,
    )


def shape(*dims, dtype=BF):
    return jax.ShapeDtypeStruct(dims, dtype)


BLOCKS = D // 128
UP_BLOCKS = 2 * BLOCKS
PART = UP_BLOCKS + 16
CHUNKS = ((0, 4), (4, 4), (8, 4), (12, 3))


def frames_kernel(pair, info, codes_ref, hf_ref, gain_ref, qkv_ref, full_ref, q_ref, kv_ref, weights, table, hf, rows, x, xn, sems, table_sems):
    def weight_copies(phase):
        return [
            pltpu.make_async_copy(
                full_ref.at[pl.ds(part * 4 ^ info[3], 4), pair, t ^ info[3], pl.ds(phase * BLOCKS, BLOCKS)],
                weights.at[phase, t, pl.ds(part * 4, 4)],
                sems.at[phase, part, t],
            )
            for part in range(2)
            for t in range(8)
        ]

    table_copies = [
        pltpu.make_async_copy(
            full_ref.at[:, part, :, pl.ds(UP_BLOCKS, 16)], table.at[:, part], table_sems.at[part]
        )
        for part in range(2)
    ]
    start(weight_copies(0))
    start(table_copies)
    start(weight_copies(1))
    for half in range(2):
        for j in range(8):
            at = 0 if j // 4 == half else 128
            hf[half * 128 : half * 128 + 128, j * 128 : j * 128 + 128] = hf_ref[
                half * 4 + j % 4, :, at : at + 128
            ]
    flat = table.reshape(VOCAB, 16, 128)
    for phase in range(2):
        finish(weight_copies(phase))
        for first, size in CHUNKS:
            w = [weights[phase, :, :, block].reshape(C, 128) for block in range(first, first + size)]
            x[:, first * 128 : (first + size) * 128] = dot(hf[...], jnp.concatenate(w, axis=1))
        if phase == 0:
            finish(table_copies)

        def look_up(i, carry):
            for j in range(8):
                row = i * 8 + j
                rows[row] = flat[codes_ref[(pair * 2 + phase) * 256 + row]].astype(F32)
            return carry

        lax.fori_loop(0, 32, look_up, 0)
        total = jnp.zeros((256, 128), F32)
        for block in range(BLOCKS):
            cols = slice(block * 128, block * 128 + 128)
            y = x[:, cols] + rows[:, block, :]
            x[:, cols] = y
            total += y
        mean = jnp.sum(total, axis=1, keepdims=True) * (1.0 / D)
        square = jnp.zeros((256, 128), F32)
        for block in range(BLOCKS):
            y = x[:, block * 128 : block * 128 + 128] - mean
            square += y * y
        factor = lax.rsqrt(jnp.sum(square, axis=1, keepdims=True) * (1.0 / D) + 1e-5)
        for block in range(BLOCKS):
            cols = slice(block * 128, block * 128 + 128)
            xn[:, cols] = ((x[:, cols] - mean) * factor * gain_ref[:, cols]).astype(BF)
        y = dot(xn[...], qkv_ref[...]).astype(BF)
        lines = slice(phase * 256, phase * 256 + 256)
        for head in range(2):
            at = head * 384
            cols = slice(head * 128, head * 128 + 128)
            q_ref[lines, cols] = y[:, at : at + 128]
            kv_ref[lines, cols] = y[:, at + 128 : at + 256]
            kv_ref[lines, 256 + head * 128 : 384 + head * 128] = y[:, at + 256 : at + 384]


def frames(pair, info, codes, hf, gain, qkv, full):
    vm = pl.BlockSpec(memory_space=pltpu.VMEM)
    sm = pl.BlockSpec(memory_space=pltpu.SMEM)
    return pl.pallas_call(
        functools.partial(frames_kernel, pair),
        out_shape=(shape(512, 256), shape(512, 512)),
        in_specs=[sm, sm, vm, vm, vm, pl.BlockSpec(memory_space=pltpu.HBM)],
        out_specs=(vm, vm),
        scratch_shapes=[
            pltpu.VMEM((2, 8, 8, BLOCKS, 16, 128), BF),
            pltpu.VMEM((8, 2, 8, 16, 16, 128), BF),
            pltpu.VMEM((256, C), BF),
            pltpu.VMEM((256, 16, 128), F32),
            pltpu.VMEM((256, D), F32),
            pltpu.VMEM((256, D), BF),
            pltpu.SemaphoreType.DMA((2, 2, 8)),
            pltpu.SemaphoreType.DMA((2,)),
        ],
        compiler_params=params(),
        cost_estimate=cost(4 * 10**9, 20 << 20),
        name="frames",
    )(info, codes, hf, gain, qkv, full)


SCALE = 128**-0.5 * 1.4426950408889634


def scores_of(q, k):
    return lax.dot_general(q, k, (((1,), (1,)), ((), ())), preferred_element_type=F32)


def fold(q_refs, kv_refs, seen_of, old_of, put):
    kv = jnp.concatenate([ref[...] for ref in kv_refs], axis=0)
    ones = jnp.ones((kv.shape[0], 128), BF)
    for head in range(2):
        k = kv[:, head * 128 : head * 128 + 128]
        v = jnp.concatenate([kv[:, 256 + head * 128 : 384 + head * 128], ones], axis=1)
        for phase in range(4):
            lines = slice(phase % 2 * 256, phase % 2 * 256 + 256)
            s = scores_of(q_refs[phase // 2][lines, head * 128 : head * 128 + 128], k)
            s = jnp.where(seen_of(phase), s, -1e30)
            top = jnp.max(s, axis=1, keepdims=True)
            old = old_of(head, phase)
            if old is None:
                put(head, phase, top, dot(jnp.exp2((s - top) * SCALE).astype(BF), v))
            else:
                top = jnp.maximum(old[0], top)
                p = jnp.exp2((s - top) * SCALE).astype(BF)
                put(head, phase, top, old[1] * jnp.exp2((old[0] - top) * SCALE) + dot(p, v))


def at_tile(head, phase):
    lines = slice(phase * 256, phase * 256 + 256)
    return (lines, slice(head, head + 1)), (lines, slice(head * 256, head * 256 + 256))


def own_kernel(q0_ref, q1_ref, kv0_ref, kv1_ref, acc_ref, top_ref):
    col = lax.broadcasted_iota(jnp.int32, (256, 1024), 1)
    ahead = (col & 255) * 4 + (col >> 8) - 4 * lax.broadcasted_iota(jnp.int32, (256, 1024), 0)

    def put(head, phase, top, acc):
        one, both = at_tile(head, phase)
        top_ref[one] = top
        acc_ref[both] = acc

    fold((q0_ref, q1_ref), (kv0_ref, kv1_ref), lambda p: ahead <= p, lambda head, phase: None, put)


def past_kernel(last, info, q0_ref, q1_ref, far_ref, near_ref, acc_ref, top_ref, *refs):
    if last:
        out_ref, acc, tops, wide = refs
    else:
        acc, tops = refs
    song = info[2]

    @pl.when(song == 0)
    def _():
        acc[...] = acc_ref[...]
        tops[...] = top_ref[...]

    @pl.when(song > 0)
    def _():
        col = lax.broadcasted_iota(jnp.int32, (256, 1024), 1)
        seen = col >= jnp.where(song == 1, 512, 0)

        def old_of(head, phase):
            one, both = at_tile(head, phase)
            return top_ref[one], acc_ref[both]

        def put(head, phase, top, total):
            one, both = at_tile(head, phase)
            tops[one] = top
            acc[both] = total

        fold((q0_ref, q1_ref), (far_ref, near_ref), lambda p: seen, old_of, put)

    if last:
        for head in range(2):
            for phase in range(4):
                both = acc[at_tile(head, phase)[1]]
                wide[pl.ds(phase, 256, stride=4), :] = both[:, :128] / both[:, 128:]
            out_ref[:, head * 128 : head * 128 + 128] = wide[...].astype(BF)


EVERY = ("song", "tensor")


def other_half():
    pairs = []
    for song in range(16):
        for rank in range(8):
            pairs.append((song * 8 + rank, (song ^ 8) * 8 + (rank ^ 4)))
    return pairs


def to_sibling(value):
    return lax.ppermute(value, "song", [(i, i ^ 1) for i in range(16)])


def exchange(value, axis="tensor", groups=None):
    return lax.all_to_all(value, axis, 0, 0, axis_index_groups=groups, tiled=True)


def on_device(
    upper_codes,
    middle_codes,
    upper_table,
    dilated_weight,
    mixing_weight,
    upsample_weight,
    middle_table,
    norm_gain,
    qkv_weight,
):
    song = lax.axis_index("song")
    rank = lax.axis_index("tensor")
    core = song % 2
    x_hi = rank // 4
    begin = song * 256 + x_hi * HALF
    info = jnp.stack([core, begin, song, x_hi * 4]).astype(jnp.int32)

    after = lax.ppermute(upper_codes[-40:], "song", [(i, i + 1) for i in range(15)])
    before = lax.ppermute(upper_codes[:40], "song", [(i + 1, i) for i in range(15)])
    codes = jnp.concatenate([after, upper_codes, before])
    codes = lax.dynamic_slice_in_dim(codes, x_hi * HALF, HALF + 80)[:, None]

    dil_half = lax.dynamic_slice_in_dim(dilated_weight, core * 512, 512, 3)
    mix_half = lax.dynamic_slice_in_dim(mixing_weight, core * 512, 512, 1)
    mix_pack = jnp.concatenate([mix_half[:, i * 128 : i * 128 + 128] for i in range(4)], axis=2)
    tab_half = lax.dynamic_slice_in_dim(upper_table, core * 1024, 1024, 0)
    tab_pack = jnp.concatenate([tab_half[i * 256 : i * 256 + 256] for i in range(4)], axis=1)
    pack0 = jnp.concatenate([dil_half[0].reshape(384, 512), mix_pack[0], tab_pack], axis=0)
    pack1 = jnp.concatenate([dil_half[1].reshape(384, 512), mix_pack[1]], axis=0)
    pack2 = jnp.concatenate([dil_half[2:].reshape(2, 384, 512), mix_pack[2:]], axis=1)
    got0 = lax.ppermute(pack0, EVERY, other_half())

    share = song ^ (8 * x_hi)
    up_part = lax.dynamic_slice(upsample_weight, (share // 2 * 16, core * 2 * D), (16, 2 * D))
    mid_part = lax.dynamic_slice_in_dim(middle_table, share * 16, 16, 0)
    up_part = up_part.reshape(16, UP_BLOCKS, 128).transpose(1, 0, 2)
    mid_part = jnp.pad(mid_part.reshape(16, BLOCKS, 128), ((0, 0), (0, 1), (0, 0)))
    part = jnp.concatenate([up_part, mid_part])
    part, pack0 = lax.optimization_barrier((part, pack0))
    mine = exchange(jnp.broadcast_to(part[None], (4, PART, 16, 128)), groups=Y_GROUPS)
    mine, got0 = lax.optimization_barrier((mine, got0))
    sib0 = to_sibling(got0)
    others = lax.ppermute(mine, EVERY, other_half())

    h, terms = call(
        first_kernel,
        (shape(ROWS[0], 256, dtype=F32), shape(4, ROWS[1], 256)),
        [*DILATED, pltpu.VMEM((ROWS[0], 256), F32)],
        n=2,
        hbm=1,
        after=2,
        name="cond0",
    )(info, codes, upper_table, dilated_weight, got0, sib0)
    for level in range(4):
        terms = exchange(terms, groups=Y_GROUPS)
        if level == 0:
            others, pack1, terms = lax.optimization_barrier((others, pack1, terms))
            full = lax.all_gather(jnp.concatenate([mine, others]), "song", axis=0, tiled=False)
            full = full.reshape(8, 2, 8, PART, 16, 128)
            got1 = lax.ppermute(pack1, EVERY, other_half())
        total = terms[0].astype(F32)
        for y in range(1, 4):
            total = total + terms[y].astype(F32)
        r = jnp.maximum(total, 0.0).astype(BF)
        r = exchange(jnp.broadcast_to(r[None], terms.shape), groups=Y_GROUPS)
        if level == 0:
            got1, pack2, r = lax.optimization_barrier((got1, pack2, r))
            sib1 = to_sibling(got1)
            got2 = lax.ppermute(pack2, EVERY, other_half())
            stacks = [(got0, sib0), (got1, sib1)]
        if level == 1:
            got2, r = lax.optimization_barrier((got2, r))
            stacks += [(got2, to_sibling(got2))] * 2
        if level < 3:
            h, terms = call(
                functools.partial(middle_kernel, level),
                (shape(ROWS[level + 1], 256, dtype=F32), shape(4, ROWS[level + 2], 256)),
                [*MIXING, *DILATED, pltpu.VMEM((ROWS[level + 1], 256), F32)],
                n=2,
                hbm=6,
                name="cond",
            )(info, r, h, mixing_weight, *stacks[level], dilated_weight, *stacks[level + 1])
        else:
            spread = call(
                last_kernel, shape(8, HALF, 256), MIXING, n=2, hbm=3, name="cond_end"
            )(info, r, h, mixing_weight, *stacks[level])
    hf = exchange(spread)

    mid = middle_codes.reshape(256, 4).T.reshape(1024)
    mid = ((mid % 256) // 16 * 128 + mid // 256 * 16 + mid % 16) ^ (x_hi * (8 * 128 + 4 * 16))
    gain = norm_gain[None]
    qkv = qkv_weight.reshape(D, 768)

    def from_two_back(value):
        return lax.ppermute(value, "song", [(i, i + 2) for i in range(14)])

    q0, kv0 = frames(0, info, mid, hf, gain, qkv, full)
    far0 = from_two_back(kv0)
    q1, kv1 = frames(1, info, mid, hf, gain, qkv, full)
    far1 = from_two_back(kv1)
    state = (shape(1024, 512, dtype=F32), shape(1024, 2, dtype=F32))
    kept = call(own_kernel, state, smem=0, n=4, flops=10**9, name="own")(q0, q1, kv0, kv1)
    near0 = to_sibling(jnp.where(core == 0, kv0, far0))
    far1, kept = lax.optimization_barrier((far1, kept))
    kept = call(functools.partial(past_kernel, False), state, n=6, flops=2 * 10**9, name="past")(
        info, q0, q1, far0, near0, *kept
    )
    near1 = to_sibling(jnp.where(core == 0, kv1, far1))
    return call(
        functools.partial(past_kernel, True),
        shape(1024, 256),
        [pltpu.VMEM((1024, 512), F32), pltpu.VMEM((1024, 2), F32), pltpu.VMEM((1024, 128), F32)],
        n=6,
        flops=2 * 10**9,
        name="past_end",
    )(info, q0, q1, far1, near1, *kept)


def solution(mesh):
    placed = (
        P("song"),
        P("song"),
        P(None, "tensor"),
        P(None, None, "tensor", None),
        P(None, None, "tensor"),
        P("tensor", None),
        P("tensor", None),
        P(),
        P(None, "tensor", None),
    )
    return jax.shard_map(
        on_device, mesh=mesh, in_specs=placed, out_specs=P("song", "tensor"), check_vma=False
    )
```

```python
import functools

import jax
import jax.numpy as jnp
from jax import lax
from jax.experimental import pallas as pl
from jax.experimental.pallas import tpu as pltpu
from jax.sharding import PartitionSpec as P

BF = jnp.bfloat16
F32 = jnp.float32
D = 1920
C = 1024
VOCAB = 2048
UPPER = 4096
HALF = 128
HALO = (40, 39, 36, 27, 0)
ROWS = (208, 208, 208, 192, 128)
VMEM_LIMIT = 60 << 20

BLOCKS = D // 128
UP_BLOCKS = 2 * BLOCKS
PART = UP_BLOCKS + 16

Y_GROUPS = [[0, 1, 2, 3], [4, 5, 6, 7]]


def params(**kw):
    return pltpu.CompilerParams(vmem_limit_bytes=VMEM_LIMIT, **kw)


def cost(flops, nbytes, trans=0):
    return pl.CostEstimate(flops=flops, bytes_accessed=nbytes, transcendentals=trans)


def dot(a, b):
    return jnp.dot(a, b, preferred_element_type=F32)


def dilated_copies(level, info, dil_hbm, got_hbm, sib_hbm, near_ref, away_ref, sems):
    own = pl.multiple_of(info[0] * 512, 512)
    other = pl.multiple_of((1 - info[0]) * 512, 512)
    pairs = []
    for ref, hbm, begin in ((near_ref, got_hbm, own), (away_ref, sib_hbm, other)):
        part = hbm if level < 2 else hbm.at[level - 2]
        pairs.append((dil_hbm.at[level, :, :, pl.ds(begin, 512)], ref.at[:, pl.ds(0, 128), :]))
        for tap in range(3):
            pairs.append((part.at[pl.ds(tap * 128, 128), :], ref.at[tap, pl.ds(128, 128), :]))
    return [pltpu.make_async_copy(a, b, sems.at[i]) for i, (a, b) in enumerate(pairs)]


def mixing_copies(level, info, mix_hbm, got_hbm, sib_hbm, mix_ref, sems):
    pairs = []
    for half, hbm in enumerate((got_hbm, sib_hbm)):
        part = hbm if level < 2 else hbm.at[level - 2]
        begin = info[0] if half == 0 else 1 - info[0]
        rows = pl.ds(pl.multiple_of(begin * 512, 512), 512)
        pairs.append((mix_hbm.at[level, rows, :], mix_ref.at[half, :, pl.ds(0, 128)]))
        for y in range(4):
            pairs.append(
                (
                    part.at[pl.ds(384, 128), pl.ds(y * 128, 128)],
                    mix_ref.at[half, pl.ds(y * 128, 128), pl.ds(128, 128)],
                )
            )
    return [pltpu.make_async_copy(a, b, sems.at[i]) for i, (a, b) in enumerate(pairs)]


def send_terms(level, info, h_ref, near_ref, away_ref, out_ref):
    step = 3**level
    count = HALF + 2 * HALO[level + 1]
    padded = out_ref.shape[1]
    rows = h_ref.shape[0]
    first = info[1] - HALO[level]
    pos = first + lax.broadcasted_iota(jnp.int32, (rows, 1), 0)
    inside = (pos >= 0) & (pos < UPPER)
    h_ref[...] = jnp.where(inside, jnp.maximum(h_ref[...], 0.0), 0.0)
    taps = [h_ref[tap * step : tap * step + count, :].astype(BF) for tap in range(3)]
    for half, ref in enumerate((near_ref, away_ref)):
        total = dot(taps[0], ref[0]) + dot(taps[1], ref[1]) + dot(taps[2], ref[2])
        total = total.astype(BF)
        for y in range(4):
            out_ref[y, :count, half * 128 : half * 128 + 128] = total[:, y * 128 : y * 128 + 128]
    if padded > count:
        for y in range(4):
            out_ref[y, count:, :] = jnp.zeros((padded - count, 256), BF)


def start(copies):
    for copy in copies:
        copy.start()


def finish(copies):
    for copy in copies:
        copy.wait()


DILATED = [pltpu.VMEM((3, 256, 512), BF), pltpu.VMEM((3, 256, 512), BF), pltpu.SemaphoreType.DMA((8,))]
MIXING = [pltpu.VMEM((2, 512, 256), BF), pltpu.SemaphoreType.DMA((10,))]


def first_kernel(info, codes_ref, table_ref, dil_hbm, got_ref, sib_ref, h_ref, out_ref, near_ref, away_ref, sems, work):
    copies = dilated_copies(0, info, dil_hbm, got_ref, sib_ref, near_ref, away_ref, sems)
    start(copies)
    codes = codes_ref[...]
    rows = codes.shape[0]
    lane = lax.broadcasted_iota(jnp.int32, (rows, 1024), 1)
    core = info[0]
    one = jnp.ones((), BF)
    zero = jnp.zeros((), BF)
    h_own = jnp.zeros((rows, 128), F32)
    h_oth = jnp.zeros((rows, 128), F32)
    for src, begin in ((got_ref, core * 1024), (sib_ref, (1 - core) * 1024)):
        hot = jnp.where(codes - begin == lane, one, zero)
        h_own += dot(hot, table_ref[pl.ds(pl.multiple_of(begin, 1024), 1024), :])
        for q in range(4):
            h_oth += dot(hot[:, q * 256 : q * 256 + 256], src[512:768, q * 128 : q * 128 + 128])
    work[:, :128] = h_own
    work[:, 128:] = h_oth
    h_ref[...] = work[...]
    finish(copies)
    send_terms(0, info, work, near_ref, away_ref, out_ref)


def mixed(level, r_ref, h_ref, mix_ref):
    step = 3**level
    count = HALF + 2 * HALO[level + 1]
    h = h_ref[step : step + count, :]
    for half in range(2):
        r = jnp.concatenate([r_ref[y, :, half * 128 : half * 128 + 128] for y in range(4)], axis=1)
        h += dot(r, mix_ref[half])[:count]
    return h


def middle_kernel(level, info, r_ref, h_ref, mix_hbm, got_hbm, sib_hbm, dil_hbm, got1_hbm, sib1_hbm, new_ref, out_ref, mix_ref, mix_sems, near_ref, away_ref, sems, work):
    first = mixing_copies(level, info, mix_hbm, got_hbm, sib_hbm, mix_ref, mix_sems)
    then = dilated_copies(level + 1, info, dil_hbm, got1_hbm, sib1_hbm, near_ref, away_ref, sems)
    start(first)
    start(then)
    finish(first)
    count = HALF + 2 * HALO[level + 1]
    if work.shape[0] > count:
        work[count:, :] = jnp.zeros((work.shape[0] - count, 256), F32)
    work[:count, :] = mixed(level, r_ref, h_ref, mix_ref)
    new_ref[...] = work[...]
    finish(then)
    send_terms(level + 1, info, work, near_ref, away_ref, out_ref)


def last_kernel(info, r_ref, h_ref, mix_hbm, got_hbm, sib_hbm, out_ref, mix_ref, mix_sems):
    copies = mixing_copies(3, info, mix_hbm, got_hbm, sib_hbm, mix_ref, mix_sems)
    start(copies)
    finish(copies)
    h = mixed(3, r_ref, h_ref, mix_ref).astype(BF)
    for peer in range(8):
        out_ref[peer] = h


def pack_kernel(info, dil_hbm, mix_hbm, tab_hbm, up_hbm, mid_hbm, pack0, pack1, pack2, part_ref, up, mid, wide, sems):
    cols = pl.ds(pl.multiple_of(info[0] * 512, 512), 512)
    pairs = [
        (up_hbm.at[pl.ds(info[4] * 16, 16), pl.ds(pl.multiple_of(info[0] * 2 * D, 128), 2 * D)], up),
        (mid_hbm.at[pl.ds(info[5] * 16, 16), :], mid),
    ]
    for level in range(4):
        dest = (pack0, pack1, pack2.at[0], pack2.at[1])[level]
        for tap in range(3):
            pairs.append((dil_hbm.at[level, tap, :, cols], dest.at[pl.ds(tap * 128, 128), :]))
        for i in range(4):
            rows = pl.ds(pl.multiple_of(info[0] * 512 + i * 128, 128), 128)
            pairs.append((mix_hbm.at[level, rows, :], dest.at[pl.ds(384, 128), pl.ds(i * 128, 128)]))
    for i in range(4):
        rows = pl.ds(pl.multiple_of(info[0] * 1024 + i * 256, 256), 256)
        pairs.append((tab_hbm.at[rows, :], pack0.at[pl.ds(512, 256), pl.ds(i * 128, 128)]))
    copies = [pltpu.make_async_copy(a, b, sems.at[i]) for i, (a, b) in enumerate(pairs)]
    start(copies)
    finish(copies[:2])
    wide[...] = jnp.zeros_like(wide)
    for block in range(BLOCKS):
        wide[:, block, :] = mid[:, block * 128 : block * 128 + 128].astype(F32)
    for y in range(4):
        for block in range(UP_BLOCKS):
            part_ref[y, block] = up[:, block * 128 : block * 128 + 128]
        part_ref[y, UP_BLOCKS:] = wide[...].astype(BF)
    finish(copies[2:])


def join_kernel(mine, others, out, sems):
    copies = [
        pltpu.make_async_copy(ref, out.at[pl.ds(i * 4, 4)], sems.at[i]) for i, ref in enumerate((mine, others))
    ]
    start(copies)
    finish(copies)


def join(mine, others):
    space = pl.BlockSpec(memory_space=pl.ANY)
    return pl.pallas_call(
        join_kernel,
        out_shape=shape(8, PART, 16, 128),
        in_specs=[space, space],
        out_specs=space,
        scratch_shapes=[pltpu.SemaphoreType.DMA((2,))],
        compiler_params=params(),
        cost_estimate=cost(0, 3 << 20),
        name="join",
    )(mine, others)


def call(body, outs, scratch=(), smem=1, n=0, hbm=0, after=0, flops=10**9, name=None):
    def spec(space):
        return pl.BlockSpec(memory_space=space)

    specs = [spec(pltpu.SMEM)] * smem + [spec(pltpu.VMEM)] * n
    specs += [spec(pl.ANY)] * hbm + [spec(pltpu.VMEM)] * after
    return pl.pallas_call(
        body,
        out_shape=outs,
        in_specs=specs,
        out_specs=jax.tree.map(lambda _: spec(pltpu.VMEM), outs),
        scratch_shapes=list(scratch),
        compiler_params=params(),
        cost_estimate=cost(flops, 4 << 20),
        name=name,
    )


def shape(*dims, dtype=BF):
    return jax.ShapeDtypeStruct(dims, dtype)


CHUNKS = ((0, 4), (4, 4), (8, 4), (12, 3))


def frames_kernel(pair, info, codes_ref, hf_ref, gain_ref, qkv_hbm, full_ref, q_ref, kv_ref, weights, table, qkv, hf, rows, x, xn, sems, table_sems, qkv_sem):
    def weight_copies(phase):
        return [
            pltpu.make_async_copy(
                full_ref.at[pl.ds(part * 4 ^ info[3], 4), pair, t ^ info[3], pl.ds(phase * BLOCKS, BLOCKS)],
                weights.at[phase, t, pl.ds(part * 4, 4)],
                sems.at[phase, part, t],
            )
            for part in range(2)
            for t in range(8)
        ]

    def product(phase):
        for first, size in CHUNKS:
            w = [weights[phase, :, :, block].reshape(C, 128) for block in range(first, first + size)]
            x[phase, :, first * 128 : (first + size) * 128] = dot(hf[...], jnp.concatenate(w, axis=1))

    def norm(phase):
        total = jnp.zeros((256, 128), F32)
        for block in range(BLOCKS):
            cols = slice(block * 128, block * 128 + 128)
            y = x[phase, :, cols] + rows[pl.ds(phase * 256, 256), block, :]
            x[phase, :, cols] = y
            total += y
        mean = jnp.sum(total, axis=1, keepdims=True) * (1.0 / D)
        square = jnp.zeros((256, 128), F32)
        for block in range(BLOCKS):
            y = x[phase, :, block * 128 : block * 128 + 128] - mean
            square += y * y
        factor = lax.rsqrt(jnp.sum(square, axis=1, keepdims=True) * (1.0 / D) + 1e-5)
        for block in range(BLOCKS):
            cols = slice(block * 128, block * 128 + 128)
            xn[phase, :, cols] = ((x[phase, :, cols] - mean) * factor * gain_ref[:, cols]).astype(BF)

    def project(phase):
        y = dot(xn[phase], qkv[...]).astype(BF)
        lines = slice(phase * 256, phase * 256 + 256)
        for head in range(2):
            at = head * 384
            cols = slice(head * 128, head * 128 + 128)
            q_ref[lines, cols] = y[:, at : at + 128]
            kv_ref[lines, cols] = y[:, at + 128 : at + 256]
            kv_ref[lines, 256 + head * 128 : 384 + head * 128] = y[:, at + 256 : at + 384]

    table_copies = [
        pltpu.make_async_copy(
            full_ref.at[:, part, :, pl.ds(UP_BLOCKS, 16)], table.at[:, part], table_sems.at[part]
        )
        for part in range(2)
    ]
    qkv_copy = pltpu.make_async_copy(qkv_hbm, qkv, qkv_sem)
    start(table_copies)
    start(weight_copies(0))
    start(weight_copies(1))
    qkv_copy.start()
    for half in range(2):
        for j in range(8):
            at = 0 if j // 4 == half else 128
            hf[half * 128 : half * 128 + 128, j * 128 : j * 128 + 128] = hf_ref[
                half * 4 + j % 4, :, at : at + 128
            ]
    flat = table.reshape(VOCAB, 16, 128)
    finish(table_copies)

    def look_up(i, carry):
        for j in range(8):
            row = i * 8 + j
            rows[row] = flat[codes_ref[pair * 512 + row]].astype(F32)
        return carry

    lax.fori_loop(0, 64, look_up, 0)
    finish(weight_copies(0))
    product(0)
    finish(weight_copies(1))
    qkv_copy.wait()
    norm(0)
    product(1)
    project(0)
    norm(1)
    project(1)


def frames(pair, info, codes, hf, gain, qkv, full):
    vm = pl.BlockSpec(memory_space=pltpu.VMEM)
    sm = pl.BlockSpec(memory_space=pltpu.SMEM)
    return pl.pallas_call(
        functools.partial(frames_kernel, pair),
        out_shape=(shape(512, 256), shape(512, 512)),
        in_specs=[sm, sm, vm, vm, pl.BlockSpec(memory_space=pl.ANY), pl.BlockSpec(memory_space=pltpu.HBM)],
        out_specs=(vm, vm),
        scratch_shapes=[
            pltpu.VMEM((2, 8, 8, BLOCKS, 16, 128), BF),
            pltpu.VMEM((8, 2, 8, 16, 16, 128), BF),
            pltpu.VMEM((D, 768), BF),
            pltpu.VMEM((256, C), BF),
            pltpu.VMEM((512, 16, 128), F32),
            pltpu.VMEM((2, 256, D), F32),
            pltpu.VMEM((2, 256, D), BF),
            pltpu.SemaphoreType.DMA((2, 2, 8)),
            pltpu.SemaphoreType.DMA((2,)),
            pltpu.SemaphoreType.DMA,
        ],
        compiler_params=params(),
        cost_estimate=cost(4 * 10**9, 20 << 20),
        name="frames",
    )(info, codes, hf, gain, qkv, full)


SCALE = 128**-0.5 * 1.4426950408889634


def scores_of(q, k):
    return lax.dot_general(q, k, (((1,), (1,)), ((), ())), preferred_element_type=F32)


def fold(q_refs, kv_refs, seen_of, old_of, put):
    kv = jnp.concatenate([ref[...] for ref in kv_refs], axis=0)
    ones = jnp.ones((kv.shape[0], 128), BF)
    for head in range(2):
        k = kv[:, head * 128 : head * 128 + 128]
        v = jnp.concatenate([kv[:, 256 + head * 128 : 384 + head * 128], ones], axis=1)
        for phase in range(4):
            lines = slice(phase % 2 * 256, phase % 2 * 256 + 256)
            s = scores_of(q_refs[phase // 2][lines, head * 128 : head * 128 + 128], k)
            s = jnp.where(seen_of(phase), s, -1e30)
            top = jnp.max(s, axis=1, keepdims=True)
            old = old_of(head, phase)
            if old is None:
                put(head, phase, top, dot(jnp.exp2((s - top) * SCALE).astype(BF), v))
            else:
                top = jnp.maximum(old[0], top)
                p = jnp.exp2((s - top) * SCALE).astype(BF)
                put(head, phase, top, old[1] * jnp.exp2((old[0] - top) * SCALE) + dot(p, v))


def at_tile(head, phase):
    lines = slice(phase * 256, phase * 256 + 256)
    return (lines, slice(head, head + 1)), (lines, slice(head * 256, head * 256 + 256))


def own_kernel(q0_ref, q1_ref, kv0_ref, kv1_ref, acc_ref, top_ref):
    col = lax.broadcasted_iota(jnp.int32, (256, 1024), 1)
    ahead = (col & 255) * 4 + (col >> 8) - 4 * lax.broadcasted_iota(jnp.int32, (256, 1024), 0)

    def put(head, phase, top, acc):
        one, both = at_tile(head, phase)
        top_ref[one] = top
        acc_ref[both] = acc

    fold((q0_ref, q1_ref), (kv0_ref, kv1_ref), lambda p: ahead <= p, lambda head, phase: None, put)


def past_kernel(last, info, q0_ref, q1_ref, far_ref, near_ref, acc_ref, top_ref, *refs):
    if last:
        out_ref, acc, tops, wide = refs
    else:
        acc, tops = refs
    song = info[2]

    @pl.when(song == 0)
    def _():
        acc[...] = acc_ref[...]
        tops[...] = top_ref[...]

    @pl.when(song > 0)
    def _():
        col = lax.broadcasted_iota(jnp.int32, (256, 1024), 1)
        seen = col >= jnp.where(song == 1, 512, 0)

        def old_of(head, phase):
            one, both = at_tile(head, phase)
            return top_ref[one], acc_ref[both]

        def put(head, phase, top, total):
            one, both = at_tile(head, phase)
            tops[one] = top
            acc[both] = total

        fold((q0_ref, q1_ref), (far_ref, near_ref), lambda p: seen, old_of, put)

    if last:
        for head in range(2):
            for phase in range(4):
                both = acc[at_tile(head, phase)[1]]
                wide[pl.ds(phase, 256, stride=4), :] = both[:, :128] / both[:, 128:]
            out_ref[:, head * 128 : head * 128 + 128] = wide[...].astype(BF)


EVERY = ("song", "tensor")


def other_half():
    pairs = []
    for song in range(16):
        for rank in range(8):
            pairs.append((song * 8 + rank, (song ^ 8) * 8 + (rank ^ 4)))
    return pairs


def song_neighbours():
    first = [(song * 8 + rank, song * 8 + 8 + rank) for song in range(15) for rank in range(4)]
    second = [(song * 8 + 8 + rank, song * 8 + rank) for song in range(15) for rank in range(4, 8)]
    return first + second


def to_sibling(value):
    return lax.ppermute(value, "song", [(i, i ^ 1) for i in range(16)])


def exchange(value, axis="tensor", groups=None):
    return lax.all_to_all(value, axis, 0, 0, axis_index_groups=groups, tiled=True)


def on_device(
    upper_codes,
    middle_codes,
    upper_table,
    dilated_weight,
    mixing_weight,
    upsample_weight,
    middle_table,
    norm_gain,
    qkv_weight,
):
    song = lax.axis_index("song")
    rank = lax.axis_index("tensor")
    core = song % 2
    x_hi = rank // 4
    begin = song * 256 + x_hi * HALF
    share = song ^ (8 * x_hi)
    info = jnp.stack([core, begin, song, x_hi * 4, share // 2, share]).astype(jnp.int32)

    pack0, pack1, pack2, part = call(
        pack_kernel,
        (shape(768, 512), shape(512, 512), shape(2, 512, 512), shape(4, PART, 16, 128)),
        [
            pltpu.VMEM((16, 2 * D), BF),
            pltpu.VMEM((16, D), BF),
            pltpu.VMEM((16, 16, 128), F32),
            pltpu.SemaphoreType.DMA((34,)),
        ],
        hbm=5,
        name="pack",
    )(info, dilated_weight, mixing_weight, upper_table, upsample_weight, middle_table)
    got0 = lax.ppermute(pack0, EVERY, other_half())
    mine = exchange(part, groups=Y_GROUPS)
    mine, got0 = lax.optimization_barrier((mine, got0))
    sib0 = to_sibling(got0)
    others = lax.ppermute(mine, EVERY, other_half())

    edge = jnp.where(x_hi == 0, upper_codes[-40:], upper_codes[:40])
    edge = lax.ppermute(edge, EVERY, song_neighbours())
    codes = jnp.where(
        x_hi == 0,
        jnp.concatenate([edge, upper_codes[: HALF + 40]]),
        jnp.concatenate([upper_codes[HALF - 40 :], edge]),
    )[:, None]

    h, terms = call(
        first_kernel,
        (shape(ROWS[0], 256, dtype=F32), shape(4, ROWS[1], 256)),
        [*DILATED, pltpu.VMEM((ROWS[0], 256), F32)],
        n=2,
        hbm=1,
        after=2,
        name="cond0",
    )(info, codes, upper_table, dilated_weight, got0, sib0)
    others, pack1, terms = lax.optimization_barrier((others, pack1, terms))
    full = lax.all_gather(join(mine, others), "song", axis=0, tiled=False)
    full = full.reshape(8, 2, 8, PART, 16, 128)
    got1 = lax.ppermute(pack1, EVERY, other_half())
    for level in range(4):
        terms = exchange(terms, groups=Y_GROUPS)
        total = terms[0].astype(F32)
        for y in range(1, 4):
            total = total + terms[y].astype(F32)
        r = jnp.maximum(total, 0.0).astype(BF)
        r = exchange(jnp.broadcast_to(r[None], terms.shape), groups=Y_GROUPS)
        if level == 0:
            got1, pack2, r = lax.optimization_barrier((got1, pack2, r))
            sib1 = to_sibling(got1)
            got2 = lax.ppermute(pack2, EVERY, other_half())
            stacks = [(got0, sib0), (got1, sib1)]
        if level == 1:
            got2, r = lax.optimization_barrier((got2, r))
            stacks += [(got2, to_sibling(got2))] * 2
        if level < 3:
            h, terms = call(
                functools.partial(middle_kernel, level),
                (shape(ROWS[level + 1], 256, dtype=F32), shape(4, ROWS[level + 2], 256)),
                [*MIXING, *DILATED, pltpu.VMEM((ROWS[level + 1], 256), F32)],
                n=2,
                hbm=6,
                name="cond",
            )(info, r, h, mixing_weight, *stacks[level], dilated_weight, *stacks[level + 1])
        else:
            spread = call(
                last_kernel, shape(8, HALF, 256), MIXING, n=2, hbm=3, name="cond_end"
            )(info, r, h, mixing_weight, *stacks[level])
    hf = exchange(spread)

    mid = middle_codes.reshape(256, 4).T.reshape(1024)
    mid = ((mid % 256) // 16 * 128 + mid // 256 * 16 + mid % 16) ^ (x_hi * (8 * 128 + 4 * 16))
    gain = norm_gain[None]
    qkv = qkv_weight.reshape(D, 768)

    def from_two_back(value):
        return lax.ppermute(value, "song", [(i, i + 2) for i in range(14)])

    q0, kv0 = frames(0, info, mid, hf, gain, qkv, full)
    far0 = from_two_back(kv0)
    q1, kv1 = frames(1, info, mid, hf, gain, qkv, full)
    far1 = from_two_back(kv1)
    state = (shape(1024, 512, dtype=F32), shape(1024, 2, dtype=F32))
    kept = call(own_kernel, state, smem=0, n=4, flops=10**9, name="own")(q0, q1, kv0, kv1)
    near0 = to_sibling(jnp.where(core == 0, kv0, far0))
    kept = call(functools.partial(past_kernel, False), state, n=6, flops=2 * 10**9, name="past")(
        info, q0, q1, far0, near0, *kept
    )
    far1, kept = lax.optimization_barrier((far1, kept))
    near1 = to_sibling(jnp.where(core == 0, kv1, far1))
    return call(
        functools.partial(past_kernel, True),
        shape(1024, 256),
        [pltpu.VMEM((1024, 512), F32), pltpu.VMEM((1024, 2), F32), pltpu.VMEM((1024, 128), F32)],
        n=6,
        flops=2 * 10**9,
        name="past_end",
    )(info, q0, q1, far1, near1, *kept)


def solution(mesh):
    placed = (
        P("song"),
        P("song"),
        P(None, "tensor"),
        P(None, None, "tensor", None),
        P(None, None, "tensor"),
        P("tensor", None),
        P("tensor", None),
        P(),
        P(None, "tensor", None),
    )
    return jax.shard_map(
        on_device, mesh=mesh, in_specs=placed, out_specs=P("song", "tensor"), check_vma=False
    )
```

```python
import functools

import jax
import jax.numpy as jnp
from jax import lax
from jax.experimental import pallas as pl
from jax.experimental.pallas import tpu as pltpu
from jax.sharding import PartitionSpec as P

BF = jnp.bfloat16
F32 = jnp.float32
D = 1920
C = 1024
VOCAB = 2048
UPPER = 4096
HALF = 128
HALO = (40, 39, 36, 27, 0)
ROWS = (208, 208, 208, 192, 128)
VMEM_LIMIT = 60 << 20

BLOCKS = D // 128
UP_BLOCKS = 2 * BLOCKS
PART = UP_BLOCKS + 16

Y_GROUPS = [[0, 1, 2, 3], [4, 5, 6, 7]]


def params(**kw):
    return pltpu.CompilerParams(vmem_limit_bytes=VMEM_LIMIT, **kw)


def cost(flops, nbytes, trans=0):
    return pl.CostEstimate(flops=flops, bytes_accessed=nbytes, transcendentals=trans)


def dot(a, b):
    return jnp.dot(a, b, preferred_element_type=F32)


def dilated_copies(level, info, dil_hbm, got_hbm, sib_hbm, near_ref, away_ref, sems):
    own = pl.multiple_of(info[0] * 512, 512)
    other = pl.multiple_of((1 - info[0]) * 512, 512)
    pairs = []
    for ref, hbm, begin in ((near_ref, got_hbm, own), (away_ref, sib_hbm, other)):
        part = hbm if level < 2 else hbm.at[level - 2]
        pairs.append((dil_hbm.at[level, :, :, pl.ds(begin, 512)], ref.at[:, pl.ds(0, 128), :]))
        for tap in range(3):
            pairs.append((part.at[pl.ds(tap * 128, 128), :], ref.at[tap, pl.ds(128, 128), :]))
    return [pltpu.make_async_copy(a, b, sems.at[i]) for i, (a, b) in enumerate(pairs)]


def mixing_copies(level, info, mix_hbm, got_hbm, sib_hbm, mix_ref, sems):
    pairs = []
    for half, hbm in enumerate((got_hbm, sib_hbm)):
        part = hbm if level < 2 else hbm.at[level - 2]
        begin = info[0] if half == 0 else 1 - info[0]
        rows = pl.ds(pl.multiple_of(begin * 512, 512), 512)
        pairs.append((mix_hbm.at[level, rows, :], mix_ref.at[half, :, pl.ds(0, 128)]))
        for y in range(4):
            pairs.append(
                (
                    part.at[pl.ds(384, 128), pl.ds(y * 128, 128)],
                    mix_ref.at[half, pl.ds(y * 128, 128), pl.ds(128, 128)],
                )
            )
    return [pltpu.make_async_copy(a, b, sems.at[i]) for i, (a, b) in enumerate(pairs)]


def send_terms(level, info, h_ref, near_ref, away_ref, out_ref):
    step = 3**level
    count = HALF + 2 * HALO[level + 1]
    padded = out_ref.shape[1]
    rows = h_ref.shape[0]
    first = info[1] - HALO[level]
    pos = first + lax.broadcasted_iota(jnp.int32, (rows, 1), 0)
    inside = (pos >= 0) & (pos < UPPER)
    h_ref[...] = jnp.where(inside, jnp.maximum(h_ref[...], 0.0), 0.0)
    taps = [h_ref[tap * step : tap * step + count, :].astype(BF) for tap in range(3)]
    for half, ref in enumerate((near_ref, away_ref)):
        total = dot(taps[0], ref[0]) + dot(taps[1], ref[1]) + dot(taps[2], ref[2])
        total = total.astype(BF)
        for y in range(4):
            out_ref[y, :count, half * 128 : half * 128 + 128] = total[:, y * 128 : y * 128 + 128]
    if padded > count:
        for y in range(4):
            out_ref[y, count:, :] = jnp.zeros((padded - count, 256), BF)


def start(copies):
    for copy in copies:
        copy.start()


def finish(copies):
    for copy in copies:
        copy.wait()


DILATED = [pltpu.VMEM((3, 256, 512), BF), pltpu.VMEM((3, 256, 512), BF), pltpu.SemaphoreType.DMA((8,))]
MIXING = [pltpu.VMEM((2, 512, 256), BF), pltpu.SemaphoreType.DMA((10,))]


def first_kernel(info, codes_ref, table_ref, dil_hbm, got_ref, sib_ref, h_ref, out_ref, near_ref, away_ref, sems, work):
    copies = dilated_copies(0, info, dil_hbm, got_ref, sib_ref, near_ref, away_ref, sems)
    start(copies)
    codes = codes_ref[...]
    rows = codes.shape[0]
    lane = lax.broadcasted_iota(jnp.int32, (rows, 1024), 1)
    core = info[0]
    one = jnp.ones((), BF)
    zero = jnp.zeros((), BF)
    h_own = jnp.zeros((rows, 128), F32)
    h_oth = jnp.zeros((rows, 128), F32)
    for src, begin in ((got_ref, core * 1024), (sib_ref, (1 - core) * 1024)):
        hot = jnp.where(codes - begin == lane, one, zero)
        h_own += dot(hot, table_ref[pl.ds(pl.multiple_of(begin, 1024), 1024), :])
        for q in range(4):
            h_oth += dot(hot[:, q * 256 : q * 256 + 256], src[512:768, q * 128 : q * 128 + 128])
    work[:, :128] = h_own
    work[:, 128:] = h_oth
    h_ref[...] = work[...]
    finish(copies)
    send_terms(0, info, work, near_ref, away_ref, out_ref)


def mixed(level, r_ref, h_ref, mix_ref):
    step = 3**level
    count = HALF + 2 * HALO[level + 1]
    h = h_ref[step : step + count, :]
    for half in range(2):
        r = jnp.concatenate([r_ref[y, :, half * 128 : half * 128 + 128] for y in range(4)], axis=1)
        h += dot(r, mix_ref[half])[:count]
    return h


def middle_kernel(level, info, r_ref, h_ref, mix_hbm, got_hbm, sib_hbm, dil_hbm, got1_hbm, sib1_hbm, new_ref, out_ref, mix_ref, mix_sems, near_ref, away_ref, sems, work):
    first = mixing_copies(level, info, mix_hbm, got_hbm, sib_hbm, mix_ref, mix_sems)
    then = dilated_copies(level + 1, info, dil_hbm, got1_hbm, sib1_hbm, near_ref, away_ref, sems)
    start(first)
    start(then)
    finish(first)
    count = HALF + 2 * HALO[level + 1]
    if work.shape[0] > count:
        work[count:, :] = jnp.zeros((work.shape[0] - count, 256), F32)
    work[:count, :] = mixed(level, r_ref, h_ref, mix_ref)
    new_ref[...] = work[...]
    finish(then)
    send_terms(level + 1, info, work, near_ref, away_ref, out_ref)


def last_kernel(info, r_ref, h_ref, mix_hbm, got_hbm, sib_hbm, out_ref, mix_ref, mix_sems):
    copies = mixing_copies(3, info, mix_hbm, got_hbm, sib_hbm, mix_ref, mix_sems)
    start(copies)
    finish(copies)
    h = mixed(3, r_ref, h_ref, mix_ref).astype(BF)
    for peer in range(8):
        out_ref[peer] = h


def half_copies(info, level, dil_hbm, mix_hbm, dest):
    cols = pl.ds(pl.multiple_of(info[0] * 512, 512), 512)
    pairs = [(dil_hbm.at[level, tap, :, cols], dest.at[pl.ds(tap * 128, 128), :]) for tap in range(3)]
    for i in range(4):
        rows = pl.ds(pl.multiple_of(info[0] * 512 + i * 128, 128), 128)
        pairs.append((mix_hbm.at[level, rows, :], dest.at[pl.ds(384, 128), pl.ds(i * 128, 128)]))
    return pairs


def copies_of(pairs, sems):
    return [pltpu.make_async_copy(a, b, sems.at[i]) for i, (a, b) in enumerate(pairs)]


def pack_kernel(info, dil_hbm, mix_hbm, tab_hbm, up_hbm, mid_hbm, pack0, part_ref, up, mid, wide, sems):
    pairs = [
        (up_hbm.at[pl.ds(info[4] * 16, 16), pl.ds(pl.multiple_of(info[0] * 2 * D, 128), 2 * D)], up),
        (mid_hbm.at[pl.ds(info[5] * 16, 16), :], mid),
    ]
    pairs += half_copies(info, 0, dil_hbm, mix_hbm, pack0)
    for i in range(4):
        rows = pl.ds(pl.multiple_of(info[0] * 1024 + i * 256, 256), 256)
        pairs.append((tab_hbm.at[rows, :], pack0.at[pl.ds(512, 256), pl.ds(i * 128, 128)]))
    copies = copies_of(pairs, sems)
    start(copies)
    finish(copies[:2])
    wide[...] = jnp.zeros_like(wide)
    for block in range(BLOCKS):
        wide[:, block, :] = mid[:, block * 128 : block * 128 + 128].astype(F32)
    for y in range(4):
        for block in range(UP_BLOCKS):
            part_ref[y, block] = up[:, block * 128 : block * 128 + 128]
        part_ref[y, UP_BLOCKS:] = wide[...].astype(BF)
    finish(copies[2:])


def later_kernel(info, dil_hbm, mix_hbm, pack1, pack2, sems):
    pairs = half_copies(info, 1, dil_hbm, mix_hbm, pack1)
    for i in range(2):
        pairs += half_copies(info, 2 + i, dil_hbm, mix_hbm, pack2.at[i])
    copies = copies_of(pairs, sems)
    start(copies)
    finish(copies)


def join_kernel(mine, others, out):
    out[:4] = mine[...]
    out[4:] = others[...]


def call(body, outs, scratch=(), smem=1, n=0, hbm=0, after=0, flops=10**9, name=None):
    def spec(space):
        return pl.BlockSpec(memory_space=space)

    specs = [spec(pltpu.SMEM)] * smem + [spec(pltpu.VMEM)] * n
    specs += [spec(pl.ANY)] * hbm + [spec(pltpu.VMEM)] * after
    return pl.pallas_call(
        body,
        out_shape=outs,
        in_specs=specs,
        out_specs=jax.tree.map(lambda _: spec(pltpu.VMEM), outs),
        scratch_shapes=list(scratch),
        compiler_params=params(),
        cost_estimate=cost(flops, 4 << 20),
        name=name,
    )


def shape(*dims, dtype=BF):
    return jax.ShapeDtypeStruct(dims, dtype)


CHUNKS = ((0, 4), (4, 4), (8, 4), (12, 3))


def frames_kernel(pair, info, codes_ref, hf_ref, gain_ref, qkv_hbm, full_ref, q_ref, kv_ref, weights, table, qkv, hf, rows, x, xn, sems, table_sems, qkv_sem):
    def weight_copies(phase):
        return [
            pltpu.make_async_copy(
                full_ref.at[pl.ds(part * 4 ^ info[3], 4), pair, t ^ info[3], pl.ds(phase * BLOCKS, BLOCKS)],
                weights.at[phase, t, pl.ds(part * 4, 4)],
                sems.at[phase, part, t],
            )
            for part in range(2)
            for t in range(8)
        ]

    def product(phase):
        for first, size in CHUNKS:
            w = [weights[phase, :, :, block].reshape(C, 128) for block in range(first, first + size)]
            x[phase, :, first * 128 : (first + size) * 128] = dot(hf[...], jnp.concatenate(w, axis=1))

    def norm(phase):
        total = jnp.zeros((256, 128), F32)
        for block in range(BLOCKS):
            cols = slice(block * 128, block * 128 + 128)
            y = x[phase, :, cols] + rows[pl.ds(phase * 256, 256), block, :]
            x[phase, :, cols] = y
            total += y
        mean = jnp.sum(total, axis=1, keepdims=True) * (1.0 / D)
        square = jnp.zeros((256, 128), F32)
        for block in range(BLOCKS):
            y = x[phase, :, block * 128 : block * 128 + 128] - mean
            square += y * y
        factor = lax.rsqrt(jnp.sum(square, axis=1, keepdims=True) * (1.0 / D) + 1e-5)
        for block in range(BLOCKS):
            cols = slice(block * 128, block * 128 + 128)
            xn[phase, :, cols] = ((x[phase, :, cols] - mean) * factor * gain_ref[:, cols]).astype(BF)

    def project(phase):
        y = dot(xn[phase], qkv[...]).astype(BF)
        lines = slice(phase * 256, phase * 256 + 256)
        for head in range(2):
            at = head * 384
            cols = slice(head * 128, head * 128 + 128)
            q_ref[lines, cols] = y[:, at : at + 128]
            kv_ref[lines, cols] = y[:, at + 128 : at + 256]
            kv_ref[lines, 256 + head * 128 : 384 + head * 128] = y[:, at + 256 : at + 384]

    table_copies = [
        pltpu.make_async_copy(
            full_ref.at[:, part, :, pl.ds(UP_BLOCKS, 16)], table.at[:, part], table_sems.at[part]
        )
        for part in range(2)
    ]
    qkv_copy = pltpu.make_async_copy(qkv_hbm, qkv, qkv_sem)
    start(table_copies)
    start(weight_copies(0))
    start(weight_copies(1))
    qkv_copy.start()
    for half in range(2):
        for j in range(8):
            at = 0 if j // 4 == half else 128
            hf[half * 128 : half * 128 + 128, j * 128 : j * 128 + 128] = hf_ref[
                half * 4 + j % 4, :, at : at + 128
            ]
    flat = table.reshape(VOCAB, 16, 128)
    finish(table_copies)

    def look_up(i, carry):
        for j in range(8):
            row = i * 8 + j
            rows[row] = flat[codes_ref[pair * 512 + row]].astype(F32)
        return carry

    lax.fori_loop(0, 64, look_up, 0)
    finish(weight_copies(0))
    product(0)
    finish(weight_copies(1))
    qkv_copy.wait()
    norm(0)
    product(1)
    project(0)
    norm(1)
    project(1)


def frames(pair, info, codes, hf, gain, qkv, full):
    vm = pl.BlockSpec(memory_space=pltpu.VMEM)
    sm = pl.BlockSpec(memory_space=pltpu.SMEM)
    return pl.pallas_call(
        functools.partial(frames_kernel, pair),
        out_shape=(shape(512, 256), shape(512, 512)),
        in_specs=[sm, sm, vm, vm, pl.BlockSpec(memory_space=pl.ANY), pl.BlockSpec(memory_space=pltpu.HBM)],
        out_specs=(vm, vm),
        scratch_shapes=[
            pltpu.VMEM((2, 8, 8, BLOCKS, 16, 128), BF),
            pltpu.VMEM((8, 2, 8, 16, 16, 128), BF),
            pltpu.VMEM((D, 768), BF),
            pltpu.VMEM((256, C), BF),
            pltpu.VMEM((512, 16, 128), F32),
            pltpu.VMEM((2, 256, D), F32),
            pltpu.VMEM((2, 256, D), BF),
            pltpu.SemaphoreType.DMA((2, 2, 8)),
            pltpu.SemaphoreType.DMA((2,)),
            pltpu.SemaphoreType.DMA,
        ],
        compiler_params=params(),
        cost_estimate=cost(4 * 10**9, 20 << 20),
        name="frames",
    )(info, codes, hf, gain, qkv, full)


SCALE = 128**-0.5 * 1.4426950408889634


def scores_of(q, k):
    return lax.dot_general(q, k, (((1,), (1,)), ((), ())), preferred_element_type=F32)


def fold(q_refs, kv, seen_of, old_of, put):
    def body(head, carry):
        k = kv[:, pl.ds(pl.multiple_of(head * 128, 128), 128)]
        v = kv[:, pl.ds(pl.multiple_of(256 + head * 128, 128), 128)]
        v = jnp.concatenate([v, jnp.ones(v.shape, BF)], axis=1)
        cols = pl.ds(pl.multiple_of(head * 128, 128), 128)
        for phase in range(4):
            s = scores_of(q_refs[phase // 2][phase % 2 * 256 : phase % 2 * 256 + 256, cols], k)
            s = jnp.where(seen_of(phase), s, -1e30)
            top = jnp.max(s, axis=1, keepdims=True)
            old = old_of(head, phase)
            if old is None:
                put(head, phase, top, dot(jnp.exp2((s - top) * SCALE).astype(BF), v))
            else:
                top = jnp.maximum(old[0], top)
                p = jnp.exp2((s - top) * SCALE).astype(BF)
                put(head, phase, top, old[1] * jnp.exp2((old[0] - top) * SCALE) + dot(p, v))
        return carry

    lax.fori_loop(0, 2, body, 0)


def join_keys(kv, first, second):
    kv[:512] = first[...]
    kv[512:] = second[...]


def own_kernel(q0_ref, q1_ref, kv0_ref, kv1_ref, acc_ref, top_ref, kv):
    join_keys(kv, kv0_ref, kv1_ref)
    col = lax.broadcasted_iota(jnp.int32, (256, 1024), 1)
    ahead = (col & 255) * 4 + (col >> 8) - 4 * lax.broadcasted_iota(jnp.int32, (256, 1024), 0)

    def put(head, phase, top, acc):
        top_ref[head, phase] = top
        acc_ref[head, phase] = acc

    fold((q0_ref, q1_ref), kv, lambda p: ahead <= p, lambda head, phase: None, put)


def past_kernel(last, info, q0_ref, q1_ref, far_ref, near_ref, acc_ref, top_ref, *refs):
    if last:
        out_ref, kv, acc, tops, wide = refs
    else:
        acc, tops, kv = refs
    song = info[2]

    @pl.when(song == 0)
    def _():
        acc[...] = acc_ref[...]
        tops[...] = top_ref[...]

    @pl.when(song > 0)
    def _():
        join_keys(kv, far_ref, near_ref)
        col = lax.broadcasted_iota(jnp.int32, (256, 1024), 1)
        seen = col >= jnp.where(song == 1, 512, 0)

        def put(head, phase, top, total):
            tops[head, phase] = top
            acc[head, phase] = total

        fold(
            (q0_ref, q1_ref),
            kv,
            lambda p: seen,
            lambda head, phase: (top_ref[head, phase], acc_ref[head, phase]),
            put,
        )

    if last:
        for head in range(2):
            for phase in range(4):
                both = acc[head, phase]
                wide[pl.ds(phase, 256, stride=4), :] = both[:, :128] / both[:, 128:]
            out_ref[:, head * 128 : head * 128 + 128] = wide[...].astype(BF)


EVERY = ("song", "tensor")


def other_half():
    pairs = []
    for song in range(16):
        for rank in range(8):
            pairs.append((song * 8 + rank, (song ^ 8) * 8 + (rank ^ 4)))
    return pairs


def song_neighbours():
    first = [(song * 8 + rank, song * 8 + 8 + rank) for song in range(15) for rank in range(4)]
    second = [(song * 8 + 8 + rank, song * 8 + rank) for song in range(15) for rank in range(4, 8)]
    return first + second


def to_sibling(value):
    return lax.ppermute(value, "song", [(i, i ^ 1) for i in range(16)])


def exchange(value, axis="tensor", groups=None):
    return lax.all_to_all(value, axis, 0, 0, axis_index_groups=groups, tiled=True)


def on_device(
    upper_codes,
    middle_codes,
    upper_table,
    dilated_weight,
    mixing_weight,
    upsample_weight,
    middle_table,
    norm_gain,
    qkv_weight,
):
    song = lax.axis_index("song")
    rank = lax.axis_index("tensor")
    core = song % 2
    x_hi = rank // 4
    begin = song * 256 + x_hi * HALF
    share = song ^ (8 * x_hi)
    info = jnp.stack([core, begin, song, x_hi * 4, share // 2, share]).astype(jnp.int32)

    pack0, part = call(
        pack_kernel,
        (shape(768, 512), shape(4, PART, 16, 128)),
        [
            pltpu.VMEM((16, 2 * D), BF),
            pltpu.VMEM((16, D), BF),
            pltpu.VMEM((16, 16, 128), F32),
            pltpu.SemaphoreType.DMA((13,)),
        ],
        hbm=5,
        name="pack",
    )(info, dilated_weight, mixing_weight, upper_table, upsample_weight, middle_table)
    got0 = lax.ppermute(pack0, EVERY, other_half())
    mine = exchange(part, groups=Y_GROUPS)
    edge = jnp.where(x_hi == 0, upper_codes[-40:], upper_codes[:40])
    edge = lax.ppermute(edge, EVERY, song_neighbours())
    mine, got0, edge = lax.optimization_barrier((mine, got0, edge))
    others = lax.ppermute(mine, EVERY, other_half())
    sib0 = to_sibling(got0)
    codes = jnp.where(
        x_hi == 0,
        jnp.concatenate([edge, upper_codes[: HALF + 40]]),
        jnp.concatenate([upper_codes[HALF - 40 :], edge]),
    )[:, None]

    h, terms = call(
        first_kernel,
        (shape(ROWS[0], 256, dtype=F32), shape(4, ROWS[1], 256)),
        [*DILATED, pltpu.VMEM((ROWS[0], 256), F32)],
        n=2,
        hbm=1,
        after=2,
        name="cond0",
    )(info, codes, upper_table, dilated_weight, got0, sib0)
    pack1, pack2 = call(
        later_kernel,
        (shape(512, 512), shape(2, 512, 512)),
        [pltpu.SemaphoreType.DMA((21,))],
        hbm=2,
        name="pack_later",
    )(info, dilated_weight, mixing_weight)

    others, pack1, terms = lax.optimization_barrier((others, pack1, terms))
    both = call(join_kernel, shape(8, PART, 16, 128), smem=0, n=2, name="join")(mine, others)
    full = lax.all_gather(both, "song", axis=0, tiled=False)
    full = full.reshape(8, 2, 8, PART, 16, 128)
    got1 = lax.ppermute(pack1, EVERY, other_half())
    for level in range(4):
        terms = exchange(terms, groups=Y_GROUPS)
        total = terms[0].astype(F32)
        for y in range(1, 4):
            total = total + terms[y].astype(F32)
        r = jnp.maximum(total, 0.0).astype(BF)
        r = exchange(jnp.broadcast_to(r[None], terms.shape), groups=Y_GROUPS)
        if level == 0:
            got1, pack2, r = lax.optimization_barrier((got1, pack2, r))
            sib1 = to_sibling(got1)
            got2 = lax.ppermute(pack2, EVERY, other_half())
            stacks = [(got0, sib0), (got1, sib1)]
        if level == 1:
            got2, r = lax.optimization_barrier((got2, r))
            stacks += [(got2, to_sibling(got2))] * 2
        if level < 3:
            h, terms = call(
                functools.partial(middle_kernel, level),
                (shape(ROWS[level + 1], 256, dtype=F32), shape(4, ROWS[level + 2], 256)),
                [*MIXING, *DILATED, pltpu.VMEM((ROWS[level + 1], 256), F32)],
                n=2,
                hbm=6,
                name="cond",
            )(info, r, h, mixing_weight, *stacks[level], dilated_weight, *stacks[level + 1])
        else:
            spread = call(
                last_kernel, shape(8, HALF, 256), MIXING, n=2, hbm=3, name="cond_end"
            )(info, r, h, mixing_weight, *stacks[level])
    hf = exchange(spread)

    mid = middle_codes.reshape(256, 4).T.reshape(1024)
    mid = ((mid % 256) // 16 * 128 + mid // 256 * 16 + mid % 16) ^ (x_hi * (8 * 128 + 4 * 16))
    gain = norm_gain[None]
    qkv = qkv_weight.reshape(D, 768)

    def from_two_back(value):
        return lax.ppermute(value, "song", [(i, i + 2) for i in range(14)])

    q0, kv0 = frames(0, info, mid, hf, gain, qkv, full)
    far0 = from_two_back(kv0)
    q1, kv1 = frames(1, info, mid, hf, gain, qkv, full)
    far1 = from_two_back(kv1)
    state = (shape(2, 4, 256, 256, dtype=F32), shape(2, 4, 256, 1, dtype=F32))
    keys = pltpu.VMEM((1024, 512), BF)
    far0, q1 = lax.optimization_barrier((far0, q1))
    kept = call(own_kernel, state, [keys], smem=0, n=4, flops=10**9, name="own")(q0, q1, kv0, kv1)
    near0 = to_sibling(jnp.where(core == 0, kv0, far0))
    kept = call(functools.partial(past_kernel, False), state, [keys], n=6, flops=10**9, name="past")(
        info, q0, q1, far0, near0, *kept
    )
    far1, kept = lax.optimization_barrier((far1, kept))
    near1 = to_sibling(jnp.where(core == 0, kv1, far1))
    return call(
        functools.partial(past_kernel, True),
        shape(1024, 256),
        [
            keys,
            pltpu.VMEM((2, 4, 256, 256), F32),
            pltpu.VMEM((2, 4, 256, 1), F32),
            pltpu.VMEM((1024, 128), F32),
        ],
        n=6,
        flops=2 * 10**9,
        name="past_end",
    )(info, q0, q1, far1, near1, *kept)


def solution(mesh):
    placed = (
        P("song"),
        P("song"),
        P(None, "tensor"),
        P(None, None, "tensor", None),
        P(None, None, "tensor"),
        P("tensor", None),
        P("tensor", None),
        P(),
        P(None, "tensor", None),
    )
    return jax.shard_map(
        on_device, mesh=mesh, in_specs=placed, out_specs=P("song", "tensor"), check_vma=False
    )
```

```python
import functools

import jax
import jax.numpy as jnp
from jax import lax
from jax.experimental import pallas as pl
from jax.experimental.pallas import tpu as pltpu
from jax.sharding import PartitionSpec as P

BF = jnp.bfloat16
F32 = jnp.float32
D = 1920
C = 1024
VOCAB = 2048
UPPER = 4096
HALF = 128
HALO = (40, 39, 36, 27, 0)
ROWS = (208, 208, 208, 192, 128)
VMEM_LIMIT = 60 << 20

BLOCKS = D // 128
UP_BLOCKS = 2 * BLOCKS
PART = UP_BLOCKS + 16

Y_GROUPS = [[0, 1, 2, 3], [4, 5, 6, 7]]


def params(**kw):
    return pltpu.CompilerParams(vmem_limit_bytes=VMEM_LIMIT, **kw)


def cost(flops, nbytes, trans=0):
    return pl.CostEstimate(flops=flops, bytes_accessed=nbytes, transcendentals=trans)


def dot(a, b):
    return jnp.dot(a, b, preferred_element_type=F32)


def dilated_copies(level, info, dil_hbm, got_hbm, sib_hbm, near_ref, away_ref, sems):
    own = pl.multiple_of(info[0] * 512, 512)
    other = pl.multiple_of((1 - info[0]) * 512, 512)
    pairs = []
    for ref, hbm, begin in ((near_ref, got_hbm, own), (away_ref, sib_hbm, other)):
        part = hbm if level < 2 else hbm.at[level - 2]
        pairs.append((dil_hbm.at[level, :, :, pl.ds(begin, 512)], ref.at[:, pl.ds(0, 128), :]))
        for tap in range(3):
            pairs.append((part.at[pl.ds(tap * 128, 128), :], ref.at[tap, pl.ds(128, 128), :]))
    return [pltpu.make_async_copy(a, b, sems.at[i]) for i, (a, b) in enumerate(pairs)]


def mixing_copies(level, info, mix_hbm, got_hbm, sib_hbm, mix_ref, sems):
    pairs = []
    for half, hbm in enumerate((got_hbm, sib_hbm)):
        part = hbm if level < 2 else hbm.at[level - 2]
        begin = info[0] if half == 0 else 1 - info[0]
        rows = pl.ds(pl.multiple_of(begin * 512, 512), 512)
        pairs.append((mix_hbm.at[level, rows, :], mix_ref.at[half, :, pl.ds(0, 128)]))
        for y in range(4):
            pairs.append(
                (
                    part.at[pl.ds(384, 128), pl.ds(y * 128, 128)],
                    mix_ref.at[half, pl.ds(y * 128, 128), pl.ds(128, 128)],
                )
            )
    return [pltpu.make_async_copy(a, b, sems.at[i]) for i, (a, b) in enumerate(pairs)]


def send_terms(level, info, h_ref, near_ref, away_ref, out_ref):
    step = 3**level
    count = HALF + 2 * HALO[level + 1]
    padded = out_ref.shape[1]
    rows = h_ref.shape[0]
    first = info[1] - HALO[level]
    pos = first + lax.broadcasted_iota(jnp.int32, (rows, 1), 0)
    inside = (pos >= 0) & (pos < UPPER)
    h_ref[...] = jnp.where(inside, jnp.maximum(h_ref[...], 0.0), 0.0)
    taps = [h_ref[tap * step : tap * step + count, :].astype(BF) for tap in range(3)]
    for half, ref in enumerate((near_ref, away_ref)):
        total = dot(taps[0], ref[0]) + dot(taps[1], ref[1]) + dot(taps[2], ref[2])
        total = total.astype(BF)
        for y in range(4):
            out_ref[y, :count, half * 128 : half * 128 + 128] = total[:, y * 128 : y * 128 + 128]
    if padded > count:
        for y in range(4):
            out_ref[y, count:, :] = jnp.zeros((padded - count, 256), BF)


def start(copies):
    for copy in copies:
        copy.start()


def finish(copies):
    for copy in copies:
        copy.wait()


DILATED = [pltpu.VMEM((3, 256, 512), BF), pltpu.VMEM((3, 256, 512), BF), pltpu.SemaphoreType.DMA((8,))]
MIXING = [pltpu.VMEM((2, 512, 256), BF), pltpu.SemaphoreType.DMA((10,))]


def first_kernel(info, codes_ref, table_ref, dil_hbm, got_ref, sib_ref, h_ref, out_ref, near_ref, away_ref, sems, work):
    copies = dilated_copies(0, info, dil_hbm, got_ref, sib_ref, near_ref, away_ref, sems)
    start(copies)
    codes = codes_ref[...]
    rows = codes.shape[0]
    lane = lax.broadcasted_iota(jnp.int32, (rows, 1024), 1)
    core = info[0]
    one = jnp.ones((), BF)
    zero = jnp.zeros((), BF)
    h_own = jnp.zeros((rows, 128), F32)
    h_oth = jnp.zeros((rows, 128), F32)
    for src, begin in ((got_ref, core * 1024), (sib_ref, (1 - core) * 1024)):
        hot = jnp.where(codes - begin == lane, one, zero)
        h_own += dot(hot, table_ref[pl.ds(pl.multiple_of(begin, 1024), 1024), :])
        for q in range(4):
            h_oth += dot(hot[:, q * 256 : q * 256 + 256], src[512:768, q * 128 : q * 128 + 128])
    work[:, :128] = h_own
    work[:, 128:] = h_oth
    h_ref[...] = work[...]
    finish(copies)
    send_terms(0, info, work, near_ref, away_ref, out_ref)


def mixed(level, r_ref, h_ref, mix_ref):
    step = 3**level
    count = HALF + 2 * HALO[level + 1]
    h = h_ref[step : step + count, :]
    for half in range(2):
        r = jnp.concatenate([r_ref[y, :, half * 128 : half * 128 + 128] for y in range(4)], axis=1)
        h += dot(r, mix_ref[half])[:count]
    return h


def middle_kernel(level, info, r_ref, h_ref, mix_hbm, got_hbm, sib_hbm, dil_hbm, got1_hbm, sib1_hbm, new_ref, out_ref, mix_ref, mix_sems, near_ref, away_ref, sems, work):
    first = mixing_copies(level, info, mix_hbm, got_hbm, sib_hbm, mix_ref, mix_sems)
    then = dilated_copies(level + 1, info, dil_hbm, got1_hbm, sib1_hbm, near_ref, away_ref, sems)
    start(first)
    start(then)
    finish(first)
    count = HALF + 2 * HALO[level + 1]
    if work.shape[0] > count:
        work[count:, :] = jnp.zeros((work.shape[0] - count, 256), F32)
    work[:count, :] = mixed(level, r_ref, h_ref, mix_ref)
    new_ref[...] = work[...]
    finish(then)
    send_terms(level + 1, info, work, near_ref, away_ref, out_ref)


def last_kernel(info, r_ref, h_ref, mix_hbm, got_hbm, sib_hbm, out_ref, mix_ref, mix_sems):
    copies = mixing_copies(3, info, mix_hbm, got_hbm, sib_hbm, mix_ref, mix_sems)
    start(copies)
    finish(copies)
    h = mixed(3, r_ref, h_ref, mix_ref).astype(BF)
    for peer in range(8):
        out_ref[peer] = h


def half_copies(info, level, dil_hbm, mix_hbm, dest):
    cols = pl.ds(pl.multiple_of(info[0] * 512, 512), 512)
    pairs = [(dil_hbm.at[level, tap, :, cols], dest.at[pl.ds(tap * 128, 128), :]) for tap in range(3)]
    for i in range(4):
        rows = pl.ds(pl.multiple_of(info[0] * 512 + i * 128, 128), 128)
        pairs.append((mix_hbm.at[level, rows, :], dest.at[pl.ds(384, 128), pl.ds(i * 128, 128)]))
    return pairs


def copies_of(pairs, sems):
    return [pltpu.make_async_copy(a, b, sems.at[i]) for i, (a, b) in enumerate(pairs)]


def pack_kernel(info, dil_hbm, mix_hbm, tab_hbm, up_hbm, mid_hbm, pack0, part_ref, up, mid, wide, sems):
    pairs = [
        (up_hbm.at[pl.ds(info[4] * 16, 16), pl.ds(pl.multiple_of(info[0] * 2 * D, 128), 2 * D)], up),
        (mid_hbm.at[pl.ds(info[5] * 16, 16), :], mid),
    ]
    pairs += half_copies(info, 0, dil_hbm, mix_hbm, pack0)
    for i in range(4):
        rows = pl.ds(pl.multiple_of(info[0] * 1024 + i * 256, 256), 256)
        pairs.append((tab_hbm.at[rows, :], pack0.at[pl.ds(512, 256), pl.ds(i * 128, 128)]))
    copies = copies_of(pairs, sems)
    start(copies)
    finish(copies[:2])
    wide[...] = jnp.zeros_like(wide)
    for block in range(BLOCKS):
        wide[:, block, :] = mid[:, block * 128 : block * 128 + 128].astype(F32)
    for y in range(4):
        for block in range(UP_BLOCKS):
            part_ref[y, block] = up[:, block * 128 : block * 128 + 128]
        part_ref[y, UP_BLOCKS:] = wide[...].astype(BF)
    finish(copies[2:])


def later_kernel(info, dil_hbm, mix_hbm, pack1, pack2, sems):
    pairs = half_copies(info, 1, dil_hbm, mix_hbm, pack1)
    for i in range(2):
        pairs += half_copies(info, 2 + i, dil_hbm, mix_hbm, pack2.at[i])
    copies = copies_of(pairs, sems)
    start(copies)
    finish(copies)


def call(body, outs, scratch=(), smem=1, n=0, hbm=0, after=0, flops=10**9, name=None):
    def spec(space):
        return pl.BlockSpec(memory_space=space)

    specs = [spec(pltpu.SMEM)] * smem + [spec(pltpu.VMEM)] * n
    specs += [spec(pl.ANY)] * hbm + [spec(pltpu.VMEM)] * after
    return pl.pallas_call(
        body,
        out_shape=outs,
        in_specs=specs,
        out_specs=jax.tree.map(lambda _: spec(pltpu.VMEM), outs),
        scratch_shapes=list(scratch),
        compiler_params=params(),
        cost_estimate=cost(flops, 4 << 20),
        name=name,
    )


def shape(*dims, dtype=BF):
    return jax.ShapeDtypeStruct(dims, dtype)


CHUNKS = ((0, 4), (4, 4), (8, 4), (12, 3))


def frames_kernel(pair, info, codes_ref, hf_ref, gain_ref, qkv_hbm, own_hbm, other_hbm, q_ref, kv_ref, weights, table, qkv, hf, rows, x, xn, sems, table_sems, qkv_sem):
    def weight_copies(phase):
        return [
            pltpu.make_async_copy(
                full.at[pl.ds(part * 4 ^ info[3], 4), pair, y, pl.ds(phase * BLOCKS, BLOCKS)],
                weights.at[phase, half, y, pl.ds(part * 4, 4)],
                sems.at[phase, half, part, y],
            )
            for half, full in enumerate((own_hbm, other_hbm))
            for part in range(2)
            for y in range(4)
        ]

    def product(phase):
        for first, size in CHUNKS:
            w = [weights[phase, :, :, :, block].reshape(C, 128) for block in range(first, first + size)]
            x[phase, :, first * 128 : (first + size) * 128] = dot(hf[...], jnp.concatenate(w, axis=1))

    def norm(phase):
        total = jnp.zeros((256, 128), F32)
        for block in range(BLOCKS):
            cols = slice(block * 128, block * 128 + 128)
            y = x[phase, :, cols] + rows[pl.ds(phase * 256, 256), block, :]
            x[phase, :, cols] = y
            total += y
        mean = jnp.sum(total, axis=1, keepdims=True) * (1.0 / D)
        square = jnp.zeros((256, 128), F32)
        for block in range(BLOCKS):
            y = x[phase, :, block * 128 : block * 128 + 128] - mean
            square += y * y
        factor = lax.rsqrt(jnp.sum(square, axis=1, keepdims=True) * (1.0 / D) + 1e-5)
        for block in range(BLOCKS):
            cols = slice(block * 128, block * 128 + 128)
            xn[phase, :, cols] = ((x[phase, :, cols] - mean) * factor * gain_ref[:, cols]).astype(BF)

    def project(phase):
        y = dot(xn[phase], qkv[...]).astype(BF)
        lines = slice(phase * 256, phase * 256 + 256)
        for head in range(2):
            at = head * 384
            cols = slice(head * 128, head * 128 + 128)
            q_ref[lines, cols] = y[:, at : at + 128]
            kv_ref[lines, cols] = y[:, at + 128 : at + 256]
            kv_ref[lines, 256 + head * 128 : 384 + head * 128] = y[:, at + 256 : at + 384]

    table_copies = [
        pltpu.make_async_copy(
            full.at[:, part, :, pl.ds(UP_BLOCKS, 16)], table.at[half, :, part], table_sems.at[half, part]
        )
        for half, full in enumerate((own_hbm, other_hbm))
        for part in range(2)
    ]
    qkv_copy = pltpu.make_async_copy(qkv_hbm, qkv, qkv_sem)
    start(table_copies)
    start(weight_copies(0))
    start(weight_copies(1))
    qkv_copy.start()
    for rows_of in range(2):
        for half in range(2):
            at = pl.multiple_of(((info[3] // 4) ^ half ^ rows_of) * 128, 128)
            for y in range(4):
                j = half * 4 + y
                hf[rows_of * 128 : rows_of * 128 + 128, j * 128 : j * 128 + 128] = hf_ref[
                    rows_of * 4 + y, :, pl.ds(at, 128)
                ]
    flat = table.reshape(VOCAB, 16, 128)

    def look_up(phase):
        for row in range(phase * 256, phase * 256 + 256):
            rows[row] = flat[codes_ref[pair * 512 + row]].astype(F32)

    finish(table_copies)
    finish(weight_copies(0))
    look_up(0)
    product(0)
    finish(weight_copies(1))
    qkv_copy.wait()
    look_up(1)
    product(1)
    norm(0)
    project(0)
    norm(1)
    project(1)


def frames(pair, info, codes, hf, gain, qkv, full_own, full_other):
    vm = pl.BlockSpec(memory_space=pltpu.VMEM)
    sm = pl.BlockSpec(memory_space=pltpu.SMEM)
    any_space = pl.BlockSpec(memory_space=pl.ANY)
    return pl.pallas_call(
        functools.partial(frames_kernel, pair),
        out_shape=(shape(512, 256), shape(512, 512)),
        in_specs=[sm, sm, vm, vm, any_space, any_space, any_space],
        out_specs=(vm, vm),
        scratch_shapes=[
            pltpu.VMEM((2, 2, 4, 8, BLOCKS, 16, 128), BF),
            pltpu.VMEM((2, 8, 2, 4, 16, 16, 128), BF),
            pltpu.VMEM((D, 768), BF),
            pltpu.VMEM((256, C), BF),
            pltpu.VMEM((512, 16, 128), F32),
            pltpu.VMEM((2, 256, D), F32),
            pltpu.VMEM((2, 256, D), BF),
            pltpu.SemaphoreType.DMA((2, 2, 2, 4)),
            pltpu.SemaphoreType.DMA((2, 2)),
            pltpu.SemaphoreType.DMA,
        ],
        compiler_params=params(),
        cost_estimate=cost(4 * 10**9, 20 << 20),
        name="frames",
    )(info, codes, hf, gain, qkv, full_own, full_other)


SCALE = 128**-0.5 * 1.4426950408889634


def scores_of(q, k):
    return lax.dot_general(q, k, (((1,), (1,)), ((), ())), preferred_element_type=F32)


def fold(q_refs, kv, seen_of, old_of, put):
    for head in range(2):
        cols = slice(head * 128, head * 128 + 128)
        k = kv[:, cols]
        v = kv[:, 256 + head * 128 : 384 + head * 128]
        v = jnp.concatenate([v, jnp.ones(v.shape, BF)], axis=1)
        for phase in range(4):
            s = scores_of(q_refs[phase // 2][phase % 2 * 256 : phase % 2 * 256 + 256, cols], k)
            s = jnp.where(seen_of(phase), s, -1e30)
            top = jnp.max(s, axis=1, keepdims=True)
            old = old_of(head, phase)
            if old is None:
                put(head, phase, top, dot(jnp.exp2((s - top) * SCALE).astype(BF), v))
            else:
                top = jnp.maximum(old[0], top)
                p = jnp.exp2((s - top) * SCALE).astype(BF)
                put(head, phase, top, old[1] * jnp.exp2((old[0] - top) * SCALE) + dot(p, v))


def join_keys(kv, first, second):
    kv[:512] = first[...]
    kv[512:] = second[...]


def own_kernel(q0_ref, q1_ref, kv0_ref, kv1_ref, acc_ref, top_ref, kv):
    join_keys(kv, kv0_ref, kv1_ref)
    col = lax.broadcasted_iota(jnp.int32, (256, 1024), 1)
    ahead = (col & 255) * 4 + (col >> 8) - 4 * lax.broadcasted_iota(jnp.int32, (256, 1024), 0)

    def put(head, phase, top, acc):
        top_ref[head, phase] = top
        acc_ref[head, phase] = acc

    fold((q0_ref, q1_ref), kv, lambda p: ahead <= p, lambda head, phase: None, put)


def past_kernel(last, info, q0_ref, q1_ref, far_ref, near_ref, acc_ref, top_ref, *refs):
    if last:
        out_ref, kv, acc, tops, wide = refs
    else:
        acc, tops, kv = refs
    song = info[2]

    @pl.when(song == 0)
    def _():
        acc[...] = acc_ref[...]
        tops[...] = top_ref[...]

    @pl.when(song > 0)
    def _():
        join_keys(kv, far_ref, near_ref)
        col = lax.broadcasted_iota(jnp.int32, (256, 1024), 1)
        seen = col >= jnp.where(song == 1, 512, 0)

        def put(head, phase, top, total):
            tops[head, phase] = top
            acc[head, phase] = total

        fold(
            (q0_ref, q1_ref),
            kv,
            lambda p: seen,
            lambda head, phase: (top_ref[head, phase], acc_ref[head, phase]),
            put,
        )

    if last:
        for head in range(2):
            for phase in range(4):
                both = acc[head, phase]
                wide[pl.ds(phase, 256, stride=4), :] = both[:, :128] / both[:, 128:]
            out_ref[:, head * 128 : head * 128 + 128] = wide[...].astype(BF)


EVERY = ("song", "tensor")


def other_half():
    pairs = []
    for song in range(16):
        for rank in range(8):
            pairs.append((song * 8 + rank, (song ^ 8) * 8 + (rank ^ 4)))
    return pairs


def song_neighbours():
    first = [(song * 8 + rank, song * 8 + 8 + rank) for song in range(15) for rank in range(4)]
    second = [(song * 8 + 8 + rank, song * 8 + rank) for song in range(15) for rank in range(4, 8)]
    return first + second


def to_sibling(value):
    return lax.ppermute(value, "song", [(i, i ^ 1) for i in range(16)])


def exchange(value, axis="tensor", groups=None):
    return lax.all_to_all(value, axis, 0, 0, axis_index_groups=groups, tiled=True)


def gathered(parts):
    return lax.all_gather(parts, "song", axis=0, tiled=False).reshape(8, 2, 4, PART, 16, 128)


def on_device(
    upper_codes,
    middle_codes,
    upper_table,
    dilated_weight,
    mixing_weight,
    upsample_weight,
    middle_table,
    norm_gain,
    qkv_weight,
):
    song = lax.axis_index("song")
    rank = lax.axis_index("tensor")
    core = song % 2
    x_hi = rank // 4
    begin = song * 256 + x_hi * HALF
    share = song ^ (8 * x_hi)
    info = jnp.stack([core, begin, song, x_hi * 4, share // 2, share]).astype(jnp.int32)

    pack0, part = call(
        pack_kernel,
        (shape(768, 512), shape(4, PART, 16, 128)),
        [
            pltpu.VMEM((16, 2 * D), BF),
            pltpu.VMEM((16, D), BF),
            pltpu.VMEM((16, 16, 128), F32),
            pltpu.SemaphoreType.DMA((13,)),
        ],
        hbm=5,
        name="pack",
    )(info, dilated_weight, mixing_weight, upper_table, upsample_weight, middle_table)
    got0 = lax.ppermute(pack0, EVERY, other_half())
    mine = exchange(part, groups=Y_GROUPS)
    edge = jnp.where(x_hi == 0, upper_codes[-40:], upper_codes[:40])
    edge = lax.ppermute(edge, EVERY, song_neighbours())
    mine, got0, edge = lax.optimization_barrier((mine, got0, edge))
    full_own = gathered(mine)
    others = lax.ppermute(mine, EVERY, other_half())
    sib0 = to_sibling(got0)
    codes = jnp.where(
        x_hi == 0,
        jnp.concatenate([edge, upper_codes[: HALF + 40]]),
        jnp.concatenate([upper_codes[HALF - 40 :], edge]),
    )[:, None]

    h, terms = call(
        first_kernel,
        (shape(ROWS[0], 256, dtype=F32), shape(4, ROWS[1], 256)),
        [*DILATED, pltpu.VMEM((ROWS[0], 256), F32)],
        n=2,
        hbm=1,
        after=2,
        name="cond0",
    )(info, codes, upper_table, dilated_weight, got0, sib0)
    pack1, pack2 = call(
        later_kernel,
        (shape(512, 512), shape(2, 512, 512)),
        [pltpu.SemaphoreType.DMA((21,))],
        hbm=2,
        name="pack_later",
    )(info, dilated_weight, mixing_weight)

    for level in range(4):
        terms = exchange(terms, groups=Y_GROUPS)
        if level == 0:
            others, pack1, terms = lax.optimization_barrier((others, pack1, terms))
            full_other = gathered(others)
            got1 = lax.ppermute(pack1, EVERY, other_half())
        total = terms[0].astype(F32)
        for y in range(1, 4):
            total = total + terms[y].astype(F32)
        r = jnp.maximum(total, 0.0).astype(BF)
        r = exchange(jnp.broadcast_to(r[None], terms.shape), groups=Y_GROUPS)
        if level == 0:
            got1, pack2, r = lax.optimization_barrier((got1, pack2, r))
            sib1 = to_sibling(got1)
            got2 = lax.ppermute(pack2, EVERY, other_half())
            stacks = [(got0, sib0), (got1, sib1)]
        if level == 1:
            got2, r = lax.optimization_barrier((got2, r))
            stacks += [(got2, to_sibling(got2))] * 2
        if level < 3:
            h, terms = call(
                functools.partial(middle_kernel, level),
                (shape(ROWS[level + 1], 256, dtype=F32), shape(4, ROWS[level + 2], 256)),
                [*MIXING, *DILATED, pltpu.VMEM((ROWS[level + 1], 256), F32)],
                n=2,
                hbm=6,
                name="cond",
            )(info, r, h, mixing_weight, *stacks[level], dilated_weight, *stacks[level + 1])
        else:
            spread = call(
                last_kernel, shape(8, HALF, 256), MIXING, n=2, hbm=3, name="cond_end"
            )(info, r, h, mixing_weight, *stacks[level])
    hf = exchange(spread)

    mid = middle_codes.reshape(256, 4).T.reshape(1024)
    mid = (mid // 1024 * 1024 + mid % 256 // 16 * 64 + mid // 256 % 4 * 16 + mid % 16) ^ (
        x_hi * (1024 + 8 * 64)
    )
    gain = norm_gain[None]
    qkv = qkv_weight.reshape(D, 768)

    def from_two_back(value):
        return lax.ppermute(value, "song", [(i, i + 2) for i in range(14)])

    q0, kv0 = frames(0, info, mid, hf, gain, qkv, full_own, full_other)
    far0 = from_two_back(kv0)
    q1, kv1 = frames(1, info, mid, hf, gain, qkv, full_own, full_other)
    far1 = from_two_back(kv1)
    state = (shape(2, 4, 256, 256, dtype=F32), shape(2, 4, 256, 1, dtype=F32))
    keys = pltpu.VMEM((1024, 512), BF)
    far0, q1 = lax.optimization_barrier((far0, q1))
    kept = call(own_kernel, state, [keys], smem=0, n=4, flops=10**9, name="own")(q0, q1, kv0, kv1)
    near0 = to_sibling(jnp.where(core == 0, kv0, far0))
    kept = call(functools.partial(past_kernel, False), state, [keys], n=6, flops=10**9, name="past")(
        info, q0, q1, far0, near0, *kept
    )
    far1, kept = lax.optimization_barrier((far1, kept))
    near1 = to_sibling(jnp.where(core == 0, kv1, far1))
    return call(
        functools.partial(past_kernel, True),
        shape(1024, 256),
        [
            keys,
            pltpu.VMEM((2, 4, 256, 256), F32),
            pltpu.VMEM((2, 4, 256, 1), F32),
            pltpu.VMEM((1024, 128), F32),
        ],
        n=6,
        flops=2 * 10**9,
        name="past_end",
    )(info, q0, q1, far1, near1, *kept)


def solution(mesh):
    placed = (
        P("song"),
        P("song"),
        P(None, "tensor"),
        P(None, None, "tensor", None),
        P(None, None, "tensor"),
        P("tensor", None),
        P("tensor", None),
        P(),
        P(None, "tensor", None),
    )
    return jax.shard_map(
        on_device, mesh=mesh, in_specs=placed, out_specs=P("song", "tensor"), check_vma=False
    )
```

```python
import functools

import jax
import jax.numpy as jnp
from jax import lax
from jax.experimental import pallas as pl
from jax.experimental.pallas import tpu as pltpu
from jax.sharding import PartitionSpec as P

BF = jnp.bfloat16
F32 = jnp.float32
D = 1920
C = 1024
VOCAB = 2048
UPPER = 4096
HALF = 128
HALO = (40, 39, 36, 27, 0)
ROWS = (208, 208, 208, 192, 128)

BLOCKS = D // 128
UP_BLOCKS = 2 * BLOCKS
PART = UP_BLOCKS + 16

Y_GROUPS = [[0, 1, 2, 3], [4, 5, 6, 7]]


def params(mib):
    return pltpu.CompilerParams(vmem_limit_bytes=mib << 20)


def cost(flops, nbytes, trans=0):
    return pl.CostEstimate(flops=flops, bytes_accessed=nbytes, transcendentals=trans)


def dot(a, b):
    return jnp.dot(a, b, preferred_element_type=F32)


def dilated_copies(level, info, dil_hbm, got_hbm, sib_hbm, near_ref, away_ref, sems):
    own = pl.multiple_of(info[0] * 512, 512)
    other = pl.multiple_of((1 - info[0]) * 512, 512)
    pairs = []
    for ref, hbm, begin in ((near_ref, got_hbm, own), (away_ref, sib_hbm, other)):
        part = hbm if level < 2 else hbm.at[level - 2]
        pairs.append((dil_hbm.at[level, :, :, pl.ds(begin, 512)], ref.at[:, pl.ds(0, 128), :]))
        for tap in range(3):
            pairs.append((part.at[pl.ds(tap * 128, 128), :], ref.at[tap, pl.ds(128, 128), :]))
    return [pltpu.make_async_copy(a, b, sems.at[i]) for i, (a, b) in enumerate(pairs)]


def mixing_copies(level, info, mix_hbm, got_hbm, sib_hbm, mix_ref, sems):
    pairs = []
    for half, hbm in enumerate((got_hbm, sib_hbm)):
        part = hbm if level < 2 else hbm.at[level - 2]
        begin = info[0] if half == 0 else 1 - info[0]
        rows = pl.ds(pl.multiple_of(begin * 512, 512), 512)
        pairs.append((mix_hbm.at[level, rows, :], mix_ref.at[half, :, pl.ds(0, 128)]))
        for y in range(4):
            pairs.append(
                (
                    part.at[pl.ds(384, 128), pl.ds(y * 128, 128)],
                    mix_ref.at[half, pl.ds(y * 128, 128), pl.ds(128, 128)],
                )
            )
    return [pltpu.make_async_copy(a, b, sems.at[i]) for i, (a, b) in enumerate(pairs)]


def send_terms(level, info, h_ref, near_ref, away_ref, out_ref):
    step = 3**level
    count = HALF + 2 * HALO[level + 1]
    padded = out_ref.shape[1]
    rows = h_ref.shape[0]
    first = info[1] - HALO[level]
    pos = first + lax.broadcasted_iota(jnp.int32, (rows, 1), 0)
    inside = (pos >= 0) & (pos < UPPER)
    h_ref[...] = jnp.where(inside, jnp.maximum(h_ref[...], 0.0), 0.0)
    taps = [h_ref[tap * step : tap * step + count, :].astype(BF) for tap in range(3)]
    for half, ref in enumerate((near_ref, away_ref)):
        total = dot(taps[0], ref[0]) + dot(taps[1], ref[1]) + dot(taps[2], ref[2])
        total = total.astype(BF)
        for y in range(4):
            out_ref[y, :count, half * 128 : half * 128 + 128] = total[:, y * 128 : y * 128 + 128]
    if padded > count:
        for y in range(4):
            out_ref[y, count:, :] = jnp.zeros((padded - count, 256), BF)


def start(copies):
    for copy in copies:
        copy.start()


def finish(copies):
    for copy in copies:
        copy.wait()


DILATED = [pltpu.VMEM((3, 256, 512), BF), pltpu.VMEM((3, 256, 512), BF), pltpu.SemaphoreType.DMA((8,))]
MIXING = [pltpu.VMEM((2, 512, 256), BF), pltpu.SemaphoreType.DMA((10,))]


def first_kernel(info, codes_ref, table_ref, dil_hbm, got_ref, sib_ref, h_ref, out_ref, near_ref, away_ref, sems, work):
    copies = dilated_copies(0, info, dil_hbm, got_ref, sib_ref, near_ref, away_ref, sems)
    start(copies)
    codes = codes_ref[...]
    rows = codes.shape[0]
    lane = lax.broadcasted_iota(jnp.int32, (rows, 1024), 1)
    core = info[0]
    one = jnp.ones((), BF)
    zero = jnp.zeros((), BF)
    h_own = jnp.zeros((rows, 128), F32)
    h_oth = jnp.zeros((rows, 128), F32)
    for src, begin in ((got_ref, core * 1024), (sib_ref, (1 - core) * 1024)):
        hot = jnp.where(codes - begin == lane, one, zero)
        h_own += dot(hot, table_ref[pl.ds(pl.multiple_of(begin, 1024), 1024), :])
        for q in range(4):
            h_oth += dot(hot[:, q * 256 : q * 256 + 256], src[512:768, q * 128 : q * 128 + 128])
    work[:, :128] = h_own
    work[:, 128:] = h_oth
    h_ref[...] = work[...]
    finish(copies)
    send_terms(0, info, work, near_ref, away_ref, out_ref)


def mixed(level, r_ref, h_ref, mix_ref):
    step = 3**level
    count = HALF + 2 * HALO[level + 1]
    h = h_ref[step : step + count, :]
    for half in range(2):
        r = jnp.concatenate([r_ref[y, :, half * 128 : half * 128 + 128] for y in range(4)], axis=1)
        h += dot(r, mix_ref[half])[:count]
    return h


def middle_kernel(level, info, r_ref, h_ref, mix_hbm, got_hbm, sib_hbm, dil_hbm, got1_hbm, sib1_hbm, new_ref, out_ref, mix_ref, mix_sems, near_ref, away_ref, sems, work):
    first = mixing_copies(level, info, mix_hbm, got_hbm, sib_hbm, mix_ref, mix_sems)
    then = dilated_copies(level + 1, info, dil_hbm, got1_hbm, sib1_hbm, near_ref, away_ref, sems)
    start(first)
    start(then)
    finish(first)
    count = HALF + 2 * HALO[level + 1]
    if work.shape[0] > count:
        work[count:, :] = jnp.zeros((work.shape[0] - count, 256), F32)
    work[:count, :] = mixed(level, r_ref, h_ref, mix_ref)
    new_ref[...] = work[...]
    finish(then)
    send_terms(level + 1, info, work, near_ref, away_ref, out_ref)


def last_kernel(info, r_ref, h_ref, mix_hbm, got_hbm, sib_hbm, out_ref, mix_ref, mix_sems):
    copies = mixing_copies(3, info, mix_hbm, got_hbm, sib_hbm, mix_ref, mix_sems)
    start(copies)
    finish(copies)
    h = mixed(3, r_ref, h_ref, mix_ref).astype(BF)
    for peer in range(8):
        out_ref[peer] = h


def half_copies(info, level, dil_hbm, mix_hbm, dest):
    cols = pl.ds(pl.multiple_of(info[0] * 512, 512), 512)
    pairs = [(dil_hbm.at[level, tap, :, cols], dest.at[pl.ds(tap * 128, 128), :]) for tap in range(3)]
    for i in range(4):
        rows = pl.ds(pl.multiple_of(info[0] * 512 + i * 128, 128), 128)
        pairs.append((mix_hbm.at[level, rows, :], dest.at[pl.ds(384, 128), pl.ds(i * 128, 128)]))
    return pairs


def copies_of(pairs, sems):
    return [pltpu.make_async_copy(a, b, sems.at[i]) for i, (a, b) in enumerate(pairs)]


def pack_kernel(info, dil_hbm, mix_hbm, tab_hbm, up_hbm, mid_hbm, pack0, part_ref, up, mid, wide, sems):
    pairs = [
        (up_hbm.at[pl.ds(info[4] * 16, 16), pl.ds(pl.multiple_of(info[0] * 2 * D, 128), 2 * D)], up),
        (mid_hbm.at[pl.ds(info[5] * 16, 16), :], mid),
    ]
    pairs += half_copies(info, 0, dil_hbm, mix_hbm, pack0)
    for i in range(4):
        rows = pl.ds(pl.multiple_of(info[0] * 1024 + i * 256, 256), 256)
        pairs.append((tab_hbm.at[rows, :], pack0.at[pl.ds(512, 256), pl.ds(i * 128, 128)]))
    copies = copies_of(pairs, sems)
    start(copies)
    finish(copies[:2])
    wide[...] = jnp.zeros_like(wide)
    for block in range(BLOCKS):
        wide[:, block, :] = mid[:, block * 128 : block * 128 + 128].astype(F32)
    for y in range(4):
        for block in range(UP_BLOCKS):
            part_ref[y, block] = up[:, block * 128 : block * 128 + 128]
        part_ref[y, UP_BLOCKS:] = wide[...].astype(BF)
    finish(copies[2:])


def later_kernel(info, dil_hbm, mix_hbm, pack1, pack2, sems):
    pairs = half_copies(info, 1, dil_hbm, mix_hbm, pack1)
    for i in range(2):
        pairs += half_copies(info, 2 + i, dil_hbm, mix_hbm, pack2.at[i])
    copies = copies_of(pairs, sems)
    start(copies)
    finish(copies)


def call(body, outs, scratch=(), smem=1, n=0, hbm=0, after=0, flops=10**9, name=None, mib=12, space=pl.ANY):
    def spec(space):
        return pl.BlockSpec(memory_space=space)

    specs = [spec(pltpu.SMEM)] * smem + [spec(pltpu.VMEM)] * n
    specs += [spec(space)] * hbm + [spec(pltpu.VMEM)] * after
    return pl.pallas_call(
        body,
        out_shape=outs,
        in_specs=specs,
        out_specs=jax.tree.map(lambda _: spec(pltpu.VMEM), outs),
        scratch_shapes=list(scratch),
        compiler_params=params(mib),
        cost_estimate=cost(flops, 4 << 20),
        name=name,
    )


def shape(*dims, dtype=BF):
    return jax.ShapeDtypeStruct(dims, dtype)


CHUNKS = ((0, 4), (4, 4), (8, 4), (12, 3))


def frames_kernel(pair, info, codes_ref, hf_ref, gain_ref, qkv_hbm, own_hbm, other_hbm, q_ref, kv_ref, weights, table, qkv, hf, rows, x, xn, sems, table_sems, qkv_sem):
    def weight_copies(phase):
        return [
            pltpu.make_async_copy(
                full.at[pl.ds(part * 4 ^ info[3], 4), pair, y, pl.ds(phase * BLOCKS, BLOCKS)],
                weights.at[phase, half, y, pl.ds(part * 4, 4)],
                sems.at[phase, half, part, y],
            )
            for half, full in enumerate((own_hbm, other_hbm))
            for part in range(2)
            for y in range(4)
        ]

    def product(phase):
        for first, size in CHUNKS:
            w = [weights[phase, :, :, :, block].reshape(C, 128) for block in range(first, first + size)]
            x[phase, :, first * 128 : (first + size) * 128] = dot(hf[...], jnp.concatenate(w, axis=1))

    def norm(phase):
        total = jnp.zeros((256, 128), F32)
        for block in range(BLOCKS):
            cols = slice(block * 128, block * 128 + 128)
            y = x[phase, :, cols] + rows[pl.ds(phase * 256, 256), block, :]
            x[phase, :, cols] = y
            total += y
        mean = jnp.sum(total, axis=1, keepdims=True) * (1.0 / D)
        square = jnp.zeros((256, 128), F32)
        for block in range(BLOCKS):
            y = x[phase, :, block * 128 : block * 128 + 128] - mean
            square += y * y
        factor = lax.rsqrt(jnp.sum(square, axis=1, keepdims=True) * (1.0 / D) + 1e-5)
        for block in range(BLOCKS):
            cols = slice(block * 128, block * 128 + 128)
            xn[phase, :, cols] = ((x[phase, :, cols] - mean) * factor * gain_ref[:, cols]).astype(BF)

    def project(phase):
        y = dot(xn[phase], qkv[...]).astype(BF)
        lines = slice(phase * 256, phase * 256 + 256)
        for head in range(2):
            at = head * 384
            cols = slice(head * 128, head * 128 + 128)
            q_ref[lines, cols] = y[:, at : at + 128]
            kv_ref[lines, cols] = y[:, at + 128 : at + 256]
            kv_ref[lines, 256 + head * 128 : 384 + head * 128] = y[:, at + 256 : at + 384]

    table_copies = [
        pltpu.make_async_copy(
            full.at[:, part, :, pl.ds(UP_BLOCKS, 16)], table.at[half, :, part], table_sems.at[half, part]
        )
        for half, full in enumerate((own_hbm, other_hbm))
        for part in range(2)
    ]
    qkv_copy = pltpu.make_async_copy(qkv_hbm, qkv, qkv_sem)
    start(weight_copies(0))
    start(table_copies)
    start(weight_copies(1))
    qkv_copy.start()
    for rows_of in range(2):
        for half in range(2):
            at = pl.multiple_of(((info[3] // 4) ^ half ^ rows_of) * 128, 128)
            for y in range(4):
                j = half * 4 + y
                hf[rows_of * 128 : rows_of * 128 + 128, j * 128 : j * 128 + 128] = hf_ref[
                    rows_of * 4 + y, :, pl.ds(at, 128)
                ]
    flat = table.reshape(VOCAB, 16, 128)

    finish(weight_copies(0))
    product(0)
    finish(table_copies)

    def look_up(i, carry):
        for j in range(16):
            row = i * 16 + j
            rows[row] = flat[codes_ref[pair * 512 + row]].astype(F32)
        return carry

    lax.fori_loop(0, 32, look_up, 0)
    finish(weight_copies(1))
    qkv_copy.wait()
    norm(0)
    product(1)
    project(0)
    norm(1)
    project(1)


def frames(pair, info, codes, hf, gain, qkv, full_own, full_other):
    vm = pl.BlockSpec(memory_space=pltpu.VMEM)
    sm = pl.BlockSpec(memory_space=pltpu.SMEM)
    any_space = pl.BlockSpec(memory_space=pl.ANY)
    return pl.pallas_call(
        functools.partial(frames_kernel, pair),
        out_shape=(shape(512, 256), shape(512, 512)),
        in_specs=[sm, sm, vm, vm, any_space, any_space, any_space],
        out_specs=(vm, vm),
        scratch_shapes=[
            pltpu.VMEM((2, 2, 4, 8, BLOCKS, 16, 128), BF),
            pltpu.VMEM((2, 8, 2, 4, 16, 16, 128), BF),
            pltpu.VMEM((D, 768), BF),
            pltpu.VMEM((256, C), BF),
            pltpu.VMEM((512, 16, 128), F32),
            pltpu.VMEM((2, 256, D), F32),
            pltpu.VMEM((2, 256, D), BF),
            pltpu.SemaphoreType.DMA((2, 2, 2, 4)),
            pltpu.SemaphoreType.DMA((2, 2)),
            pltpu.SemaphoreType.DMA,
        ],
        compiler_params=params(40),
        cost_estimate=cost(4 * 10**9, 20 << 20),
        name="frames",
    )(info, codes, hf, gain, qkv, full_own, full_other)


SCALE = 128**-0.5 * 1.4426950408889634


def scores_of(q, k):
    return lax.dot_general(q, k, (((1,), (1,)), ((), ())), preferred_element_type=F32)


def fold(tiles, kv, old_of, put):
    for head in range(2):
        cols = slice(head * 128, head * 128 + 128)
        k = kv[:, cols]
        v = kv[:, 256 + head * 128 : 384 + head * 128]
        v = jnp.concatenate([v, jnp.ones(v.shape, BF)], axis=1)
        for tile, (queries, seen) in enumerate(tiles):
            s = jnp.where(seen, scores_of(queries[:, cols], k), -1e30)
            top = jnp.max(s, axis=1, keepdims=True)
            old = old_of(head, tile)
            if old is None:
                put(head, tile, top, dot(jnp.exp2((s - top) * SCALE).astype(BF), v))
            else:
                top = jnp.maximum(old[0], top)
                p = jnp.exp2((s - top) * SCALE).astype(BF)
                put(head, tile, top, old[1] * jnp.exp2((old[0] - top) * SCALE) + dot(p, v))


def phase_tiles(q0_ref, q1_ref, seen):
    return [(ref[at : at + 256], seen) for ref in (q0_ref, q1_ref) for at in (0, 256)]


def join_keys(kv, first, second):
    kv[:512] = first[...]
    kv[512:] = second[...]


def own_kernel(q0_ref, q1_ref, kv0_ref, kv1_ref, acc_ref, top_ref, kv):
    for part in range(2):
        keys = 128 * (part + 1)
        for phase, ref in enumerate((kv0_ref, kv0_ref, kv1_ref, kv1_ref)):
            kv[phase * keys : (phase + 1) * keys] = ref[phase % 2 * 256 : phase % 2 * 256 + keys]
        col = lax.broadcasted_iota(jnp.int32, (256, 4 * keys), 1)
        row = lax.broadcasted_iota(jnp.int32, (256, 4 * keys), 0)
        ahead = col % keys * 4 + col // keys - (part * 512 + row % 128 * 4 + row // 128)
        tiles = []
        for pair, ref in enumerate((q0_ref, q1_ref)):
            lines = slice(part * 128, part * 128 + 128), slice(256 + part * 128, 384 + part * 128)
            tiles.append((jnp.concatenate([ref[at, :] for at in lines]), ahead <= 2 * pair))

        def put(head, tile, top, acc):
            lines = slice(part * 128, part * 128 + 128)
            for i in range(2):
                top_ref[head, tile * 2 + i, lines] = top[i * 128 : i * 128 + 128]
                acc_ref[head, tile * 2 + i, lines] = acc[i * 128 : i * 128 + 128]

        fold(tiles, kv[: 4 * keys], lambda head, tile: None, put)


def past_kernel(last, info, q0_ref, q1_ref, far_ref, near_ref, acc_ref, top_ref, *refs):
    if last:
        out_ref, kv, acc, tops, wide = refs
    else:
        acc, tops, kv = refs
    song = info[2]

    @pl.when(song == 0)
    def _():
        acc[...] = acc_ref[...]
        tops[...] = top_ref[...]

    @pl.when(song > 0)
    def _():
        join_keys(kv, far_ref, near_ref)
        col = lax.broadcasted_iota(jnp.int32, (256, 1024), 1)
        seen = col >= jnp.where(song == 1, 512, 0)

        def put(head, phase, top, total):
            tops[head, phase] = top
            acc[head, phase] = total

        fold(
            phase_tiles(q0_ref, q1_ref, seen),
            kv[...],
            lambda head, phase: (top_ref[head, phase], acc_ref[head, phase]),
            put,
        )

    if last:
        for head in range(2):
            for phase in range(4):
                both = acc[head, phase]
                wide[pl.ds(phase, 256, stride=4), :] = both[:, :128] / both[:, 128:]
            out_ref[:, head * 128 : head * 128 + 128] = wide[...].astype(BF)


EVERY = ("song", "tensor")


def other_half():
    pairs = []
    for song in range(16):
        for rank in range(8):
            pairs.append((song * 8 + rank, (song ^ 8) * 8 + (rank ^ 4)))
    return pairs


def song_neighbours():
    first = [(song * 8 + rank, song * 8 + 8 + rank) for song in range(15) for rank in range(4)]
    second = [(song * 8 + 8 + rank, song * 8 + rank) for song in range(15) for rank in range(4, 8)]
    return first + second


def to_sibling(value):
    return lax.ppermute(value, "song", [(i, i ^ 1) for i in range(16)])


def exchange(value, axis="tensor", groups=None):
    return lax.all_to_all(value, axis, 0, 0, axis_index_groups=groups, tiled=True)


def gathered(parts):
    return lax.all_gather(parts, "song", axis=0, tiled=False).reshape(8, 2, 4, PART, 16, 128)


def on_device(
    upper_codes,
    middle_codes,
    upper_table,
    dilated_weight,
    mixing_weight,
    upsample_weight,
    middle_table,
    norm_gain,
    qkv_weight,
):
    song = lax.axis_index("song")
    rank = lax.axis_index("tensor")
    core = song % 2
    x_hi = rank // 4
    begin = song * 256 + x_hi * HALF
    share = song ^ (8 * x_hi)
    info = jnp.stack([core, begin, song, x_hi * 4, share // 2, share]).astype(jnp.int32)

    pack0, part = call(
        pack_kernel,
        (shape(768, 512), shape(4, PART, 16, 128)),
        [
            pltpu.VMEM((16, 2 * D), BF),
            pltpu.VMEM((16, D), BF),
            pltpu.VMEM((16, 16, 128), F32),
            pltpu.SemaphoreType.DMA((13,)),
        ],
        hbm=5,
        name="pack",
        space=pltpu.HBM,
    )(info, dilated_weight, mixing_weight, upper_table, upsample_weight, middle_table)
    got0 = lax.ppermute(pack0, EVERY, other_half())
    mine = exchange(part, groups=Y_GROUPS)
    edge = jnp.where(x_hi == 0, upper_codes[-40:], upper_codes[:40])
    edge = lax.ppermute(edge, EVERY, song_neighbours())
    mine, edge = lax.optimization_barrier((mine, edge))
    full_own = gathered(mine)
    mine, got0 = lax.optimization_barrier((mine, got0))
    others = lax.ppermute(mine, EVERY, other_half())
    sib0 = to_sibling(got0)
    codes = jnp.where(
        x_hi == 0,
        jnp.concatenate([edge, upper_codes[: HALF + 40]]),
        jnp.concatenate([upper_codes[HALF - 40 :], edge]),
    )[:, None]

    h, terms = call(
        first_kernel,
        (shape(ROWS[0], 256, dtype=F32), shape(4, ROWS[1], 256)),
        [*DILATED, pltpu.VMEM((ROWS[0], 256), F32)],
        n=2,
        hbm=1,
        after=2,
        name="cond0",
    )(info, codes, upper_table, dilated_weight, got0, sib0)
    pack1, pack2 = call(
        later_kernel,
        (shape(512, 512), shape(2, 512, 512)),
        [pltpu.SemaphoreType.DMA((21,))],
        hbm=2,
        name="pack_later",
        space=pltpu.HBM,
    )(info, dilated_weight, mixing_weight)

    for level in range(4):
        terms = exchange(terms, groups=Y_GROUPS)
        if level == 0:
            others, pack1, terms = lax.optimization_barrier((others, pack1, terms))
            full_other = gathered(others)
            got1 = lax.ppermute(pack1, EVERY, other_half())
        total = terms[0].astype(F32)
        for y in range(1, 4):
            total = total + terms[y].astype(F32)
        r = jnp.maximum(total, 0.0).astype(BF)
        r = exchange(jnp.broadcast_to(r[None], terms.shape), groups=Y_GROUPS)
        if level == 0:
            got1, pack2, r = lax.optimization_barrier((got1, pack2, r))
            sib1 = to_sibling(got1)
            got2 = lax.ppermute(pack2, EVERY, other_half())
            stacks = [(got0, sib0), (got1, sib1)]
        if level == 1:
            got2, r = lax.optimization_barrier((got2, r))
            stacks += [(got2, to_sibling(got2))] * 2
        if level < 3:
            h, terms = call(
                functools.partial(middle_kernel, level),
                (shape(ROWS[level + 1], 256, dtype=F32), shape(4, ROWS[level + 2], 256)),
                [*MIXING, *DILATED, pltpu.VMEM((ROWS[level + 1], 256), F32)],
                n=2,
                hbm=6,
                name="cond",
            )(info, r, h, mixing_weight, *stacks[level], dilated_weight, *stacks[level + 1])
        else:
            spread = call(
                last_kernel, shape(8, HALF, 256), MIXING, n=2, hbm=3, name="cond_end"
            )(info, r, h, mixing_weight, *stacks[level])
    hf = exchange(spread)

    mid = middle_codes.reshape(256, 4).T.reshape(1024)
    mid = (mid // 1024 * 1024 + mid % 256 // 16 * 64 + mid // 256 % 4 * 16 + mid % 16) ^ (
        x_hi * (1024 + 8 * 64)
    )
    gain = norm_gain[None]
    qkv = qkv_weight.reshape(D, 768)

    def from_two_back(value):
        return lax.ppermute(value, "song", [(i, i + 2) for i in range(14)])

    q0, kv0 = frames(0, info, mid, hf, gain, qkv, full_own, full_other)
    far0 = from_two_back(kv0)
    q1, kv1 = frames(1, info, mid, hf, gain, qkv, full_own, full_other)
    far1 = from_two_back(kv1)
    state = (shape(2, 4, 256, 256, dtype=F32), shape(2, 4, 256, 1, dtype=F32))
    keys = pltpu.VMEM((1024, 512), BF)
    far0, q1 = lax.optimization_barrier((far0, q1))
    kept = call(own_kernel, state, [keys], smem=0, n=4, flops=10**9, name="own", mib=24)(q0, q1, kv0, kv1)
    near0 = to_sibling(jnp.where(core == 0, kv0, far0))
    kept = call(functools.partial(past_kernel, False), state, [keys], n=6, flops=10**9, name="past", mib=24)(
        info, q0, q1, far0, near0, *kept
    )
    far1, kept = lax.optimization_barrier((far1, kept))
    near1 = to_sibling(jnp.where(core == 0, kv1, far1))
    return call(
        functools.partial(past_kernel, True),
        shape(1024, 256),
        [
            keys,
            pltpu.VMEM((2, 4, 256, 256), F32),
            pltpu.VMEM((2, 4, 256, 1), F32),
            pltpu.VMEM((1024, 128), F32),
        ],
        n=6,
        flops=2 * 10**9,
        name="past_end",
        mib=24,
    )(info, q0, q1, far1, near1, *kept)


def solution(mesh):
    placed = (
        P("song"),
        P("song"),
        P(None, "tensor"),
        P(None, None, "tensor", None),
        P(None, None, "tensor"),
        P("tensor", None),
        P("tensor", None),
        P(),
        P(None, "tensor", None),
    )
    return jax.shard_map(
        on_device, mesh=mesh, in_specs=placed, out_specs=P("song", "tensor"), check_vma=False
    )
```

```python
import functools

import jax
import jax.numpy as jnp
from jax import lax
from jax.experimental import pallas as pl
from jax.experimental.pallas import tpu as pltpu
from jax.sharding import PartitionSpec as P

BF = jnp.bfloat16
F32 = jnp.float32
D = 1920
C = 1024
VOCAB = 2048
UPPER = 4096
HALF = 128
HALO = (40, 39, 36, 27, 0)
ROWS = (208, 208, 208, 192, 128)

BLOCKS = D // 128
UP_BLOCKS = 2 * BLOCKS
PART = UP_BLOCKS + 16

Y_GROUPS = [[0, 1, 2, 3], [4, 5, 6, 7]]


def params(mib):
    return pltpu.CompilerParams(vmem_limit_bytes=mib << 20)


def cost(flops, nbytes, trans=0):
    return pl.CostEstimate(flops=flops, bytes_accessed=nbytes, transcendentals=trans)


def dot(a, b):
    return jnp.dot(a, b, preferred_element_type=F32)


def dilated_copies(level, info, dil_hbm, got_hbm, sib_hbm, near_ref, away_ref, sems):
    own = pl.multiple_of(info[0] * 512, 512)
    other = pl.multiple_of((1 - info[0]) * 512, 512)
    pairs = []
    for ref, hbm, begin in ((near_ref, got_hbm, own), (away_ref, sib_hbm, other)):
        part = hbm if level < 2 else hbm.at[level - 2]
        pairs.append((dil_hbm.at[level, :, :, pl.ds(begin, 512)], ref.at[:, pl.ds(0, 128), :]))
        for tap in range(3):
            pairs.append((part.at[pl.ds(tap * 128, 128), :], ref.at[tap, pl.ds(128, 128), :]))
    return [pltpu.make_async_copy(a, b, sems.at[i]) for i, (a, b) in enumerate(pairs)]


def mixing_copies(level, info, mix_hbm, got_hbm, sib_hbm, mix_ref, sems):
    pairs = []
    for half, hbm in enumerate((got_hbm, sib_hbm)):
        part = hbm if level < 2 else hbm.at[level - 2]
        begin = info[0] if half == 0 else 1 - info[0]
        rows = pl.ds(pl.multiple_of(begin * 512, 512), 512)
        pairs.append((mix_hbm.at[level, rows, :], mix_ref.at[half, :, pl.ds(0, 128)]))
        for y in range(4):
            pairs.append(
                (
                    part.at[pl.ds(384, 128), pl.ds(y * 128, 128)],
                    mix_ref.at[half, pl.ds(y * 128, 128), pl.ds(128, 128)],
                )
            )
    return [pltpu.make_async_copy(a, b, sems.at[i]) for i, (a, b) in enumerate(pairs)]


def send_terms(level, info, h_ref, near_ref, away_ref, out_ref):
    step = 3**level
    count = HALF + 2 * HALO[level + 1]
    padded = out_ref.shape[1]
    rows = h_ref.shape[0]
    first = info[1] - HALO[level]
    pos = first + lax.broadcasted_iota(jnp.int32, (rows, 1), 0)
    inside = (pos >= 0) & (pos < UPPER)
    h_ref[...] = jnp.where(inside, jnp.maximum(h_ref[...], 0.0), 0.0)
    taps = [h_ref[tap * step : tap * step + count, :].astype(BF) for tap in range(3)]
    for half, ref in enumerate((near_ref, away_ref)):
        total = dot(taps[0], ref[0]) + dot(taps[1], ref[1]) + dot(taps[2], ref[2])
        total = total.astype(BF)
        for y in range(4):
            out_ref[y, :count, half * 128 : half * 128 + 128] = total[:, y * 128 : y * 128 + 128]
    if padded > count:
        for y in range(4):
            out_ref[y, count:, :] = jnp.zeros((padded - count, 256), BF)


def start(copies):
    for copy in copies:
        copy.start()


def finish(copies):
    for copy in copies:
        copy.wait()


DILATED = [pltpu.VMEM((3, 256, 512), BF), pltpu.VMEM((3, 256, 512), BF), pltpu.SemaphoreType.DMA((8,))]
MIXING = [pltpu.VMEM((2, 512, 256), BF), pltpu.SemaphoreType.DMA((10,))]


def first_kernel(info, codes_ref, table_ref, dil_hbm, got_ref, sib_ref, h_ref, out_ref, near_ref, away_ref, sems, work):
    copies = dilated_copies(0, info, dil_hbm, got_ref, sib_ref, near_ref, away_ref, sems)
    start(copies)
    codes = codes_ref[...]
    rows = codes.shape[0]
    lane = lax.broadcasted_iota(jnp.int32, (rows, 1024), 1)
    core = info[0]
    one = jnp.ones((), BF)
    zero = jnp.zeros((), BF)
    h_own = jnp.zeros((rows, 128), F32)
    h_oth = jnp.zeros((rows, 128), F32)
    for src, begin in ((got_ref, core * 1024), (sib_ref, (1 - core) * 1024)):
        hot = jnp.where(codes - begin == lane, one, zero)
        h_own += dot(hot, table_ref[pl.ds(pl.multiple_of(begin, 1024), 1024), :])
        for q in range(4):
            h_oth += dot(hot[:, q * 256 : q * 256 + 256], src[512:768, q * 128 : q * 128 + 128])
    work[:, :128] = h_own
    work[:, 128:] = h_oth
    h_ref[...] = work[...]
    finish(copies)
    send_terms(0, info, work, near_ref, away_ref, out_ref)


def mixed(level, r_ref, h_ref, mix_ref):
    step = 3**level
    count = HALF + 2 * HALO[level + 1]
    h = h_ref[step : step + count, :]
    for half in range(2):
        r = jnp.concatenate([r_ref[y, :, half * 128 : half * 128 + 128] for y in range(4)], axis=1)
        h += dot(r, mix_ref[half])[:count]
    return h


def middle_kernel(level, info, r_ref, h_ref, mix_hbm, got_hbm, sib_hbm, dil_hbm, got1_hbm, sib1_hbm, new_ref, out_ref, mix_ref, mix_sems, near_ref, away_ref, sems, work):
    first = mixing_copies(level, info, mix_hbm, got_hbm, sib_hbm, mix_ref, mix_sems)
    then = dilated_copies(level + 1, info, dil_hbm, got1_hbm, sib1_hbm, near_ref, away_ref, sems)
    start(first)
    start(then)
    finish(first)
    count = HALF + 2 * HALO[level + 1]
    if work.shape[0] > count:
        work[count:, :] = jnp.zeros((work.shape[0] - count, 256), F32)
    work[:count, :] = mixed(level, r_ref, h_ref, mix_ref)
    new_ref[...] = work[...]
    finish(then)
    send_terms(level + 1, info, work, near_ref, away_ref, out_ref)


def last_kernel(info, r_ref, h_ref, mix_hbm, got_hbm, sib_hbm, out_ref, mix_ref, mix_sems):
    copies = mixing_copies(3, info, mix_hbm, got_hbm, sib_hbm, mix_ref, mix_sems)
    start(copies)
    finish(copies)
    h = mixed(3, r_ref, h_ref, mix_ref).astype(BF)
    for peer in range(8):
        out_ref[peer] = h


def half_copies(info, level, dil_hbm, mix_hbm, dest):
    cols = pl.ds(pl.multiple_of(info[0] * 512, 512), 512)
    pairs = [(dil_hbm.at[level, tap, :, cols], dest.at[pl.ds(tap * 128, 128), :]) for tap in range(3)]
    for i in range(4):
        rows = pl.ds(pl.multiple_of(info[0] * 512 + i * 128, 128), 128)
        pairs.append((mix_hbm.at[level, rows, :], dest.at[pl.ds(384, 128), pl.ds(i * 128, 128)]))
    return pairs


def copies_of(pairs, sems):
    return [pltpu.make_async_copy(a, b, sems.at[i]) for i, (a, b) in enumerate(pairs)]


def pack_kernel(info, dil_hbm, mix_hbm, tab_hbm, up_hbm, mid_hbm, pack0, part_ref, up, mid, wide, sems):
    pairs = [
        (up_hbm.at[pl.ds(info[4] * 16, 16), pl.ds(pl.multiple_of(info[0] * 2 * D, 128), 2 * D)], up),
        (mid_hbm.at[pl.ds(info[5] * 16, 16), :], mid),
    ]
    pairs += half_copies(info, 0, dil_hbm, mix_hbm, pack0)
    for i in range(4):
        rows = pl.ds(pl.multiple_of(info[0] * 1024 + i * 256, 256), 256)
        pairs.append((tab_hbm.at[rows, :], pack0.at[pl.ds(512, 256), pl.ds(i * 128, 128)]))
    copies = copies_of(pairs, sems)
    start(copies)
    finish(copies[:2])
    wide[...] = jnp.zeros_like(wide)
    for block in range(BLOCKS):
        wide[:, block, :] = mid[:, block * 128 : block * 128 + 128].astype(F32)
    for y in range(4):
        for block in range(UP_BLOCKS):
            part_ref[y, block] = up[:, block * 128 : block * 128 + 128]
        part_ref[y, UP_BLOCKS:] = wide[...].astype(BF)
    finish(copies[2:])


def later_kernel(info, dil_hbm, mix_hbm, pack1, pack2, sems):
    pairs = half_copies(info, 1, dil_hbm, mix_hbm, pack1)
    for i in range(2):
        pairs += half_copies(info, 2 + i, dil_hbm, mix_hbm, pack2.at[i])
    copies = copies_of(pairs, sems)
    start(copies)
    finish(copies)


def call(body, outs, scratch=(), smem=1, n=0, hbm=0, after=0, flops=10**9, name=None, mib=12):
    def spec(space):
        return pl.BlockSpec(memory_space=space)

    specs = [spec(pltpu.SMEM)] * smem + [spec(pltpu.VMEM)] * n
    specs += [spec(pl.ANY)] * hbm + [spec(pltpu.VMEM)] * after
    return pl.pallas_call(
        body,
        out_shape=outs,
        in_specs=specs,
        out_specs=jax.tree.map(lambda _: spec(pltpu.VMEM), outs),
        scratch_shapes=list(scratch),
        compiler_params=params(mib),
        cost_estimate=cost(flops, 4 << 20),
        name=name,
    )


def shape(*dims, dtype=BF):
    return jax.ShapeDtypeStruct(dims, dtype)


CHUNKS = ((0, 4), (4, 4), (8, 4), (12, 3))


def frames_kernel(pair, info, codes_ref, hf_ref, gain_ref, qkv_hbm, own_hbm, other_hbm, q_ref, kv_ref, weights, table, qkv, hf, rows, x, xn, sems, table_sems, qkv_sem):
    def weight_copies(phase):
        return [
            pltpu.make_async_copy(
                full.at[pl.ds(part * 4 ^ info[3], 4), pair, y, pl.ds(phase * BLOCKS, BLOCKS)],
                weights.at[phase, half, y, pl.ds(part * 4, 4)],
                sems.at[phase, half, part, y],
            )
            for half, full in enumerate((own_hbm, other_hbm))
            for part in range(2)
            for y in range(4)
        ]

    def product(phase):
        for first, size in CHUNKS:
            w = [weights[phase, :, :, :, block].reshape(C, 128) for block in range(first, first + size)]
            x[phase, :, first * 128 : (first + size) * 128] = dot(hf[...], jnp.concatenate(w, axis=1))

    def norm(phase):
        total = jnp.zeros((256, 128), F32)
        for block in range(BLOCKS):
            cols = slice(block * 128, block * 128 + 128)
            y = x[phase, :, cols] + rows[pl.ds(phase * 256, 256), block, :]
            x[phase, :, cols] = y
            total += y
        mean = jnp.sum(total, axis=1, keepdims=True) * (1.0 / D)
        square = jnp.zeros((256, 128), F32)
        for block in range(BLOCKS):
            y = x[phase, :, block * 128 : block * 128 + 128] - mean
            square += y * y
        factor = lax.rsqrt(jnp.sum(square, axis=1, keepdims=True) * (1.0 / D) + 1e-5)
        for block in range(BLOCKS):
            cols = slice(block * 128, block * 128 + 128)
            xn[phase, :, cols] = ((x[phase, :, cols] - mean) * factor * gain_ref[:, cols]).astype(BF)

    def project(phase):
        y = dot(xn[phase], qkv[...]).astype(BF)
        lines = slice(phase * 256, phase * 256 + 256)
        for head in range(2):
            at = head * 384
            cols = slice(head * 128, head * 128 + 128)
            q_ref[lines, cols] = y[:, at : at + 128]
            kv_ref[lines, cols] = y[:, at + 128 : at + 256]
            kv_ref[lines, 256 + head * 128 : 384 + head * 128] = y[:, at + 256 : at + 384]

    table_copies = [
        pltpu.make_async_copy(
            full.at[:, part, :, pl.ds(UP_BLOCKS, 16)], table.at[half, :, part], table_sems.at[half, part]
        )
        for half, full in enumerate((own_hbm, other_hbm))
        for part in range(2)
    ]
    qkv_copy = pltpu.make_async_copy(qkv_hbm, qkv, qkv_sem)
    start(weight_copies(0))
    start(table_copies)
    start(weight_copies(1))
    qkv_copy.start()
    for rows_of in range(2):
        for half in range(2):
            at = pl.multiple_of(((info[3] // 4) ^ half ^ rows_of) * 128, 128)
            for y in range(4):
                j = half * 4 + y
                hf[rows_of * 128 : rows_of * 128 + 128, j * 128 : j * 128 + 128] = hf_ref[
                    rows_of * 4 + y, :, pl.ds(at, 128)
                ]
    flat = table.reshape(VOCAB, 16, 128)

    finish(weight_copies(0))
    product(0)
    finish(table_copies)

    def look_up(i, carry):
        for j in range(16):
            row = i * 16 + j
            rows[row] = flat[codes_ref[pair * 512 + row]].astype(F32)
        return carry

    lax.fori_loop(0, 32, look_up, 0)
    finish(weight_copies(1))
    qkv_copy.wait()
    norm(0)
    product(1)
    project(0)
    norm(1)
    project(1)


def frames(pair, info, codes, hf, gain, qkv, full_own, full_other):
    vm = pl.BlockSpec(memory_space=pltpu.VMEM)
    sm = pl.BlockSpec(memory_space=pltpu.SMEM)
    any_space = pl.BlockSpec(memory_space=pl.ANY)
    return pl.pallas_call(
        functools.partial(frames_kernel, pair),
        out_shape=(shape(512, 256), shape(512, 512)),
        in_specs=[sm, sm, vm, vm, any_space, any_space, any_space],
        out_specs=(vm, vm),
        scratch_shapes=[
            pltpu.VMEM((2, 2, 4, 8, BLOCKS, 16, 128), BF),
            pltpu.VMEM((2, 8, 2, 4, 16, 16, 128), BF),
            pltpu.VMEM((D, 768), BF),
            pltpu.VMEM((256, C), BF),
            pltpu.VMEM((512, 16, 128), F32),
            pltpu.VMEM((2, 256, D), F32),
            pltpu.VMEM((2, 256, D), BF),
            pltpu.SemaphoreType.DMA((2, 2, 2, 4)),
            pltpu.SemaphoreType.DMA((2, 2)),
            pltpu.SemaphoreType.DMA,
        ],
        compiler_params=params(40),
        cost_estimate=cost(4 * 10**9, 20 << 20),
        name="frames",
    )(info, codes, hf, gain, qkv, full_own, full_other)


SCALE = 128**-0.5 * 1.4426950408889634


def scores_of(q, k):
    return lax.dot_general(q, k, (((1,), (1,)), ((), ())), preferred_element_type=F32)


def fold(tiles, kv, old_of, put):
    for head in range(2):
        cols = slice(head * 128, head * 128 + 128)
        k = kv[:, cols]
        v = kv[:, 256 + head * 128 : 384 + head * 128]
        v = jnp.concatenate([v, jnp.ones(v.shape, BF)], axis=1)
        for tile, (queries, seen) in enumerate(tiles):
            s = jnp.where(seen, scores_of(queries[:, cols], k), -1e30)
            top = jnp.max(s, axis=1, keepdims=True)
            old = old_of(head, tile)
            if old is None:
                put(head, tile, top, dot(jnp.exp2((s - top) * SCALE).astype(BF), v))
            else:
                top = jnp.maximum(old[0], top)
                p = jnp.exp2((s - top) * SCALE).astype(BF)
                put(head, tile, top, old[1] * jnp.exp2((old[0] - top) * SCALE) + dot(p, v))


def phase_tiles(q0_ref, q1_ref, seen):
    return [(ref[at : at + 256], seen) for ref in (q0_ref, q1_ref) for at in (0, 256)]


def join_keys(kv, first, second):
    kv[:512] = first[...]
    kv[512:] = second[...]


def own_kernel(q0_ref, q1_ref, kv0_ref, kv1_ref, acc_ref, top_ref, kv):
    for part in range(2):
        keys = 128 * (part + 1)
        for phase, ref in enumerate((kv0_ref, kv0_ref, kv1_ref, kv1_ref)):
            kv[phase * keys : (phase + 1) * keys] = ref[phase % 2 * 256 : phase % 2 * 256 + keys]
        col = lax.broadcasted_iota(jnp.int32, (256, 4 * keys), 1)
        row = lax.broadcasted_iota(jnp.int32, (256, 4 * keys), 0)
        ahead = col % keys * 4 + col // keys - (part * 512 + row % 128 * 4 + row // 128)
        tiles = []
        for pair, ref in enumerate((q0_ref, q1_ref)):
            lines = slice(part * 128, part * 128 + 128), slice(256 + part * 128, 384 + part * 128)
            tiles.append((jnp.concatenate([ref[at, :] for at in lines]), ahead <= 2 * pair))

        def put(head, tile, top, acc):
            lines = slice(part * 128, part * 128 + 128)
            for i in range(2):
                top_ref[head, tile * 2 + i, lines] = top[i * 128 : i * 128 + 128]
                acc_ref[head, tile * 2 + i, lines] = acc[i * 128 : i * 128 + 128]

        fold(tiles, kv[: 4 * keys], lambda head, tile: None, put)


def past_kernel(last, info, q0_ref, q1_ref, far_ref, near_ref, acc_ref, top_ref, *refs):
    if last:
        out_ref, kv, acc, tops, wide = refs
    else:
        acc, tops, kv = refs
    song = info[2]

    @pl.when(song == 0)
    def _():
        acc[...] = acc_ref[...]
        tops[...] = top_ref[...]

    @pl.when(song > 0)
    def _():
        join_keys(kv, far_ref, near_ref)
        col = lax.broadcasted_iota(jnp.int32, (256, 1024), 1)
        seen = col >= jnp.where(song == 1, 512, 0)

        def put(head, phase, top, total):
            tops[head, phase] = top
            acc[head, phase] = total

        fold(
            phase_tiles(q0_ref, q1_ref, seen),
            kv[...],
            lambda head, phase: (top_ref[head, phase], acc_ref[head, phase]),
            put,
        )

    if last:
        for head in range(2):
            for phase in range(4):
                both = acc[head, phase]
                wide[pl.ds(phase, 256, stride=4), :] = both[:, :128] / both[:, 128:]
            out_ref[:, head * 128 : head * 128 + 128] = wide[...].astype(BF)


EVERY = ("song", "tensor")


def other_half():
    pairs = []
    for song in range(16):
        for rank in range(8):
            pairs.append((song * 8 + rank, (song ^ 8) * 8 + (rank ^ 4)))
    return pairs


def song_neighbours():
    first = [(song * 8 + rank, song * 8 + 8 + rank) for song in range(15) for rank in range(4)]
    second = [(song * 8 + 8 + rank, song * 8 + rank) for song in range(15) for rank in range(4, 8)]
    return first + second


def to_sibling(value):
    return lax.ppermute(value, "song", [(i, i ^ 1) for i in range(16)])


def exchange(value, axis="tensor", groups=None):
    return lax.all_to_all(value, axis, 0, 0, axis_index_groups=groups, tiled=True)


def gathered(parts):
    return lax.all_gather(parts, "song", axis=0, tiled=False).reshape(8, 2, 4, PART, 16, 128)


def on_device(
    upper_codes,
    middle_codes,
    upper_table,
    dilated_weight,
    mixing_weight,
    upsample_weight,
    middle_table,
    norm_gain,
    qkv_weight,
):
    song = lax.axis_index("song")
    rank = lax.axis_index("tensor")
    core = song % 2
    x_hi = rank // 4
    begin = song * 256 + x_hi * HALF
    share = song ^ (8 * x_hi)
    dilated_weight = pltpu.with_memory_space_constraint(dilated_weight, pltpu.HBM)
    mixing_weight = pltpu.with_memory_space_constraint(mixing_weight, pltpu.HBM)
    info = jnp.stack([core, begin, song, x_hi * 4, share // 2, share]).astype(jnp.int32)

    pack0, part = call(
        pack_kernel,
        (shape(768, 512), shape(4, PART, 16, 128)),
        [
            pltpu.VMEM((16, 2 * D), BF),
            pltpu.VMEM((16, D), BF),
            pltpu.VMEM((16, 16, 128), F32),
            pltpu.SemaphoreType.DMA((13,)),
        ],
        hbm=5,
        name="pack",
        mib=60,
    )(info, dilated_weight, mixing_weight, upper_table, upsample_weight, middle_table)
    got0 = lax.ppermute(pack0, EVERY, other_half())
    mine = exchange(part, groups=Y_GROUPS)
    edge = jnp.where(x_hi == 0, upper_codes[-40:], upper_codes[:40])
    edge = lax.ppermute(edge, EVERY, song_neighbours())
    pack1, pack2 = call(
        later_kernel,
        (shape(512, 512), shape(2, 512, 512)),
        [pltpu.SemaphoreType.DMA((21,))],
        hbm=2,
        name="pack_later",
        mib=60,
    )(info, dilated_weight, mixing_weight)
    mine, got0, edge, pack1, pack2 = lax.optimization_barrier((mine, got0, edge, pack1, pack2))
    full_own = gathered(mine)
    others = lax.ppermute(mine, EVERY, other_half())
    sib0 = to_sibling(got0)
    codes = jnp.where(
        x_hi == 0,
        jnp.concatenate([edge, upper_codes[: HALF + 40]]),
        jnp.concatenate([upper_codes[HALF - 40 :], edge]),
    )[:, None]

    h, terms = call(
        first_kernel,
        (shape(ROWS[0], 256, dtype=F32), shape(4, ROWS[1], 256)),
        [*DILATED, pltpu.VMEM((ROWS[0], 256), F32)],
        n=2,
        hbm=1,
        after=2,
        name="cond0",
    )(info, codes, upper_table, dilated_weight, got0, sib0)
    for level in range(4):
        terms = exchange(terms, groups=Y_GROUPS)
        if level == 0:
            others, pack1, terms = lax.optimization_barrier((others, pack1, terms))
            full_other = gathered(others)
            got1 = lax.ppermute(pack1, EVERY, other_half())
        total = terms[0].astype(F32)
        for y in range(1, 4):
            total = total + terms[y].astype(F32)
        r = jnp.maximum(total, 0.0).astype(BF)
        r = exchange(jnp.broadcast_to(r[None], terms.shape), groups=Y_GROUPS)
        if level == 0:
            got1, pack2, r = lax.optimization_barrier((got1, pack2, r))
            sib1 = to_sibling(got1)
            got2 = lax.ppermute(pack2, EVERY, other_half())
            stacks = [(got0, sib0), (got1, sib1)]
        if level == 1:
            got2, r = lax.optimization_barrier((got2, r))
            stacks += [(got2, to_sibling(got2))] * 2
        if level < 3:
            h, terms = call(
                functools.partial(middle_kernel, level),
                (shape(ROWS[level + 1], 256, dtype=F32), shape(4, ROWS[level + 2], 256)),
                [*MIXING, *DILATED, pltpu.VMEM((ROWS[level + 1], 256), F32)],
                n=2,
                hbm=6,
                name="cond",
            )(info, r, h, mixing_weight, *stacks[level], dilated_weight, *stacks[level + 1])
        else:
            spread = call(
                last_kernel, shape(8, HALF, 256), MIXING, n=2, hbm=3, name="cond_end"
            )(info, r, h, mixing_weight, *stacks[level])
    hf = exchange(spread)

    mid = middle_codes.reshape(256, 4).T.reshape(1024)
    mid = (mid // 1024 * 1024 + mid % 256 // 16 * 64 + mid // 256 % 4 * 16 + mid % 16) ^ (
        x_hi * (1024 + 8 * 64)
    )
    gain = norm_gain[None]
    qkv = qkv_weight.reshape(D, 768)

    def from_two_back(value):
        return lax.ppermute(value, "song", [(i, i + 2) for i in range(14)])

    q0, kv0 = frames(0, info, mid, hf, gain, qkv, full_own, full_other)
    far0 = from_two_back(kv0)
    q1, kv1 = frames(1, info, mid, hf, gain, qkv, full_own, full_other)
    far1 = from_two_back(kv1)
    state = (shape(2, 4, 256, 256, dtype=F32), shape(2, 4, 256, 1, dtype=F32))
    keys = pltpu.VMEM((1024, 512), BF)
    far0, q1 = lax.optimization_barrier((far0, q1))
    kept = call(own_kernel, state, [keys], smem=0, n=4, flops=10**9, name="own", mib=24)(q0, q1, kv0, kv1)
    near0 = to_sibling(jnp.where(core == 0, kv0, far0))
    kept = call(functools.partial(past_kernel, False), state, [keys], n=6, flops=10**9, name="past", mib=24)(
        info, q0, q1, far0, near0, *kept
    )
    far1, kept = lax.optimization_barrier((far1, kept))
    near1 = to_sibling(jnp.where(core == 0, kv1, far1))
    return call(
        functools.partial(past_kernel, True),
        shape(1024, 256),
        [
            keys,
            pltpu.VMEM((2, 4, 256, 256), F32),
            pltpu.VMEM((2, 4, 256, 1), F32),
            pltpu.VMEM((1024, 128), F32),
        ],
        n=6,
        flops=2 * 10**9,
        name="past_end",
        mib=24,
    )(info, q0, q1, far1, near1, *kept)


def solution(mesh):
    placed = (
        P("song"),
        P("song"),
        P(None, "tensor"),
        P(None, None, "tensor", None),
        P(None, None, "tensor"),
        P("tensor", None),
        P("tensor", None),
        P(),
        P(None, "tensor", None),
    )
    return jax.shard_map(
        on_device, mesh=mesh, in_specs=placed, out_specs=P("song", "tensor"), check_vma=False
    )
```

```python
import functools

import jax
import jax.numpy as jnp
from jax import lax
from jax.experimental import pallas as pl
from jax.experimental.pallas import tpu as pltpu
from jax.sharding import PartitionSpec as P

BF = jnp.bfloat16
F32 = jnp.float32
D = 1920
C = 1024
VOCAB = 2048
UPPER = 4096
HALF = 128
HALO = (40, 39, 36, 27, 0)
ROWS = (208, 208, 208, 192, 128)

BLOCKS = D // 128
UP_BLOCKS = 2 * BLOCKS
PART = UP_BLOCKS + 16

Y_GROUPS = [[0, 1, 2, 3], [4, 5, 6, 7]]


def params(mib):
    return pltpu.CompilerParams(vmem_limit_bytes=mib << 20)


def cost(flops, nbytes, trans=0):
    return pl.CostEstimate(flops=flops, bytes_accessed=nbytes, transcendentals=trans)


def dot(a, b):
    return jnp.dot(a, b, preferred_element_type=F32)


def dilated_copies(level, info, dil_hbm, got_hbm, sib_hbm, near_ref, away_ref, sems):
    own = pl.multiple_of(info[0] * 512, 512)
    other = pl.multiple_of((1 - info[0]) * 512, 512)
    pairs = []
    for ref, hbm, begin in ((near_ref, got_hbm, own), (away_ref, sib_hbm, other)):
        part = hbm if level < 2 else hbm.at[level - 2]
        pairs.append((dil_hbm.at[level, :, :, pl.ds(begin, 512)], ref.at[:, pl.ds(0, 128), :]))
        for tap in range(3):
            pairs.append((part.at[pl.ds(tap * 128, 128), :], ref.at[tap, pl.ds(128, 128), :]))
    return [pltpu.make_async_copy(a, b, sems.at[i]) for i, (a, b) in enumerate(pairs)]


def mixing_copies(level, info, mix_hbm, got_hbm, sib_hbm, mix_ref, sems):
    pairs = []
    for half, hbm in enumerate((got_hbm, sib_hbm)):
        part = hbm if level < 2 else hbm.at[level - 2]
        begin = info[0] if half == 0 else 1 - info[0]
        rows = pl.ds(pl.multiple_of(begin * 512, 512), 512)
        pairs.append((mix_hbm.at[level, rows, :], mix_ref.at[half, :, pl.ds(0, 128)]))
        for y in range(4):
            pairs.append(
                (
                    part.at[pl.ds(384, 128), pl.ds(y * 128, 128)],
                    mix_ref.at[half, pl.ds(y * 128, 128), pl.ds(128, 128)],
                )
            )
    return [pltpu.make_async_copy(a, b, sems.at[i]) for i, (a, b) in enumerate(pairs)]


def send_terms(level, info, h_ref, near_ref, away_ref, out_ref):
    step = 3**level
    count = HALF + 2 * HALO[level + 1]
    padded = out_ref.shape[1]
    rows = h_ref.shape[0]
    first = info[1] - HALO[level]
    pos = first + lax.broadcasted_iota(jnp.int32, (rows, 1), 0)
    inside = (pos >= 0) & (pos < UPPER)
    h_ref[...] = jnp.where(inside, jnp.maximum(h_ref[...], 0.0), 0.0)
    taps = [h_ref[tap * step : tap * step + count, :].astype(BF) for tap in range(3)]
    for half, ref in enumerate((near_ref, away_ref)):
        total = dot(taps[0], ref[0]) + dot(taps[1], ref[1]) + dot(taps[2], ref[2])
        total = total.astype(BF)
        for y in range(4):
            out_ref[y, :count, half * 128 : half * 128 + 128] = total[:, y * 128 : y * 128 + 128]
    if padded > count:
        for y in range(4):
            out_ref[y, count:, :] = jnp.zeros((padded - count, 256), BF)


def start(copies):
    for copy in copies:
        copy.start()


def finish(copies):
    for copy in copies:
        copy.wait()


DILATED = [pltpu.VMEM((3, 256, 512), BF), pltpu.VMEM((3, 256, 512), BF), pltpu.SemaphoreType.DMA((8,))]
MIXING = [pltpu.VMEM((2, 512, 256), BF), pltpu.SemaphoreType.DMA((10,))]


def first_kernel(info, codes_ref, table_ref, dil_hbm, got_ref, sib_ref, h_ref, out_ref, near_ref, away_ref, sems, work):
    copies = dilated_copies(0, info, dil_hbm, got_ref, sib_ref, near_ref, away_ref, sems)
    start(copies)
    codes = codes_ref[...]
    rows = codes.shape[0]
    lane = lax.broadcasted_iota(jnp.int32, (rows, 1024), 1)
    core = info[0]
    one = jnp.ones((), BF)
    zero = jnp.zeros((), BF)
    h_own = jnp.zeros((rows, 128), F32)
    h_oth = jnp.zeros((rows, 128), F32)
    for src, begin in ((got_ref, core * 1024), (sib_ref, (1 - core) * 1024)):
        hot = jnp.where(codes - begin == lane, one, zero)
        h_own += dot(hot, table_ref[pl.ds(pl.multiple_of(begin, 1024), 1024), :])
        for q in range(4):
            h_oth += dot(hot[:, q * 256 : q * 256 + 256], src[512:768, q * 128 : q * 128 + 128])
    work[:, :128] = h_own
    work[:, 128:] = h_oth
    h_ref[...] = work[...]
    finish(copies)
    send_terms(0, info, work, near_ref, away_ref, out_ref)


def mixed(level, r_ref, h_ref, mix_ref):
    step = 3**level
    count = HALF + 2 * HALO[level + 1]
    h = h_ref[step : step + count, :]
    for half in range(2):
        r = jnp.concatenate([r_ref[y, :, half * 128 : half * 128 + 128] for y in range(4)], axis=1)
        h += dot(r, mix_ref[half])[:count]
    return h


def middle_kernel(level, info, r_ref, h_ref, mix_hbm, got_hbm, sib_hbm, dil_hbm, got1_hbm, sib1_hbm, new_ref, out_ref, mix_ref, mix_sems, near_ref, away_ref, sems, work):
    first = mixing_copies(level, info, mix_hbm, got_hbm, sib_hbm, mix_ref, mix_sems)
    then = dilated_copies(level + 1, info, dil_hbm, got1_hbm, sib1_hbm, near_ref, away_ref, sems)
    start(first)
    start(then)
    finish(first)
    count = HALF + 2 * HALO[level + 1]
    if work.shape[0] > count:
        work[count:, :] = jnp.zeros((work.shape[0] - count, 256), F32)
    work[:count, :] = mixed(level, r_ref, h_ref, mix_ref)
    new_ref[...] = work[...]
    finish(then)
    send_terms(level + 1, info, work, near_ref, away_ref, out_ref)


def last_kernel(info, r_ref, h_ref, mix_hbm, got_hbm, sib_hbm, out_ref, mix_ref, mix_sems):
    copies = mixing_copies(3, info, mix_hbm, got_hbm, sib_hbm, mix_ref, mix_sems)
    start(copies)
    finish(copies)
    h = mixed(3, r_ref, h_ref, mix_ref).astype(BF)
    for peer in range(8):
        out_ref[peer] = h


def half_copies(info, level, dil_hbm, mix_hbm, dest):
    cols = pl.ds(pl.multiple_of(info[0] * 512, 512), 512)
    pairs = [(dil_hbm.at[level, tap, :, cols], dest.at[pl.ds(tap * 128, 128), :]) for tap in range(3)]
    for i in range(4):
        rows = pl.ds(pl.multiple_of(info[0] * 512 + i * 128, 128), 128)
        pairs.append((mix_hbm.at[level, rows, :], dest.at[pl.ds(384, 128), pl.ds(i * 128, 128)]))
    return pairs


def copies_of(pairs, sems):
    return [pltpu.make_async_copy(a, b, sems.at[i]) for i, (a, b) in enumerate(pairs)]


def share_kernel(info, up_hbm, mid_hbm, part_ref, up, mid, wide, sems):
    pairs = [
        (up_hbm.at[pl.ds(info[4] * 16, 16), pl.ds(pl.multiple_of(info[0] * 2 * D, 128), 2 * D)], up),
        (mid_hbm.at[pl.ds(info[5] * 16, 16), :], mid),
    ]
    copies = copies_of(pairs, sems)
    start(copies)
    wide[...] = jnp.zeros_like(wide)
    finish(copies)
    for block in range(BLOCKS):
        wide[:, block, :] = mid[:, block * 128 : block * 128 + 128].astype(F32)
    for y in range(4):
        for block in range(UP_BLOCKS):
            part_ref[y, block] = up[:, block * 128 : block * 128 + 128]
        part_ref[y, UP_BLOCKS:] = wide[...].astype(BF)


def pack_kernel(info, dil_hbm, mix_hbm, tab_hbm, pack0, pack1, pack2, sems):
    pairs = half_copies(info, 0, dil_hbm, mix_hbm, pack0) + half_copies(info, 1, dil_hbm, mix_hbm, pack1)
    for i in range(2):
        pairs += half_copies(info, 2 + i, dil_hbm, mix_hbm, pack2.at[i])
    for i in range(4):
        rows = pl.ds(pl.multiple_of(info[0] * 1024 + i * 256, 256), 256)
        pairs.append((tab_hbm.at[rows, :], pack0.at[pl.ds(512, 256), pl.ds(i * 128, 128)]))
    copies = copies_of(pairs, sems)
    start(copies)
    finish(copies)


def call(body, outs, scratch=(), smem=1, n=0, hbm=0, after=0, flops=10**9, name=None, mib=12):
    def spec(space):
        return pl.BlockSpec(memory_space=space)

    specs = [spec(pltpu.SMEM)] * smem + [spec(pltpu.VMEM)] * n
    specs += [spec(pl.ANY)] * hbm + [spec(pltpu.VMEM)] * after
    return pl.pallas_call(
        body,
        out_shape=outs,
        in_specs=specs,
        out_specs=jax.tree.map(lambda _: spec(pltpu.VMEM), outs),
        scratch_shapes=list(scratch),
        compiler_params=params(mib),
        cost_estimate=cost(flops, 4 << 20),
        name=name,
    )


def shape(*dims, dtype=BF):
    return jax.ShapeDtypeStruct(dims, dtype)


CHUNKS = ((0, 4), (4, 4), (8, 4), (12, 3))


def frames_kernel(pair, info, codes_ref, hf_ref, gain_ref, qkv_hbm, own_hbm, other_hbm, q_ref, kv_ref, weights, table, qkv, hf, rows, x, xn, sems, table_sems, qkv_sem):
    def weight_copies(phase):
        return [
            pltpu.make_async_copy(
                full.at[pl.ds(part * 4 ^ info[3], 4), pair, y, pl.ds(phase * BLOCKS, BLOCKS)],
                weights.at[phase, half, y, pl.ds(part * 4, 4)],
                sems.at[phase, half, part, y],
            )
            for half, full in enumerate((own_hbm, other_hbm))
            for part in range(2)
            for y in range(4)
        ]

    def product(phase):
        for first, size in CHUNKS:
            w = [weights[phase, :, :, :, block].reshape(C, 128) for block in range(first, first + size)]
            x[phase, :, first * 128 : (first + size) * 128] = dot(hf[...], jnp.concatenate(w, axis=1))

    def norm(phase):
        total = jnp.zeros((256, 128), F32)
        for block in range(BLOCKS):
            cols = slice(block * 128, block * 128 + 128)
            y = x[phase, :, cols] + rows[pl.ds(phase * 256, 256), block, :]
            x[phase, :, cols] = y
            total += y
        mean = jnp.sum(total, axis=1, keepdims=True) * (1.0 / D)
        square = jnp.zeros((256, 128), F32)
        for block in range(BLOCKS):
            y = x[phase, :, block * 128 : block * 128 + 128] - mean
            square += y * y
        factor = lax.rsqrt(jnp.sum(square, axis=1, keepdims=True) * (1.0 / D) + 1e-5)
        for block in range(BLOCKS):
            cols = slice(block * 128, block * 128 + 128)
            xn[phase, :, cols] = ((x[phase, :, cols] - mean) * factor * gain_ref[:, cols]).astype(BF)

    def project(phase):
        y = dot(xn[phase], qkv[...]).astype(BF)
        lines = slice(phase * 256, phase * 256 + 256)
        for head in range(2):
            at = head * 384
            cols = slice(head * 128, head * 128 + 128)
            q_ref[lines, cols] = y[:, at : at + 128]
            kv_ref[lines, cols] = y[:, at + 128 : at + 256]
            kv_ref[lines, 256 + head * 128 : 384 + head * 128] = y[:, at + 256 : at + 384]

    table_copies = [
        pltpu.make_async_copy(
            full.at[:, part, :, pl.ds(UP_BLOCKS, 16)], table.at[half, :, part], table_sems.at[half, part]
        )
        for half, full in enumerate((own_hbm, other_hbm))
        for part in range(2)
    ]
    qkv_copy = pltpu.make_async_copy(qkv_hbm, qkv, qkv_sem)
    start(weight_copies(0))
    start(table_copies)
    start(weight_copies(1))
    qkv_copy.start()
    for rows_of in range(2):
        for half in range(2):
            at = pl.multiple_of(((info[3] // 4) ^ half ^ rows_of) * 128, 128)
            for y in range(4):
                j = half * 4 + y
                hf[rows_of * 128 : rows_of * 128 + 128, j * 128 : j * 128 + 128] = hf_ref[
                    rows_of * 4 + y, :, pl.ds(at, 128)
                ]
    flat = table.reshape(VOCAB, 16, 128)

    finish(weight_copies(0))
    product(0)
    finish(table_copies)

    def look_up(i, carry):
        for j in range(16):
            row = i * 16 + j
            rows[row] = flat[codes_ref[pair * 512 + row]].astype(F32)
        return carry

    lax.fori_loop(0, 32, look_up, 0)
    finish(weight_copies(1))
    qkv_copy.wait()
    norm(0)
    product(1)
    project(0)
    norm(1)
    project(1)


def frames(pair, info, codes, hf, gain, qkv, full_own, full_other):
    vm = pl.BlockSpec(memory_space=pltpu.VMEM)
    sm = pl.BlockSpec(memory_space=pltpu.SMEM)
    any_space = pl.BlockSpec(memory_space=pl.ANY)
    return pl.pallas_call(
        functools.partial(frames_kernel, pair),
        out_shape=(shape(512, 256), shape(512, 512)),
        in_specs=[sm, sm, vm, vm, any_space, any_space, any_space],
        out_specs=(vm, vm),
        scratch_shapes=[
            pltpu.VMEM((2, 2, 4, 8, BLOCKS, 16, 128), BF),
            pltpu.VMEM((2, 8, 2, 4, 16, 16, 128), BF),
            pltpu.VMEM((D, 768), BF),
            pltpu.VMEM((256, C), BF),
            pltpu.VMEM((512, 16, 128), F32),
            pltpu.VMEM((2, 256, D), F32),
            pltpu.VMEM((2, 256, D), BF),
            pltpu.SemaphoreType.DMA((2, 2, 2, 4)),
            pltpu.SemaphoreType.DMA((2, 2)),
            pltpu.SemaphoreType.DMA,
        ],
        compiler_params=params(40),
        cost_estimate=cost(4 * 10**9, 20 << 20),
        name="frames",
    )(info, codes, hf, gain, qkv, full_own, full_other)


SCALE = 128**-0.5 * 1.4426950408889634


def scores_of(q, k):
    return lax.dot_general(q, k, (((1,), (1,)), ((), ())), preferred_element_type=F32)


def fold(tiles, kv, old_of, put):
    for head in range(2):
        cols = slice(head * 128, head * 128 + 128)
        k = kv[:, cols]
        v = kv[:, 256 + head * 128 : 384 + head * 128]
        v = jnp.concatenate([v, jnp.ones(v.shape, BF)], axis=1)
        for tile, (queries, seen) in enumerate(tiles):
            s = jnp.where(seen, scores_of(queries[:, cols], k), -1e30)
            top = jnp.max(s, axis=1, keepdims=True)
            old = old_of(head, tile)
            if old is None:
                put(head, tile, top, dot(jnp.exp2((s - top) * SCALE).astype(BF), v))
            else:
                top = jnp.maximum(old[0], top)
                p = jnp.exp2((s - top) * SCALE).astype(BF)
                put(head, tile, top, old[1] * jnp.exp2((old[0] - top) * SCALE) + dot(p, v))


def phase_tiles(q0_ref, q1_ref, seen):
    return [(ref[at : at + 256], seen) for ref in (q0_ref, q1_ref) for at in (0, 256)]


def join_keys(kv, first, second):
    kv[:512] = first[...]
    kv[512:] = second[...]


def own_kernel(q0_ref, q1_ref, kv0_ref, kv1_ref, acc_ref, top_ref, kv):
    for part in range(2):
        keys = 128 * (part + 1)
        for phase, ref in enumerate((kv0_ref, kv0_ref, kv1_ref, kv1_ref)):
            kv[phase * keys : (phase + 1) * keys] = ref[phase % 2 * 256 : phase % 2 * 256 + keys]
        col = lax.broadcasted_iota(jnp.int32, (256, 4 * keys), 1)
        row = lax.broadcasted_iota(jnp.int32, (256, 4 * keys), 0)
        ahead = col % keys * 4 + col // keys - (part * 512 + row % 128 * 4 + row // 128)
        tiles = []
        for pair, ref in enumerate((q0_ref, q1_ref)):
            lines = slice(part * 128, part * 128 + 128), slice(256 + part * 128, 384 + part * 128)
            tiles.append((jnp.concatenate([ref[at, :] for at in lines]), ahead <= 2 * pair))

        def put(head, tile, top, acc):
            lines = slice(part * 128, part * 128 + 128)
            for i in range(2):
                top_ref[head, tile * 2 + i, lines] = top[i * 128 : i * 128 + 128]
                acc_ref[head, tile * 2 + i, lines] = acc[i * 128 : i * 128 + 128]

        fold(tiles, kv[: 4 * keys], lambda head, tile: None, put)


def past_kernel(last, info, q0_ref, q1_ref, far_ref, near_ref, acc_ref, top_ref, *refs):
    if last:
        out_ref, kv, acc, tops, wide = refs
    else:
        acc, tops, kv = refs
    song = info[2]

    @pl.when(song == 0)
    def _():
        acc[...] = acc_ref[...]
        tops[...] = top_ref[...]

    @pl.when(song > 0)
    def _():
        join_keys(kv, far_ref, near_ref)
        col = lax.broadcasted_iota(jnp.int32, (256, 1024), 1)
        seen = col >= jnp.where(song == 1, 512, 0)

        def put(head, phase, top, total):
            tops[head, phase] = top
            acc[head, phase] = total

        fold(
            phase_tiles(q0_ref, q1_ref, seen),
            kv[...],
            lambda head, phase: (top_ref[head, phase], acc_ref[head, phase]),
            put,
        )

    if last:
        for head in range(2):
            for phase in range(4):
                both = acc[head, phase]
                wide[pl.ds(phase, 256, stride=4), :] = both[:, :128] / both[:, 128:]
            out_ref[:, head * 128 : head * 128 + 128] = wide[...].astype(BF)


EVERY = ("song", "tensor")


def other_half():
    pairs = []
    for song in range(16):
        for rank in range(8):
            pairs.append((song * 8 + rank, (song ^ 8) * 8 + (rank ^ 4)))
    return pairs


def song_neighbours():
    first = [(song * 8 + rank, song * 8 + 8 + rank) for song in range(15) for rank in range(4)]
    second = [(song * 8 + 8 + rank, song * 8 + rank) for song in range(15) for rank in range(4, 8)]
    return first + second


def to_sibling(value):
    return lax.ppermute(value, "song", [(i, i ^ 1) for i in range(16)])


def exchange(value, axis="tensor", groups=None):
    return lax.all_to_all(value, axis, 0, 0, axis_index_groups=groups, tiled=True)


def gathered(parts):
    return lax.all_gather(parts, "song", axis=0, tiled=False).reshape(8, 2, 4, PART, 16, 128)


def on_device(
    upper_codes,
    middle_codes,
    upper_table,
    dilated_weight,
    mixing_weight,
    upsample_weight,
    middle_table,
    norm_gain,
    qkv_weight,
):
    song = lax.axis_index("song")
    rank = lax.axis_index("tensor")
    core = song % 2
    x_hi = rank // 4
    begin = song * 256 + x_hi * HALF
    share = song ^ (8 * x_hi)
    dilated_weight = pltpu.with_memory_space_constraint(dilated_weight, pltpu.HBM)
    mixing_weight = pltpu.with_memory_space_constraint(mixing_weight, pltpu.HBM)
    info = jnp.stack([core, begin, song, x_hi * 4, share // 2, share]).astype(jnp.int32)

    part = call(
        share_kernel,
        shape(4, PART, 16, 128),
        [
            pltpu.VMEM((16, 2 * D), BF),
            pltpu.VMEM((16, D), BF),
            pltpu.VMEM((16, 16, 128), F32),
            pltpu.SemaphoreType.DMA((2,)),
        ],
        hbm=2,
        name="share",
        mib=60,
    )(info, upsample_weight, middle_table)
    mine = exchange(part, groups=Y_GROUPS)

    pack0, pack1, pack2 = call(
        pack_kernel,
        (shape(768, 512), shape(512, 512), shape(2, 512, 512)),
        [pltpu.SemaphoreType.DMA((32,))],
        hbm=3,
        name="pack",
        mib=60,
    )(info, dilated_weight, mixing_weight, upper_table)
    got0 = lax.ppermute(pack0, EVERY, other_half())

    edge = jnp.where(x_hi == 0, upper_codes[-40:], upper_codes[:40])
    edge = lax.ppermute(edge, EVERY, song_neighbours())
    mine, edge, pack1 = lax.optimization_barrier((mine, edge, pack1))
    full_own = gathered(mine)
    pack1, got0 = lax.optimization_barrier((pack1, got0))
    sib0 = to_sibling(got0)
    got1 = lax.ppermute(pack1, EVERY, other_half())
    codes = jnp.where(
        x_hi == 0,
        jnp.concatenate([edge, upper_codes[: HALF + 40]]),
        jnp.concatenate([upper_codes[HALF - 40 :], edge]),
    )[:, None]

    h, terms = call(
        first_kernel,
        (shape(ROWS[0], 256, dtype=F32), shape(4, ROWS[1], 256)),
        [*DILATED, pltpu.VMEM((ROWS[0], 256), F32)],
        n=2,
        hbm=1,
        after=2,
        name="cond0",
    )(info, codes, upper_table, dilated_weight, got0, sib0)
    for level in range(4):
        terms = exchange(terms, groups=Y_GROUPS)
        if level == 0:
            mine, terms = lax.optimization_barrier((mine, terms))
            others = lax.ppermute(mine, EVERY, other_half())
        total = terms[0].astype(F32)
        for y in range(1, 4):
            total = total + terms[y].astype(F32)
        r = jnp.maximum(total, 0.0).astype(BF)
        r = exchange(jnp.broadcast_to(r[None], terms.shape), groups=Y_GROUPS)
        if level == 0:
            got1, others, pack2, r = lax.optimization_barrier((got1, others, pack2, r))
            full_other = gathered(others)
            sib1 = to_sibling(got1)
            got2 = lax.ppermute(pack2, EVERY, other_half())
            stacks = [(got0, sib0), (got1, sib1)]
        if level == 1:
            got2, r = lax.optimization_barrier((got2, r))
            stacks += [(got2, to_sibling(got2))] * 2
        if level < 3:
            h, terms = call(
                functools.partial(middle_kernel, level),
                (shape(ROWS[level + 1], 256, dtype=F32), shape(4, ROWS[level + 2], 256)),
                [*MIXING, *DILATED, pltpu.VMEM((ROWS[level + 1], 256), F32)],
                n=2,
                hbm=6,
                name="cond",
            )(info, r, h, mixing_weight, *stacks[level], dilated_weight, *stacks[level + 1])
        else:
            spread = call(
                last_kernel, shape(8, HALF, 256), MIXING, n=2, hbm=3, name="cond_end"
            )(info, r, h, mixing_weight, *stacks[level])
    hf = exchange(spread)

    mid = middle_codes.reshape(256, 4).T.reshape(1024)
    mid = (mid // 1024 * 1024 + mid % 256 // 16 * 64 + mid // 256 % 4 * 16 + mid % 16) ^ (
        x_hi * (1024 + 8 * 64)
    )
    gain = norm_gain[None]
    qkv = qkv_weight.reshape(D, 768)

    def from_two_back(value):
        return lax.ppermute(value, "song", [(i, i + 2) for i in range(14)])

    q0, kv0 = frames(0, info, mid, hf, gain, qkv, full_own, full_other)
    far0 = from_two_back(kv0)
    q1, kv1 = frames(1, info, mid, hf, gain, qkv, full_own, full_other)
    far1 = from_two_back(kv1)
    state = (shape(2, 4, 256, 256, dtype=F32), shape(2, 4, 256, 1, dtype=F32))
    keys = pltpu.VMEM((1024, 512), BF)
    far0, q1 = lax.optimization_barrier((far0, q1))
    kept = call(own_kernel, state, [keys], smem=0, n=4, flops=10**9, name="own", mib=24)(q0, q1, kv0, kv1)
    near0 = to_sibling(jnp.where(core == 0, kv0, far0))
    kept = call(functools.partial(past_kernel, False), state, [keys], n=6, flops=10**9, name="past", mib=24)(
        info, q0, q1, far0, near0, *kept
    )
    far1, kept = lax.optimization_barrier((far1, kept))
    near1 = to_sibling(jnp.where(core == 0, kv1, far1))
    return call(
        functools.partial(past_kernel, True),
        shape(1024, 256),
        [
            keys,
            pltpu.VMEM((2, 4, 256, 256), F32),
            pltpu.VMEM((2, 4, 256, 1), F32),
            pltpu.VMEM((1024, 128), F32),
        ],
        n=6,
        flops=2 * 10**9,
        name="past_end",
        mib=24,
    )(info, q0, q1, far1, near1, *kept)


def solution(mesh):
    placed = (
        P("song"),
        P("song"),
        P(None, "tensor"),
        P(None, None, "tensor", None),
        P(None, None, "tensor"),
        P("tensor", None),
        P("tensor", None),
        P(),
        P(None, "tensor", None),
    )
    return jax.shard_map(
        on_device, mesh=mesh, in_specs=placed, out_specs=P("song", "tensor"), check_vma=False
    )
```

```python
import functools

import jax
import jax.numpy as jnp
from jax import lax
from jax.experimental import pallas as pl
from jax.experimental.pallas import tpu as pltpu
from jax.sharding import PartitionSpec as P

BF = jnp.bfloat16
F32 = jnp.float32
D = 1920
C = 1024
VOCAB = 2048
UPPER = 4096
HALF = 128
HALO = (40, 39, 36, 27, 0)
ROWS = (208, 208, 208, 192, 128)

BLOCKS = D // 128
UP_BLOCKS = 2 * BLOCKS
PART = UP_BLOCKS + 16

Y_GROUPS = [[0, 1, 2, 3], [4, 5, 6, 7]]


def params(mib):
    return pltpu.CompilerParams(vmem_limit_bytes=mib << 20)


def cost(flops, nbytes, trans=0):
    return pl.CostEstimate(flops=flops, bytes_accessed=nbytes, transcendentals=trans)


def dot(a, b):
    return jnp.dot(a, b, preferred_element_type=F32)


def dilated_copies(level, info, dil_hbm, got_hbm, sib_hbm, near_ref, away_ref, sems):
    own = pl.multiple_of(info[0] * 512, 512)
    other = pl.multiple_of((1 - info[0]) * 512, 512)
    pairs = []
    for ref, hbm, begin in ((near_ref, got_hbm, own), (away_ref, sib_hbm, other)):
        part = hbm if level < 2 else hbm.at[level - 2]
        pairs.append((dil_hbm.at[level, :, :, pl.ds(begin, 512)], ref.at[:, pl.ds(0, 128), :]))
        for tap in range(3):
            pairs.append((part.at[pl.ds(tap * 128, 128), :], ref.at[tap, pl.ds(128, 128), :]))
    return [pltpu.make_async_copy(a, b, sems.at[i]) for i, (a, b) in enumerate(pairs)]


def mixing_copies(level, info, mix_hbm, got_hbm, sib_hbm, mix_ref, sems):
    pairs = []
    for half, hbm in enumerate((got_hbm, sib_hbm)):
        part = hbm if level < 2 else hbm.at[level - 2]
        begin = info[0] if half == 0 else 1 - info[0]
        rows = pl.ds(pl.multiple_of(begin * 512, 512), 512)
        pairs.append((mix_hbm.at[level, rows, :], mix_ref.at[half, :, pl.ds(0, 128)]))
        for y in range(4):
            pairs.append(
                (
                    part.at[pl.ds(384, 128), pl.ds(y * 128, 128)],
                    mix_ref.at[half, pl.ds(y * 128, 128), pl.ds(128, 128)],
                )
            )
    return [pltpu.make_async_copy(a, b, sems.at[i]) for i, (a, b) in enumerate(pairs)]


def send_terms(level, info, h_ref, near_ref, away_ref, out_ref):
    step = 3**level
    count = HALF + 2 * HALO[level + 1]
    padded = out_ref.shape[1]
    rows = h_ref.shape[0]
    first = info[1] - HALO[level]
    pos = first + lax.broadcasted_iota(jnp.int32, (rows, 1), 0)
    inside = (pos >= 0) & (pos < UPPER)
    h_ref[...] = jnp.where(inside, jnp.maximum(h_ref[...], 0.0), 0.0)
    taps = [h_ref[tap * step : tap * step + count, :].astype(BF) for tap in range(3)]
    for half, ref in enumerate((near_ref, away_ref)):
        total = dot(taps[0], ref[0]) + dot(taps[1], ref[1]) + dot(taps[2], ref[2])
        total = total.astype(BF)
        for y in range(4):
            out_ref[y, :count, half * 128 : half * 128 + 128] = total[:, y * 128 : y * 128 + 128]
    if padded > count:
        for y in range(4):
            out_ref[y, count:, :] = jnp.zeros((padded - count, 256), BF)


def start(copies):
    for copy in copies:
        copy.start()


def finish(copies):
    for copy in copies:
        copy.wait()


DILATED = [pltpu.VMEM((3, 256, 512), BF), pltpu.VMEM((3, 256, 512), BF), pltpu.SemaphoreType.DMA((8,))]
MIXING = [pltpu.VMEM((2, 512, 256), BF), pltpu.SemaphoreType.DMA((10,))]


def first_kernel(info, codes_ref, table_ref, dil_hbm, got_ref, sib_ref, h_ref, out_ref, near_ref, away_ref, sems, work):
    copies = dilated_copies(0, info, dil_hbm, got_ref, sib_ref, near_ref, away_ref, sems)
    start(copies)
    codes = codes_ref[...]
    rows = codes.shape[0]
    lane = lax.broadcasted_iota(jnp.int32, (rows, 1024), 1)
    core = info[0]
    one = jnp.ones((), BF)
    zero = jnp.zeros((), BF)
    h_own = jnp.zeros((rows, 128), F32)
    h_oth = jnp.zeros((rows, 128), F32)
    for src, begin in ((got_ref, core * 1024), (sib_ref, (1 - core) * 1024)):
        hot = jnp.where(codes - begin == lane, one, zero)
        h_own += dot(hot, table_ref[pl.ds(pl.multiple_of(begin, 1024), 1024), :])
        for q in range(4):
            h_oth += dot(hot[:, q * 256 : q * 256 + 256], src[512:768, q * 128 : q * 128 + 128])
    work[:, :128] = h_own
    work[:, 128:] = h_oth
    h_ref[...] = work[...]
    finish(copies)
    send_terms(0, info, work, near_ref, away_ref, out_ref)


def mixed(level, r_ref, h_ref, mix_ref):
    step = 3**level
    count = HALF + 2 * HALO[level + 1]
    h = h_ref[step : step + count, :]
    for half in range(2):
        r = jnp.concatenate([r_ref[y, :, half * 128 : half * 128 + 128] for y in range(4)], axis=1)
        h += dot(r, mix_ref[half])[:count]
    return h


def middle_kernel(level, info, r_ref, h_ref, mix_hbm, got_hbm, sib_hbm, dil_hbm, got1_hbm, sib1_hbm, new_ref, out_ref, mix_ref, mix_sems, near_ref, away_ref, sems, work):
    first = mixing_copies(level, info, mix_hbm, got_hbm, sib_hbm, mix_ref, mix_sems)
    then = dilated_copies(level + 1, info, dil_hbm, got1_hbm, sib1_hbm, near_ref, away_ref, sems)
    start(first)
    start(then)
    finish(first)
    count = HALF + 2 * HALO[level + 1]
    if work.shape[0] > count:
        work[count:, :] = jnp.zeros((work.shape[0] - count, 256), F32)
    work[:count, :] = mixed(level, r_ref, h_ref, mix_ref)
    new_ref[...] = work[...]
    finish(then)
    send_terms(level + 1, info, work, near_ref, away_ref, out_ref)


def last_kernel(info, r_ref, h_ref, mix_hbm, got_hbm, sib_hbm, out_ref, mix_ref, mix_sems):
    copies = mixing_copies(3, info, mix_hbm, got_hbm, sib_hbm, mix_ref, mix_sems)
    start(copies)
    finish(copies)
    h = mixed(3, r_ref, h_ref, mix_ref).astype(BF)
    for peer in range(8):
        out_ref[peer] = h


def half_copies(info, level, dil_hbm, mix_hbm, dest):
    cols = pl.ds(pl.multiple_of(info[0] * 512, 512), 512)
    pairs = [(dil_hbm.at[level, tap, :, cols], dest.at[pl.ds(tap * 128, 128), :]) for tap in range(3)]
    for i in range(4):
        rows = pl.ds(pl.multiple_of(info[0] * 512 + i * 128, 128), 128)
        pairs.append((mix_hbm.at[level, rows, :], dest.at[pl.ds(384, 128), pl.ds(i * 128, 128)]))
    return pairs


def copies_of(pairs, sems):
    return [pltpu.make_async_copy(a, b, sems.at[i]) for i, (a, b) in enumerate(pairs)]


def share_kernel(info, up_hbm, mid_hbm, part_ref, up, mid, wide, sems):
    pairs = [
        (up_hbm.at[pl.ds(info[4] * 16, 16), pl.ds(pl.multiple_of(info[0] * 2 * D, 128), 2 * D)], up),
        (mid_hbm.at[pl.ds(info[5] * 16, 16), :], mid),
    ]
    copies = copies_of(pairs, sems)
    start(copies)
    wide[...] = jnp.zeros_like(wide)
    finish(copies)
    for block in range(BLOCKS):
        wide[:, block, :] = mid[:, block * 128 : block * 128 + 128].astype(F32)
    for y in range(4):
        for block in range(UP_BLOCKS):
            part_ref[y, block] = up[:, block * 128 : block * 128 + 128]
        part_ref[y, UP_BLOCKS:] = wide[...].astype(BF)


def pack_kernel(info, dil_hbm, mix_hbm, tab_hbm, pack0, pack1, pack2, sems):
    pairs = half_copies(info, 0, dil_hbm, mix_hbm, pack0) + half_copies(info, 1, dil_hbm, mix_hbm, pack1)
    for i in range(2):
        pairs += half_copies(info, 2 + i, dil_hbm, mix_hbm, pack2.at[i])
    for i in range(4):
        rows = pl.ds(pl.multiple_of(info[0] * 1024 + i * 256, 256), 256)
        pairs.append((tab_hbm.at[rows, :], pack0.at[pl.ds(512, 256), pl.ds(i * 128, 128)]))
    copies = copies_of(pairs, sems)
    start(copies)
    finish(copies)


def call(body, outs, scratch=(), smem=1, n=0, hbm=0, after=0, flops=10**9, name=None, mib=12):
    def spec(space):
        return pl.BlockSpec(memory_space=space)

    specs = [spec(pltpu.SMEM)] * smem + [spec(pltpu.VMEM)] * n
    specs += [spec(pl.ANY)] * hbm + [spec(pltpu.VMEM)] * after
    return pl.pallas_call(
        body,
        out_shape=outs,
        in_specs=specs,
        out_specs=jax.tree.map(lambda _: spec(pltpu.VMEM), outs),
        scratch_shapes=list(scratch),
        compiler_params=params(mib),
        cost_estimate=cost(flops, 4 << 20),
        name=name,
    )


def shape(*dims, dtype=BF):
    return jax.ShapeDtypeStruct(dims, dtype)


CHUNKS = ((0, 4), (4, 4), (8, 4), (12, 3))


def frames_kernel(pair, info, codes_ref, hf_ref, gain_ref, qkv_hbm, own_hbm, other_hbm, q_ref, kv_ref, weights, table, qkv, hf, rows, x, xn, sems, table_sems, qkv_sem):
    def weight_copies(phase):
        return [
            pltpu.make_async_copy(
                full.at[pl.ds(part * 4 ^ info[3], 4), pair, y, pl.ds(phase * BLOCKS, BLOCKS)],
                weights.at[phase, half, y, pl.ds(part * 4, 4)],
                sems.at[phase, half, part, y],
            )
            for half, full in enumerate((own_hbm, other_hbm))
            for part in range(2)
            for y in range(4)
        ]

    def product(phase):
        for first, size in CHUNKS:
            w = [weights[phase, :, :, :, block].reshape(C, 128) for block in range(first, first + size)]
            x[phase, :, first * 128 : (first + size) * 128] = dot(hf[...], jnp.concatenate(w, axis=1))

    def norm(phase):
        total = jnp.zeros((256, 128), F32)
        for block in range(BLOCKS):
            cols = slice(block * 128, block * 128 + 128)
            y = x[phase, :, cols] + rows[pl.ds(phase * 256, 256), block, :]
            x[phase, :, cols] = y
            total += y
        mean = jnp.sum(total, axis=1, keepdims=True) * (1.0 / D)
        square = jnp.zeros((256, 128), F32)
        for block in range(BLOCKS):
            y = x[phase, :, block * 128 : block * 128 + 128] - mean
            square += y * y
        factor = lax.rsqrt(jnp.sum(square, axis=1, keepdims=True) * (1.0 / D) + 1e-5)
        for block in range(BLOCKS):
            cols = slice(block * 128, block * 128 + 128)
            xn[phase, :, cols] = ((x[phase, :, cols] - mean) * factor * gain_ref[:, cols]).astype(BF)

    def project(phase):
        y = dot(xn[phase], qkv[...]).astype(BF)
        lines = slice(phase * 256, phase * 256 + 256)
        for head in range(2):
            at = head * 384
            cols = slice(head * 128, head * 128 + 128)
            q_ref[lines, cols] = y[:, at : at + 128]
            kv_ref[lines, cols] = y[:, at + 128 : at + 256]
            kv_ref[lines, 256 + head * 128 : 384 + head * 128] = y[:, at + 256 : at + 384]

    table_copies = [
        pltpu.make_async_copy(
            full.at[:, part, :, pl.ds(UP_BLOCKS, 16)], table.at[half, :, part], table_sems.at[half, part]
        )
        for half, full in enumerate((own_hbm, other_hbm))
        for part in range(2)
    ]
    qkv_copy = pltpu.make_async_copy(qkv_hbm, qkv, qkv_sem)
    start(weight_copies(0))
    start(table_copies)
    start(weight_copies(1))
    qkv_copy.start()
    for rows_of in range(2):
        for half in range(2):
            at = pl.multiple_of(((info[3] // 4) ^ half ^ rows_of) * 128, 128)
            for y in range(4):
                j = half * 4 + y
                hf[rows_of * 128 : rows_of * 128 + 128, j * 128 : j * 128 + 128] = hf_ref[
                    rows_of * 4 + y, :, pl.ds(at, 128)
                ]
    flat = table.reshape(VOCAB, 16, 128)

    finish(weight_copies(0))
    product(0)
    finish(table_copies)

    def look_up(i, carry):
        for j in range(16):
            row = i * 16 + j
            rows[row] = flat[codes_ref[pair * 512 + row]].astype(F32)
        return carry

    lax.fori_loop(0, 32, look_up, 0)
    finish(weight_copies(1))
    qkv_copy.wait()
    norm(0)
    product(1)
    project(0)
    norm(1)
    project(1)


def frames(pair, info, codes, hf, gain, qkv, full_own, full_other):
    vm = pl.BlockSpec(memory_space=pltpu.VMEM)
    sm = pl.BlockSpec(memory_space=pltpu.SMEM)
    any_space = pl.BlockSpec(memory_space=pl.ANY)
    return pl.pallas_call(
        functools.partial(frames_kernel, pair),
        out_shape=(shape(512, 256), shape(512, 512)),
        in_specs=[sm, sm, vm, vm, any_space, any_space, any_space],
        out_specs=(vm, vm),
        scratch_shapes=[
            pltpu.VMEM((2, 2, 4, 8, BLOCKS, 16, 128), BF),
            pltpu.VMEM((2, 8, 2, 4, 16, 16, 128), BF),
            pltpu.VMEM((D, 768), BF),
            pltpu.VMEM((256, C), BF),
            pltpu.VMEM((512, 16, 128), F32),
            pltpu.VMEM((2, 256, D), F32),
            pltpu.VMEM((2, 256, D), BF),
            pltpu.SemaphoreType.DMA((2, 2, 2, 4)),
            pltpu.SemaphoreType.DMA((2, 2)),
            pltpu.SemaphoreType.DMA,
        ],
        compiler_params=params(40),
        cost_estimate=cost(4 * 10**9, 20 << 20),
        name="frames",
    )(info, codes, hf, gain, qkv, full_own, full_other)


SCALE = 128**-0.5 * 1.4426950408889634


def scores_of(q, k):
    return lax.dot_general(q, k, (((1,), (1,)), ((), ())), preferred_element_type=F32)


def fold(tiles, kv, old_of, put):
    for head in range(2):
        cols = slice(head * 128, head * 128 + 128)
        k = kv[:, cols]
        v = kv[:, 256 + head * 128 : 384 + head * 128]
        v = jnp.concatenate([v, jnp.ones(v.shape, BF)], axis=1)
        for tile, (queries, seen) in enumerate(tiles):
            s = jnp.where(seen, scores_of(queries[:, cols], k), -1e30)
            top = jnp.max(s, axis=1, keepdims=True)
            old = old_of(head, tile)
            if old is None:
                put(head, tile, top, dot(jnp.exp2((s - top) * SCALE).astype(BF), v))
            else:
                top = jnp.maximum(old[0], top)
                p = jnp.exp2((s - top) * SCALE).astype(BF)
                put(head, tile, top, old[1] * jnp.exp2((old[0] - top) * SCALE) + dot(p, v))


def phase_tiles(q0_ref, q1_ref, seen):
    return [(ref[at : at + 256], seen) for ref in (q0_ref, q1_ref) for at in (0, 256)]


def join_keys(kv, first, second):
    kv[:512] = first[...]
    kv[512:] = second[...]


def own_kernel(q0_ref, q1_ref, kv0_ref, kv1_ref, acc_ref, top_ref, kv):
    for part in range(2):
        keys = 128 * (part + 1)
        for phase, ref in enumerate((kv0_ref, kv0_ref, kv1_ref, kv1_ref)):
            kv[phase * keys : (phase + 1) * keys] = ref[phase % 2 * 256 : phase % 2 * 256 + keys]
        col = lax.broadcasted_iota(jnp.int32, (256, 4 * keys), 1)
        row = lax.broadcasted_iota(jnp.int32, (256, 4 * keys), 0)
        ahead = col % keys * 4 + col // keys - (part * 512 + row % 128 * 4 + row // 128)
        tiles = []
        for pair, ref in enumerate((q0_ref, q1_ref)):
            lines = slice(part * 128, part * 128 + 128), slice(256 + part * 128, 384 + part * 128)
            tiles.append((jnp.concatenate([ref[at, :] for at in lines]), ahead <= 2 * pair))

        def put(head, tile, top, acc):
            lines = slice(part * 128, part * 128 + 128)
            for i in range(2):
                top_ref[head, tile * 2 + i, lines] = top[i * 128 : i * 128 + 128]
                acc_ref[head, tile * 2 + i, lines] = acc[i * 128 : i * 128 + 128]

        fold(tiles, kv[: 4 * keys], lambda head, tile: None, put)


def past_kernel(last, info, q0_ref, q1_ref, far_ref, near_ref, acc_ref, top_ref, *refs):
    if last:
        out_ref, kv, acc, tops, wide = refs
    else:
        acc, tops, kv = refs
    song = info[2]

    @pl.when(song == 0)
    def _():
        acc[...] = acc_ref[...]
        tops[...] = top_ref[...]

    @pl.when(song > 0)
    def _():
        join_keys(kv, far_ref, near_ref)
        col = lax.broadcasted_iota(jnp.int32, (256, 1024), 1)
        seen = col >= jnp.where(song == 1, 512, 0)

        def put(head, phase, top, total):
            tops[head, phase] = top
            acc[head, phase] = total

        fold(
            phase_tiles(q0_ref, q1_ref, seen),
            kv[...],
            lambda head, phase: (top_ref[head, phase], acc_ref[head, phase]),
            put,
        )

    if last:
        for head in range(2):
            for phase in range(4):
                both = acc[head, phase]
                wide[pl.ds(phase, 256, stride=4), :] = both[:, :128] / both[:, 128:]
            out_ref[:, head * 128 : head * 128 + 128] = wide[...].astype(BF)


EVERY = ("song", "tensor")


def other_half():
    pairs = []
    for song in range(16):
        for rank in range(8):
            pairs.append((song * 8 + rank, (song ^ 8) * 8 + (rank ^ 4)))
    return pairs


def song_neighbours():
    first = [(song * 8 + rank, song * 8 + 8 + rank) for song in range(15) for rank in range(4)]
    second = [(song * 8 + 8 + rank, song * 8 + rank) for song in range(15) for rank in range(4, 8)]
    return first + second


def to_sibling(value):
    return lax.ppermute(value, "song", [(i, i ^ 1) for i in range(16)])


def exchange(value, axis="tensor", groups=None):
    return lax.all_to_all(value, axis, 0, 0, axis_index_groups=groups, tiled=True)


def gathered(parts):
    return lax.all_gather(parts, "song", axis=0, tiled=False).reshape(8, 2, 4, PART, 16, 128)


def on_device(
    upper_codes,
    middle_codes,
    upper_table,
    dilated_weight,
    mixing_weight,
    upsample_weight,
    middle_table,
    norm_gain,
    qkv_weight,
):
    song = lax.axis_index("song")
    rank = lax.axis_index("tensor")
    core = song % 2
    x_hi = rank // 4
    begin = song * 256 + x_hi * HALF
    share = song ^ (8 * x_hi)
    dilated_weight = pltpu.with_memory_space_constraint(dilated_weight, pltpu.HBM)
    mixing_weight = pltpu.with_memory_space_constraint(mixing_weight, pltpu.HBM)
    info = jnp.stack([core, begin, song, x_hi * 4, share // 2, share]).astype(jnp.int32)

    part = call(
        share_kernel,
        shape(4, PART, 16, 128),
        [
            pltpu.VMEM((16, 2 * D), BF),
            pltpu.VMEM((16, D), BF),
            pltpu.VMEM((16, 16, 128), F32),
            pltpu.SemaphoreType.DMA((2,)),
        ],
        hbm=2,
        name="share",
        mib=60,
    )(info, upsample_weight, middle_table)
    mine = exchange(part, groups=Y_GROUPS)

    pack0, pack1, pack2 = call(
        pack_kernel,
        (shape(768, 512), shape(512, 512), shape(2, 512, 512)),
        [pltpu.SemaphoreType.DMA((32,))],
        hbm=3,
        name="pack",
        mib=60,
    )(info, dilated_weight, mixing_weight, upper_table)
    got0 = lax.ppermute(pack0, EVERY, other_half())

    edge = jnp.where(x_hi == 0, upper_codes[-40:], upper_codes[:40])
    edge = lax.ppermute(edge, EVERY, song_neighbours())
    mine, edge, pack1 = lax.optimization_barrier((mine, edge, pack1))
    full_own = gathered(mine)
    pack1, got0 = lax.optimization_barrier((pack1, got0))
    sib0 = to_sibling(got0)
    got1 = lax.ppermute(pack1, EVERY, other_half())
    codes = jnp.where(
        x_hi == 0,
        jnp.concatenate([edge, upper_codes[: HALF + 40]]),
        jnp.concatenate([upper_codes[HALF - 40 :], edge]),
    )[:, None]

    h, terms = call(
        first_kernel,
        (shape(ROWS[0], 256, dtype=F32), shape(4, ROWS[1], 256)),
        [*DILATED, pltpu.VMEM((ROWS[0], 256), F32)],
        n=2,
        hbm=1,
        after=2,
        name="cond0",
    )(info, codes, upper_table, dilated_weight, got0, sib0)
    for level in range(4):
        terms = exchange(terms, groups=Y_GROUPS)
        if level == 0:
            got1, mine, terms = lax.optimization_barrier((got1, mine, terms))
            others = lax.ppermute(mine, EVERY, other_half())
            sib1 = to_sibling(got1)
        total = terms[0].astype(F32)
        for y in range(1, 4):
            total = total + terms[y].astype(F32)
        r = jnp.maximum(total, 0.0).astype(BF)
        r = exchange(jnp.broadcast_to(r[None], terms.shape), groups=Y_GROUPS)
        if level == 0:
            others, pack2, r = lax.optimization_barrier((others, pack2, r))
            full_other = gathered(others)
            got2 = lax.ppermute(pack2, EVERY, other_half())
            stacks = [(got0, sib0), (got1, sib1)]
        if level == 1:
            got2, r = lax.optimization_barrier((got2, r))
            stacks += [(got2, to_sibling(got2))] * 2
        if level < 3:
            h, terms = call(
                functools.partial(middle_kernel, level),
                (shape(ROWS[level + 1], 256, dtype=F32), shape(4, ROWS[level + 2], 256)),
                [*MIXING, *DILATED, pltpu.VMEM((ROWS[level + 1], 256), F32)],
                n=2,
                hbm=6,
                name="cond",
            )(info, r, h, mixing_weight, *stacks[level], dilated_weight, *stacks[level + 1])
        else:
            spread = call(
                last_kernel, shape(8, HALF, 256), MIXING, n=2, hbm=3, name="cond_end"
            )(info, r, h, mixing_weight, *stacks[level])
    hf = exchange(spread)

    mid = middle_codes.reshape(256, 4).T.reshape(1024)
    mid = (mid // 1024 * 1024 + mid % 256 // 16 * 64 + mid // 256 % 4 * 16 + mid % 16) ^ (
        x_hi * (1024 + 8 * 64)
    )
    gain = norm_gain[None]
    qkv = qkv_weight.reshape(D, 768)

    def from_two_back(value):
        return lax.ppermute(value, "song", [(i, i + 2) for i in range(14)])

    q0, kv0 = frames(0, info, mid, hf, gain, qkv, full_own, full_other)
    far0 = from_two_back(kv0)
    q1, kv1 = frames(1, info, mid, hf, gain, qkv, full_own, full_other)
    far1 = from_two_back(kv1)
    state = (shape(2, 4, 256, 256, dtype=F32), shape(2, 4, 256, 1, dtype=F32))
    keys = pltpu.VMEM((1024, 512), BF)
    far0, q1 = lax.optimization_barrier((far0, q1))
    kept = call(own_kernel, state, [keys], smem=0, n=4, flops=10**9, name="own", mib=24)(q0, q1, kv0, kv1)
    near0 = to_sibling(jnp.where(core == 0, kv0, far0))
    kept = call(functools.partial(past_kernel, False), state, [keys], n=6, flops=10**9, name="past", mib=24)(
        info, q0, q1, far0, near0, *kept
    )
    far1, kept = lax.optimization_barrier((far1, kept))
    near1 = to_sibling(jnp.where(core == 0, kv1, far1))
    return call(
        functools.partial(past_kernel, True),
        shape(1024, 256),
        [
            keys,
            pltpu.VMEM((2, 4, 256, 256), F32),
            pltpu.VMEM((2, 4, 256, 1), F32),
            pltpu.VMEM((1024, 128), F32),
        ],
        n=6,
        flops=2 * 10**9,
        name="past_end",
        mib=24,
    )(info, q0, q1, far1, near1, *kept)


def solution(mesh):
    placed = (
        P("song"),
        P("song"),
        P(None, "tensor"),
        P(None, None, "tensor", None),
        P(None, None, "tensor"),
        P("tensor", None),
        P("tensor", None),
        P(),
        P(None, "tensor", None),
    )
    return jax.shard_map(
        on_device, mesh=mesh, in_specs=placed, out_specs=P("song", "tensor"), check_vma=False
    )
```

```python
import functools

import jax
import jax.numpy as jnp
from jax import lax
from jax.experimental import pallas as pl
from jax.experimental.pallas import tpu as pltpu
from jax.sharding import PartitionSpec as P

BF = jnp.bfloat16
F32 = jnp.float32
D = 1920
C = 1024
VOCAB = 2048
UPPER = 4096
HALF = 128
HALO = (40, 39, 36, 27, 0)
ROWS = (208, 208, 208, 192, 128)

BLOCKS = D // 128
UP_BLOCKS = 2 * BLOCKS
PART = UP_BLOCKS + 16

Y_GROUPS = [[0, 1, 2, 3], [4, 5, 6, 7]]


def params(mib):
    return pltpu.CompilerParams(vmem_limit_bytes=mib << 20)


def cost(flops, nbytes, trans=0):
    return pl.CostEstimate(flops=flops, bytes_accessed=nbytes, transcendentals=trans)


def dot(a, b):
    return jnp.dot(a, b, preferred_element_type=F32)


def dilated_copies(level, info, dil_hbm, got_hbm, sib_hbm, near_ref, away_ref, sems):
    own = pl.multiple_of(info[0] * 512, 512)
    other = pl.multiple_of((1 - info[0]) * 512, 512)
    pairs = []
    for ref, hbm, begin in ((near_ref, got_hbm, own), (away_ref, sib_hbm, other)):
        part = hbm if level < 2 else hbm.at[level - 2]
        pairs.append((dil_hbm.at[level, :, :, pl.ds(begin, 512)], ref.at[:, pl.ds(0, 128), :]))
        for tap in range(3):
            pairs.append((part.at[pl.ds(tap * 128, 128), :], ref.at[tap, pl.ds(128, 128), :]))
    return [pltpu.make_async_copy(a, b, sems.at[i]) for i, (a, b) in enumerate(pairs)]


def mixing_copies(level, info, mix_hbm, got_hbm, sib_hbm, mix_ref, sems):
    pairs = []
    for half, hbm in enumerate((got_hbm, sib_hbm)):
        part = hbm if level < 2 else hbm.at[level - 2]
        begin = info[0] if half == 0 else 1 - info[0]
        rows = pl.ds(pl.multiple_of(begin * 512, 512), 512)
        pairs.append((mix_hbm.at[level, rows, :], mix_ref.at[half, :, pl.ds(0, 128)]))
        for y in range(4):
            pairs.append(
                (
                    part.at[pl.ds(384, 128), pl.ds(y * 128, 128)],
                    mix_ref.at[half, pl.ds(y * 128, 128), pl.ds(128, 128)],
                )
            )
    return [pltpu.make_async_copy(a, b, sems.at[i]) for i, (a, b) in enumerate(pairs)]


def send_terms(level, info, h_ref, near_ref, away_ref, out_ref):
    step = 3**level
    count = HALF + 2 * HALO[level + 1]
    padded = out_ref.shape[1]
    rows = h_ref.shape[0]
    first = info[1] - HALO[level]
    pos = first + lax.broadcasted_iota(jnp.int32, (rows, 1), 0)
    inside = (pos >= 0) & (pos < UPPER)
    h_ref[...] = jnp.where(inside, jnp.maximum(h_ref[...], 0.0), 0.0)
    taps = [h_ref[tap * step : tap * step + count, :].astype(BF) for tap in range(3)]
    for half, ref in enumerate((near_ref, away_ref)):
        total = dot(taps[0], ref[0]) + dot(taps[1], ref[1]) + dot(taps[2], ref[2])
        total = total.astype(BF)
        for y in range(4):
            out_ref[y, :count, half * 128 : half * 128 + 128] = total[:, y * 128 : y * 128 + 128]
    if padded > count:
        for y in range(4):
            out_ref[y, count:, :] = jnp.zeros((padded - count, 256), BF)


def start(copies):
    for copy in copies:
        copy.start()


def finish(copies):
    for copy in copies:
        copy.wait()


DILATED = [pltpu.VMEM((3, 256, 512), BF), pltpu.VMEM((3, 256, 512), BF), pltpu.SemaphoreType.DMA((8,))]
MIXING = [pltpu.VMEM((2, 512, 256), BF), pltpu.SemaphoreType.DMA((10,))]


def first_kernel(info, codes_ref, table_ref, dil_hbm, got_ref, sib_ref, h_ref, out_ref, near_ref, away_ref, sems, work):
    copies = dilated_copies(0, info, dil_hbm, got_ref, sib_ref, near_ref, away_ref, sems)
    start(copies)
    codes = codes_ref[...]
    rows = codes.shape[0]
    lane = lax.broadcasted_iota(jnp.int32, (rows, 1024), 1)
    core = info[0]
    one = jnp.ones((), BF)
    zero = jnp.zeros((), BF)
    h_own = jnp.zeros((rows, 128), F32)
    h_oth = jnp.zeros((rows, 128), F32)
    for src, begin in ((got_ref, core * 1024), (sib_ref, (1 - core) * 1024)):
        hot = jnp.where(codes - begin == lane, one, zero)
        h_own += dot(hot, table_ref[pl.ds(pl.multiple_of(begin, 1024), 1024), :])
        for q in range(4):
            h_oth += dot(hot[:, q * 256 : q * 256 + 256], src[512:768, q * 128 : q * 128 + 128])
    work[:, :128] = h_own
    work[:, 128:] = h_oth
    h_ref[...] = work[...]
    finish(copies)
    send_terms(0, info, work, near_ref, away_ref, out_ref)


def mixed(level, r_ref, h_ref, mix_ref):
    step = 3**level
    count = HALF + 2 * HALO[level + 1]
    h = h_ref[step : step + count, :]
    for half in range(2):
        r = jnp.concatenate([r_ref[y, :, half * 128 : half * 128 + 128] for y in range(4)], axis=1)
        h += dot(r, mix_ref[half])[:count]
    return h


def middle_kernel(level, info, r_ref, h_ref, mix_hbm, got_hbm, sib_hbm, dil_hbm, got1_hbm, sib1_hbm, new_ref, out_ref, mix_ref, mix_sems, near_ref, away_ref, sems, work):
    first = mixing_copies(level, info, mix_hbm, got_hbm, sib_hbm, mix_ref, mix_sems)
    then = dilated_copies(level + 1, info, dil_hbm, got1_hbm, sib1_hbm, near_ref, away_ref, sems)
    start(first)
    start(then)
    finish(first)
    count = HALF + 2 * HALO[level + 1]
    if work.shape[0] > count:
        work[count:, :] = jnp.zeros((work.shape[0] - count, 256), F32)
    work[:count, :] = mixed(level, r_ref, h_ref, mix_ref)
    new_ref[...] = work[...]
    finish(then)
    send_terms(level + 1, info, work, near_ref, away_ref, out_ref)


def last_kernel(info, r_ref, h_ref, mix_hbm, got_hbm, sib_hbm, out_ref, mix_ref, mix_sems):
    copies = mixing_copies(3, info, mix_hbm, got_hbm, sib_hbm, mix_ref, mix_sems)
    start(copies)
    finish(copies)
    h = mixed(3, r_ref, h_ref, mix_ref).astype(BF)
    for peer in range(8):
        out_ref[peer] = h


def half_copies(info, level, dil_hbm, mix_hbm, dest):
    cols = pl.ds(pl.multiple_of(info[0] * 512, 512), 512)
    pairs = [(dil_hbm.at[level, tap, :, cols], dest.at[pl.ds(tap * 128, 128), :]) for tap in range(3)]
    for i in range(4):
        rows = pl.ds(pl.multiple_of(info[0] * 512 + i * 128, 128), 128)
        pairs.append((mix_hbm.at[level, rows, :], dest.at[pl.ds(384, 128), pl.ds(i * 128, 128)]))
    return pairs


def copies_of(pairs, sems):
    return [pltpu.make_async_copy(a, b, sems.at[i]) for i, (a, b) in enumerate(pairs)]


def share_kernel(info, up_hbm, mid_hbm, part_ref, up, mid, wide, sems):
    pairs = [
        (up_hbm.at[pl.ds(info[4] * 16, 16), pl.ds(pl.multiple_of(info[0] * 2 * D, 128), 2 * D)], up),
        (mid_hbm.at[pl.ds(info[5] * 16, 16), :], mid),
    ]
    copies = copies_of(pairs, sems)
    start(copies)
    wide[...] = jnp.zeros_like(wide)
    finish(copies)
    for block in range(BLOCKS):
        wide[:, block, :] = mid[:, block * 128 : block * 128 + 128].astype(F32)
    for y in range(4):
        for block in range(UP_BLOCKS):
            part_ref[y, block] = up[:, block * 128 : block * 128 + 128]
        part_ref[y, UP_BLOCKS:] = wide[...].astype(BF)


def pack_kernel(info, dil_hbm, mix_hbm, tab_hbm, pack0, pack1, pack2, sems):
    pairs = half_copies(info, 0, dil_hbm, mix_hbm, pack0) + half_copies(info, 1, dil_hbm, mix_hbm, pack1)
    for i in range(2):
        pairs += half_copies(info, 2 + i, dil_hbm, mix_hbm, pack2.at[i])
    for i in range(4):
        rows = pl.ds(pl.multiple_of(info[0] * 1024 + i * 256, 256), 256)
        pairs.append((tab_hbm.at[rows, :], pack0.at[pl.ds(512, 256), pl.ds(i * 128, 128)]))
    copies = copies_of(pairs, sems)
    start(copies)
    finish(copies)


def call(body, outs, scratch=(), smem=1, n=0, hbm=0, after=0, flops=10**9, name=None, mib=12):
    def spec(space):
        return pl.BlockSpec(memory_space=space)

    specs = [spec(pltpu.SMEM)] * smem + [spec(pltpu.VMEM)] * n
    specs += [spec(pl.ANY)] * hbm + [spec(pltpu.VMEM)] * after
    return pl.pallas_call(
        body,
        out_shape=outs,
        in_specs=specs,
        out_specs=jax.tree.map(lambda _: spec(pltpu.VMEM), outs),
        scratch_shapes=list(scratch),
        compiler_params=params(mib),
        cost_estimate=cost(flops, 4 << 20),
        name=name,
    )


def shape(*dims, dtype=BF):
    return jax.ShapeDtypeStruct(dims, dtype)


CHUNKS = ((0, 4), (4, 4), (8, 4), (12, 3))


def frames_kernel(pair, info, codes_ref, hf_ref, gain_ref, qkv_hbm, own_hbm, other_hbm, q_ref, kv_ref, weights, table, qkv, hf, rows, x, xn, sems, table_sems, qkv_sem):
    def weight_copies(phase):
        return [
            pltpu.make_async_copy(
                full.at[pl.ds(part * 4 ^ info[3], 4), pair, y, pl.ds(phase * BLOCKS, BLOCKS)],
                weights.at[phase, half, y, pl.ds(part * 4, 4)],
                sems.at[phase, half, part, y],
            )
            for half, full in enumerate((own_hbm, other_hbm))
            for part in range(2)
            for y in range(4)
        ]

    def product(phase):
        for first, size in CHUNKS:
            w = [weights[phase, :, :, :, block].reshape(C, 128) for block in range(first, first + size)]
            x[phase, :, first * 128 : (first + size) * 128] = dot(hf[...], jnp.concatenate(w, axis=1))

    def norm(phase):
        total = jnp.zeros((256, 128), F32)
        for block in range(BLOCKS):
            cols = slice(block * 128, block * 128 + 128)
            y = x[phase, :, cols] + rows[pl.ds(phase * 256, 256), block, :]
            x[phase, :, cols] = y
            total += y
        mean = jnp.sum(total, axis=1, keepdims=True) * (1.0 / D)
        square = jnp.zeros((256, 128), F32)
        for block in range(BLOCKS):
            y = x[phase, :, block * 128 : block * 128 + 128] - mean
            square += y * y
        factor = lax.rsqrt(jnp.sum(square, axis=1, keepdims=True) * (1.0 / D) + 1e-5)
        for block in range(BLOCKS):
            cols = slice(block * 128, block * 128 + 128)
            xn[phase, :, cols] = ((x[phase, :, cols] - mean) * factor * gain_ref[:, cols]).astype(BF)

    def project(phase):
        y = dot(xn[phase], qkv[...]).astype(BF)
        lines = slice(phase * 256, phase * 256 + 256)
        for head in range(2):
            at = head * 384
            cols = slice(head * 128, head * 128 + 128)
            q_ref[lines, cols] = y[:, at : at + 128]
            kv_ref[lines, cols] = y[:, at + 128 : at + 256]
            kv_ref[lines, 256 + head * 128 : 384 + head * 128] = y[:, at + 256 : at + 384]

    table_copies = [
        pltpu.make_async_copy(
            full.at[:, part, :, pl.ds(UP_BLOCKS, 16)], table.at[half, :, part], table_sems.at[half, part]
        )
        for half, full in enumerate((own_hbm, other_hbm))
        for part in range(2)
    ]
    qkv_copy = pltpu.make_async_copy(qkv_hbm, qkv, qkv_sem)
    start(weight_copies(0))
    start(table_copies)
    start(weight_copies(1))
    qkv_copy.start()
    for rows_of in range(2):
        for half in range(2):
            at = pl.multiple_of(((info[3] // 4) ^ half ^ rows_of) * 128, 128)
            for y in range(4):
                j = half * 4 + y
                hf[rows_of * 128 : rows_of * 128 + 128, j * 128 : j * 128 + 128] = hf_ref[
                    rows_of * 4 + y, :, pl.ds(at, 128)
                ]
    flat = table.reshape(VOCAB, 16, 128)

    finish(weight_copies(0))
    product(0)
    finish(table_copies)

    def look_up(i, carry):
        for j in range(16):
            row = i * 16 + j
            rows[row] = flat[codes_ref[pair * 512 + row]].astype(F32)
        return carry

    lax.fori_loop(0, 32, look_up, 0)
    finish(weight_copies(1))
    qkv_copy.wait()
    norm(0)
    product(1)
    project(0)
    norm(1)
    project(1)


def frames(pair, info, codes, hf, gain, qkv, full_own, full_other):
    vm = pl.BlockSpec(memory_space=pltpu.VMEM)
    sm = pl.BlockSpec(memory_space=pltpu.SMEM)
    any_space = pl.BlockSpec(memory_space=pl.ANY)
    return pl.pallas_call(
        functools.partial(frames_kernel, pair),
        out_shape=(shape(512, 256), shape(512, 512)),
        in_specs=[sm, sm, vm, vm, any_space, any_space, any_space],
        out_specs=(vm, vm),
        scratch_shapes=[
            pltpu.VMEM((2, 2, 4, 8, BLOCKS, 16, 128), BF),
            pltpu.VMEM((2, 8, 2, 4, 16, 16, 128), BF),
            pltpu.VMEM((D, 768), BF),
            pltpu.VMEM((256, C), BF),
            pltpu.VMEM((512, 16, 128), F32),
            pltpu.VMEM((2, 256, D), F32),
            pltpu.VMEM((2, 256, D), BF),
            pltpu.SemaphoreType.DMA((2, 2, 2, 4)),
            pltpu.SemaphoreType.DMA((2, 2)),
            pltpu.SemaphoreType.DMA,
        ],
        compiler_params=params(40),
        cost_estimate=cost(4 * 10**9, 20 << 20),
        name="frames",
    )(info, codes, hf, gain, qkv, full_own, full_other)


SCALE = 128**-0.5 * 1.4426950408889634


def scores_of(q, k):
    return lax.dot_general(q, k, (((1,), (1,)), ((), ())), preferred_element_type=F32)


def fold(tiles, kv, old_of, put):
    for head in range(2):
        cols = slice(head * 128, head * 128 + 128)
        k = kv[:, cols]
        v = kv[:, 256 + head * 128 : 384 + head * 128]
        v = jnp.concatenate([v, jnp.ones(v.shape, BF)], axis=1)
        for tile, (queries, seen) in enumerate(tiles):
            s = jnp.where(seen, scores_of(queries[:, cols], k), -1e30)
            top = jnp.max(s, axis=1, keepdims=True)
            old = old_of(head, tile)
            if old is None:
                put(head, tile, top, dot(jnp.exp2((s - top) * SCALE).astype(BF), v))
            else:
                top = jnp.maximum(old[0], top)
                p = jnp.exp2((s - top) * SCALE).astype(BF)
                put(head, tile, top, old[1] * jnp.exp2((old[0] - top) * SCALE) + dot(p, v))


def phase_tiles(q0_ref, q1_ref, seen):
    return [(ref[at : at + 256], seen) for ref in (q0_ref, q1_ref) for at in (0, 256)]


def join_keys(kv, first, second):
    kv[:512] = first[...]
    kv[512:] = second[...]


def own_kernel(q0_ref, q1_ref, kv0_ref, kv1_ref, acc_ref, top_ref, kv):
    for part in range(2):
        keys = 128 * (part + 1)
        for phase, ref in enumerate((kv0_ref, kv0_ref, kv1_ref, kv1_ref)):
            kv[phase * keys : (phase + 1) * keys] = ref[phase % 2 * 256 : phase % 2 * 256 + keys]
        col = lax.broadcasted_iota(jnp.int32, (256, 4 * keys), 1)
        row = lax.broadcasted_iota(jnp.int32, (256, 4 * keys), 0)
        ahead = col % keys * 4 + col // keys - (part * 512 + row % 128 * 4 + row // 128)
        tiles = []
        for pair, ref in enumerate((q0_ref, q1_ref)):
            lines = slice(part * 128, part * 128 + 128), slice(256 + part * 128, 384 + part * 128)
            tiles.append((jnp.concatenate([ref[at, :] for at in lines]), ahead <= 2 * pair))

        def put(head, tile, top, acc):
            lines = slice(part * 128, part * 128 + 128)
            for i in range(2):
                top_ref[head, tile * 2 + i, lines] = top[i * 128 : i * 128 + 128]
                acc_ref[head, tile * 2 + i, lines] = acc[i * 128 : i * 128 + 128]

        fold(tiles, kv[: 4 * keys], lambda head, tile: None, put)


def past_kernel(last, info, q0_ref, q1_ref, far_ref, near_ref, acc_ref, top_ref, *refs):
    if last:
        out_ref, kv, acc, tops, wide = refs
    else:
        acc, tops, kv = refs
    song = info[2]

    @pl.when(song == 0)
    def _():
        acc[...] = acc_ref[...]
        tops[...] = top_ref[...]

    @pl.when(song > 0)
    def _():
        join_keys(kv, far_ref, near_ref)
        col = lax.broadcasted_iota(jnp.int32, (256, 1024), 1)
        seen = col >= jnp.where(song == 1, 512, 0)

        def put(head, phase, top, total):
            tops[head, phase] = top
            acc[head, phase] = total

        fold(
            phase_tiles(q0_ref, q1_ref, seen),
            kv[...],
            lambda head, phase: (top_ref[head, phase], acc_ref[head, phase]),
            put,
        )

    if last:
        for head in range(2):
            for phase in range(4):
                both = acc[head, phase]
                wide[pl.ds(phase, 256, stride=4), :] = both[:, :128] / both[:, 128:]
            out_ref[:, head * 128 : head * 128 + 128] = wide[...].astype(BF)


EVERY = ("song", "tensor")


def other_half():
    pairs = []
    for song in range(16):
        for rank in range(8):
            pairs.append((song * 8 + rank, (song ^ 8) * 8 + (rank ^ 4)))
    return pairs


def song_neighbours():
    first = [(song * 8 + rank, song * 8 + 8 + rank) for song in range(15) for rank in range(4)]
    second = [(song * 8 + 8 + rank, song * 8 + rank) for song in range(15) for rank in range(4, 8)]
    return first + second


def to_sibling(value):
    return lax.ppermute(value, "song", [(i, i ^ 1) for i in range(16)])


def exchange(value, axis="tensor", groups=None):
    return lax.all_to_all(value, axis, 0, 0, axis_index_groups=groups, tiled=True)


def gathered(parts):
    return lax.all_gather(parts, "song", axis=0, tiled=False).reshape(8, 2, 4, PART, 16, 128)


def on_device(
    upper_codes,
    middle_codes,
    upper_table,
    dilated_weight,
    mixing_weight,
    upsample_weight,
    middle_table,
    norm_gain,
    qkv_weight,
):
    song = lax.axis_index("song")
    rank = lax.axis_index("tensor")
    core = song % 2
    x_hi = rank // 4
    begin = song * 256 + x_hi * HALF
    share = song ^ (8 * x_hi)
    dilated_weight = pltpu.with_memory_space_constraint(dilated_weight, pltpu.HBM)
    mixing_weight = pltpu.with_memory_space_constraint(mixing_weight, pltpu.HBM)
    info = jnp.stack([core, begin, song, x_hi * 4, share // 2, share]).astype(jnp.int32)

    part = call(
        share_kernel,
        shape(4, PART, 16, 128),
        [
            pltpu.VMEM((16, 2 * D), BF),
            pltpu.VMEM((16, D), BF),
            pltpu.VMEM((16, 16, 128), F32),
            pltpu.SemaphoreType.DMA((2,)),
        ],
        hbm=2,
        name="share",
        mib=60,
    )(info, upsample_weight, middle_table)
    mine = exchange(part, groups=Y_GROUPS)

    pack0, pack1, pack2 = call(
        pack_kernel,
        (shape(768, 512), shape(512, 512), shape(2, 512, 512)),
        [pltpu.SemaphoreType.DMA((32,))],
        hbm=3,
        name="pack",
        mib=60,
    )(info, dilated_weight, mixing_weight, upper_table)
    got0 = lax.ppermute(pack0, EVERY, other_half())

    edge = jnp.where(x_hi == 0, upper_codes[-40:], upper_codes[:40])
    edge = lax.ppermute(edge, EVERY, song_neighbours())
    mine, edge, pack1 = lax.optimization_barrier((mine, edge, pack1))
    full_own = gathered(mine)
    pack1, got0 = lax.optimization_barrier((pack1, got0))
    sib0 = to_sibling(got0)
    got1 = lax.ppermute(pack1, EVERY, other_half())
    codes = jnp.where(
        x_hi == 0,
        jnp.concatenate([edge, upper_codes[: HALF + 40]]),
        jnp.concatenate([upper_codes[HALF - 40 :], edge]),
    )[:, None]

    h, terms = call(
        first_kernel,
        (shape(ROWS[0], 256, dtype=F32), shape(4, ROWS[1], 256)),
        [*DILATED, pltpu.VMEM((ROWS[0], 256), F32)],
        n=2,
        hbm=1,
        after=2,
        name="cond0",
    )(info, codes, upper_table, dilated_weight, got0, sib0)
    for level in range(4):
        if level == 1:
            others, terms = lax.optimization_barrier((others, terms))
            full_other = gathered(others)
        terms = exchange(terms, groups=Y_GROUPS)
        if level == 0:
            got1, mine, terms = lax.optimization_barrier((got1, mine, terms))
            others = lax.ppermute(mine, EVERY, other_half())
            sib1 = to_sibling(got1)
        total = terms[0].astype(F32)
        for y in range(1, 4):
            total = total + terms[y].astype(F32)
        r = jnp.maximum(total, 0.0).astype(BF)
        r = exchange(jnp.broadcast_to(r[None], terms.shape), groups=Y_GROUPS)
        if level == 0:
            pack2, r = lax.optimization_barrier((pack2, r))
            got2 = lax.ppermute(pack2, EVERY, other_half())
            stacks = [(got0, sib0), (got1, sib1)]
        if level == 1:
            got2, r = lax.optimization_barrier((got2, r))
            stacks += [(got2, to_sibling(got2))] * 2
        if level < 3:
            h, terms = call(
                functools.partial(middle_kernel, level),
                (shape(ROWS[level + 1], 256, dtype=F32), shape(4, ROWS[level + 2], 256)),
                [*MIXING, *DILATED, pltpu.VMEM((ROWS[level + 1], 256), F32)],
                n=2,
                hbm=6,
                name="cond",
            )(info, r, h, mixing_weight, *stacks[level], dilated_weight, *stacks[level + 1])
        else:
            spread = call(
                last_kernel, shape(8, HALF, 256), MIXING, n=2, hbm=3, name="cond_end"
            )(info, r, h, mixing_weight, *stacks[level])
    hf = exchange(spread)

    mid = middle_codes.reshape(256, 4).T.reshape(1024)
    mid = (mid // 1024 * 1024 + mid % 256 // 16 * 64 + mid // 256 % 4 * 16 + mid % 16) ^ (
        x_hi * (1024 + 8 * 64)
    )
    gain = norm_gain[None]
    qkv = qkv_weight.reshape(D, 768)

    def from_two_back(value):
        return lax.ppermute(value, "song", [(i, i + 2) for i in range(14)])

    q0, kv0 = frames(0, info, mid, hf, gain, qkv, full_own, full_other)
    far0 = from_two_back(kv0)
    q1, kv1 = frames(1, info, mid, hf, gain, qkv, full_own, full_other)
    far1 = from_two_back(kv1)
    state = (shape(2, 4, 256, 256, dtype=F32), shape(2, 4, 256, 1, dtype=F32))
    keys = pltpu.VMEM((1024, 512), BF)
    far0, q1 = lax.optimization_barrier((far0, q1))
    kept = call(own_kernel, state, [keys], smem=0, n=4, flops=10**9, name="own", mib=24)(q0, q1, kv0, kv1)
    near0 = to_sibling(jnp.where(core == 0, kv0, far0))
    kept = call(functools.partial(past_kernel, False), state, [keys], n=6, flops=10**9, name="past", mib=24)(
        info, q0, q1, far0, near0, *kept
    )
    far1, kept = lax.optimization_barrier((far1, kept))
    near1 = to_sibling(jnp.where(core == 0, kv1, far1))
    return call(
        functools.partial(past_kernel, True),
        shape(1024, 256),
        [
            keys,
            pltpu.VMEM((2, 4, 256, 256), F32),
            pltpu.VMEM((2, 4, 256, 1), F32),
            pltpu.VMEM((1024, 128), F32),
        ],
        n=6,
        flops=2 * 10**9,
        name="past_end",
        mib=24,
    )(info, q0, q1, far1, near1, *kept)


def solution(mesh):
    placed = (
        P("song"),
        P("song"),
        P(None, "tensor"),
        P(None, None, "tensor", None),
        P(None, None, "tensor"),
        P("tensor", None),
        P("tensor", None),
        P(),
        P(None, "tensor", None),
    )
    return jax.shard_map(
        on_device, mesh=mesh, in_specs=placed, out_specs=P("song", "tensor"), check_vma=False
    )
```
